256 devices in a mesh: grp: 32 (over z_lo, x, core), tp: 8 (over y, z_hi).
Axes of the slice: x: 4, y: 4, z: 8 (z_hi: 2, z_lo: 4; z = z_hi * 4 + z_lo), core: 2. Of those that a mesh axis runs over, the one named last changes fastest.
Arguments:
- hidden: bfloat16 [8192, 4096], P('grp'), may hold values from -6 to 6
- norm_gain: float32 [4096], replicated, may hold values from 0.1 to 1.9
- w_query: bfloat16 [4096, 2048], P(None, 'tp'), may hold values from -0.09375 to 0.09375
- w_keyval: bfloat16 [4096, 512], P(None, 'tp'), may hold values from -0.09375 to 0.09375
- w_out: bfloat16 [2048, 4096], P('tp'), may hold values from -0.125 to 0.125
- kv_cache: bfloat16 [327680, 512], P(('grp', 'tp')), may hold values from -110 to 110, as said below
- cache_len: int32 [64], replicated, may hold values from 1 to 8192, as said below
- partner: int32 [32], replicated, may hold values from 0 to 31, as said below
Outputs:
- attn_out: bfloat16 [8192, 4096], P('grp', 'tp')
The draws below stay inside these ranges and needn't reach their ends.
Inputs may be any that keep to these rules, and one draw needn't show every extreme that they name: `cache_len`: entry g*2 is the cached length of group g's first request, at most 8192 and equal to 8192 for some group; every other entry is at most 2048, and equal to 2048 for some group. partner[g] is g XOR m for one m of 1 to 31 that is the same for every group, so partner[partner[g]] = g. `kv_cache`: cached keys and values of earlier tokens, laid out as row_owner describes.
All inputs are finite; a program needn't handle non-finite values.
Results may differ from the reference program's by a relative error of at most 0.013.
The reference program's roundings to bfloat16 on the way (of `normed`, `keyval`, `queries`, `new_keys`, `weights` and `attention`) count: a program that leaves them out, or rounds other values in their place, can miss the bound.
Values may be sent and summed in bfloat16 or wider, within the bound.
A program may use at most 128 MiB of HBM per device.

```python
import jax
import jax.numpy as jnp
from jax import lax

D = 4096
HD = 128
QH = 16
KVH = 2
C = 128
R = 2
LONG = 8192
SHORT = 2048
GROUPS = 32
TOK_G = 256
TOKENS = 8192
CACHE_G = 10240
CACHE = 327680
QW = 2048
KVW = 512


def draw_cache_len(key, part):
    key_list = jax.random.split(key, 6)
    shift_long = jax.random.randint(key_list[0], (GROUPS,), 0, 4)
    top_len = jnp.right_shift(jnp.full((GROUPS,), LONG, jnp.int32), shift_long)
    cut_len = jax.random.randint(key_list[1], (GROUPS,), 0, 1 << 30) % (top_len // 2 + 1)
    long_len = top_len - cut_len
    chosen = jax.random.randint(key_list[2], (), 0, GROUPS)
    long_len = jnp.where(jnp.arange(GROUPS) == chosen, LONG, long_len)
    shift_short = jax.random.randint(key_list[3], (GROUPS, R - 1), 0, 5)
    span_len = jnp.right_shift(jnp.full((GROUPS, R - 1), SHORT, jnp.int32), shift_short)
    short_len = 1 + jax.random.randint(key_list[4], (GROUPS, R - 1), 0, 1 << 30) % span_len
    chosen_short = jax.random.randint(key_list[5], (), 0, GROUPS)
    first_short = jnp.where(jnp.arange(GROUPS) == chosen_short, SHORT, short_len[:, 0])
    short_len = jnp.concatenate([first_short[:, None], short_len[:, 1:]], 1)
    return jnp.concatenate([long_len[:, None], short_len], 1).reshape(GROUPS * R).astype(jnp.int32)


def draw_partner(key, part):
    flip_mask = jax.random.randint(key, (), 1, GROUPS)
    return jnp.bitwise_xor(jnp.arange(GROUPS, dtype=jnp.int32), flip_mask).astype(jnp.int32)


def draw_kv_cache(key, part):
    key_list = jax.random.split(key, 1)
    values = jax.random.truncated_normal(key_list[0], -4.0, 4.0, (CACHE, KVW), jnp.float32)
    return values.astype(jnp.bfloat16)


def block_levels(rng, extent, pieces, smallest, top_value):
    factor_of, own = 1.0, jax.random.fold_in(rng, 6)
    for axis_at, shards_of in pieces:
        steps = jnp.exp(jax.random.uniform(jax.random.fold_in(own, axis_at), (shards_of,), jnp.float32, smallest / len(pieces), top_value / len(pieces)))
        factor_of = factor_of * jnp.repeat(steps, extent[axis_at] // shards_of).reshape([-1 if axis == axis_at else 1 for axis in range(len(extent))])
    return factor_of


def noise(rng, extent, spread, limit, cuts=(), kind=jnp.bfloat16):
    result = jax.random.normal(rng, extent, jnp.float32) * spread
    if len(cuts) > 0:
        result = block_levels(rng, extent, cuts, -0.22, 0.18) * result
    return jnp.clip(result, min=-limit, max=limit).astype(kind)


def setup_inputs(seed: int = 0) -> dict:
    seeds = jax.random.split(jax.random.key(seed), 9)
    return {
        "hidden": noise(seeds[0], (TOKENS, D), 1.0, 6.0, ((0, 32),)),
        "norm_gain": jnp.clip(1.0 + 0.18 * jax.random.normal(seeds[1], (D,), jnp.float32), 0.1, 1.9),
        "w_query": noise(seeds[2], (D, QW), D ** -0.5, 0.09375, ((1, 8),)),
        "w_keyval": noise(seeds[3], (D, KVW), D ** -0.5, 0.09375, ((1, 8),)),
        "w_out": noise(seeds[4], (QW, D), QW ** -0.5, 0.125, ((0, 8),)),
        "kv_cache": draw_kv_cache(jax.random.fold_in(seeds[8], 71), 0),
        "cache_len": draw_cache_len(jax.random.fold_in(seeds[8], 71), 0),
        "partner": draw_partner(jax.random.fold_in(seeds[8], 71), 0),
    }


THETA = 5000000.0
EPS = 1e-05

def rotate_pairs(values, positions):
    width = values.shape[-1]
    half_width = width // 2
    frequency = THETA ** (-2.0 * jnp.arange(half_width, dtype=jnp.float32) / width)
    angles = positions.astype(jnp.float32)[:, None] * frequency[None, :]
    cosine_part = jnp.cos(angles)[:, None, :]
    sine_part = jnp.sin(angles)[:, None, :]
    first_half = values[..., :half_width]
    second_half = values[..., half_width:]
    return jnp.concatenate([first_half * cosine_part - second_half * sine_part, second_half * cosine_part + first_half * sine_part], -1)

def row_owners(cache_len, partner, group_index, first_row, row_count):
    row_ids = first_row + jnp.arange(row_count, dtype=jnp.int32)
    lengths = lax.dynamic_slice_in_dim(cache_len, (group_index * R).astype(jnp.int32), R)
    stored = lengths.at[0].set(lengths[0] - lengths[0] // 2)
    bounds = jnp.concatenate([jnp.zeros((1,), jnp.int32), jnp.cumsum(stored).astype(jnp.int32)])
    far_count = cache_len[partner[group_index] * R] // 2
    owners = jnp.full((row_count,), -1, jnp.int32)
    for request in range(R):
        owners = jnp.where((row_ids >= bounds[request]) & (row_ids < bounds[request + 1]), request, owners)
    owners = jnp.where((row_ids >= bounds[R]) & (row_ids < bounds[R] + far_count), R, owners)
    return owners.astype(jnp.int32)

def reference(hidden, norm_gain, w_query, w_keyval, w_out, kv_cache, cache_len, partner):
    group_size = QH // KVH
    scale_factor = HD ** (-0.5)

    def one_group(group_index):
        float_rows = lax.dynamic_slice_in_dim(hidden, group_index * TOK_G, TOK_G, 0).astype(jnp.float32)
        normed = (float_rows * lax.rsqrt(lax.optimization_barrier(jnp.mean(float_rows * float_rows, -1, keepdims=True)) + EPS) * norm_gain).astype(jnp.bfloat16)
        query_raw = jnp.dot(normed, w_query, preferred_element_type=jnp.float32)
        keyval = jnp.dot(normed, w_keyval, preferred_element_type=jnp.float32).astype(jnp.bfloat16)
        lengths = lax.dynamic_slice_in_dim(cache_len, (group_index * R).astype(jnp.int32), R)
        positions = (lengths[:, None] + jnp.arange(C, dtype=jnp.int32)[None, :]).reshape(TOK_G)
        queries = rotate_pairs(query_raw.reshape(TOK_G, QH, HD), positions).astype(jnp.bfloat16)
        new_keys = rotate_pairs(keyval[:, :KVH * HD].astype(jnp.float32).reshape(TOK_G, KVH, HD), positions).astype(jnp.bfloat16)
        new_values = keyval[:, KVH * HD:]
        far_group = partner[group_index]
        own_rows = lax.dynamic_slice_in_dim(kv_cache, group_index * CACHE_G, CACHE_G, 0)
        far_rows = lax.dynamic_slice_in_dim(kv_cache, far_group * CACHE_G, CACHE_G, 0)
        own_ids = row_owners(cache_len, partner, group_index, 0, CACHE_G)
        far_ids = row_owners(cache_len, partner, far_group, 0, CACHE_G)
        token_index = jnp.arange(TOK_G, dtype=jnp.int32)
        request_of = token_index // C
        within = token_index % C
        seen_own = own_ids[None, :] == request_of[:, None]
        seen_far = (far_ids[None, :] == R) & (request_of[:, None] == 0)
        seen_new = (request_of[:, None] == request_of[None, :]) & (within[None, :] <= within[:, None])
        visible = jnp.concatenate([seen_own, seen_far, seen_new], 1)
        key_table = jnp.concatenate([own_rows[:, :KVH * HD], far_rows[:, :KVH * HD], new_keys.reshape(TOK_G, KVH * HD)], 0)
        value_table = jnp.concatenate([own_rows[:, KVH * HD:], far_rows[:, KVH * HD:], new_values], 0)

        def one_head(head_index):
            kv_head = head_index // group_size
            key_rows = lax.dynamic_slice_in_dim(key_table, kv_head * HD, HD, 1)
            value_rows = lax.dynamic_slice_in_dim(value_table, kv_head * HD, HD, 1)
            query_head = lax.dynamic_index_in_dim(queries, head_index, 1, keepdims=False)
            scores = jnp.dot(query_head, key_rows.T, preferred_element_type=jnp.float32) * scale_factor
            scores = jnp.where(visible, scores, -jnp.inf)
            row_peak = lax.optimization_barrier(jnp.max(scores, 1, keepdims=True))
            weights = jnp.where(visible, jnp.exp(scores - row_peak), 0.0)
            row_total = lax.optimization_barrier(jnp.sum(weights, 1))
            weighted = jnp.dot(weights.astype(jnp.bfloat16), value_rows, preferred_element_type=jnp.float32)
            return weighted / row_total[:, None]
        heads_out = lax.map(one_head, jnp.arange(QH, dtype=jnp.int32))
        attention = jnp.transpose(heads_out, (1, 0, 2)).reshape(TOK_G, QH * HD).astype(jnp.bfloat16)
        return jnp.dot(attention, w_out, preferred_element_type=jnp.float32).astype(jnp.bfloat16)
    results = lax.map(one_group, jnp.arange(GROUPS, dtype=jnp.int32))
    return results.reshape(TOKENS, D)
```

```python
import functools

import jax
import jax.numpy as jnp
from jax import lax
from jax.experimental import pallas as pl
from jax.experimental.pallas import tpu as pltpu
from jax.sharding import PartitionSpec as P

HD = 128
QH = 16
KVH = 2
C = 128
R = 2

THETA = 5000000.0
EPS = 1e-05
NEG = -1e30
CHUNK = 256
MESH = pl.DeviceIdType.MESH


def rotate_pairs(values, positions):
    width = values.shape[-1]
    half_width = width // 2
    frequency = THETA ** (-2.0 * jnp.arange(half_width, dtype=jnp.float32) / width)
    angles = positions.astype(jnp.float32)[:, None] * frequency[None, :]
    cosine_part = jnp.cos(angles)[:, None, :]
    sine_part = jnp.sin(angles)[:, None, :]
    first_half = values[..., :half_width]
    second_half = values[..., half_width:]
    return jnp.concatenate(
        [
            first_half * cosine_part - second_half * sine_part,
            second_half * cosine_part + first_half * sine_part,
        ],
        -1,
    )


def exchange_kernel(n, modes, *refs):
    count = len(modes)
    ins, outs = refs[:count], refs[count : 2 * count]
    send_sem, recv_sem = refs[2 * count :]
    me = lax.axis_index("tp")
    grp = lax.axis_index("grp")
    barrier = pltpu.get_barrier_semaphore()
    for step in range(1, n):
        pl.semaphore_signal(
            barrier, inc=1, device_id=(grp, lax.rem(me + step, n)), device_id_type=MESH
        )
    pl.semaphore_wait(barrier, n - 1)
    copies = []
    for index in range(count):
        for step in range(1, n):
            peer = lax.rem(me + step, n)
            source = ins[index] if modes[index] else ins[index].at[peer]
            copy = pltpu.make_async_remote_copy(
                src_ref=source,
                dst_ref=outs[index].at[me],
                send_sem=send_sem.at[index, step],
                recv_sem=recv_sem.at[index, step],
                device_id=(grp, peer),
                device_id_type=MESH,
            )
            copy.start()
            copies.append(copy)
        if modes[index]:
            outs[index][me] = ins[index][...]
        else:
            outs[index][me] = ins[index][me]
    for copy in copies:
        copy.wait()


def tp_exchange(arrays, modes, collective_id):
    n = lax.axis_size("tp")
    shapes = []
    for array, gather in zip(arrays, modes):
        block = array.shape if gather else array.shape[1:]
        shapes.append(jax.ShapeDtypeStruct((n,) + tuple(block), array.dtype))
    vmem = pl.BlockSpec(memory_space=pltpu.VMEM)
    return pl.pallas_call(
        functools.partial(exchange_kernel, n, tuple(modes)),
        out_shape=tuple(shapes),
        in_specs=[vmem] * len(arrays),
        out_specs=tuple([vmem] * len(arrays)),
        scratch_shapes=[
            pltpu.SemaphoreType.DMA((len(arrays), n)),
            pltpu.SemaphoreType.DMA((len(arrays), n)),
        ],
        compiler_params=pltpu.CompilerParams(
            collective_id=collective_id, has_side_effects=True, vmem_limit_bytes=48 * 1024 * 1024
        ),
    )(*arrays)


def attention_kernel(lo_ref, hi_ref, q_ref, cache_ref, mix_ref, peak_ref, total_ref, m_sc, l_sc, acc_sc):
    block = pl.program_id(0)
    kv_head = pl.program_id(1)
    lo = lo_ref[block]
    hi = hi_ref[block]
    heads, tokens, width = q_ref.shape
    query = q_ref[...].reshape(heads * tokens, width)
    m_sc[...] = jnp.full_like(m_sc, NEG)
    l_sc[...] = jnp.zeros_like(l_sc)
    acc_sc[...] = jnp.zeros_like(acc_sc)
    key_col = pl.multiple_of(kv_head * HD, HD)
    value_col = pl.multiple_of((KVH + kv_head) * HD, HD)
    first = lo // CHUNK
    last = jnp.where(hi > lo, (hi + CHUNK - 1) // CHUNK, first)

    def body(chunk, carry):
        start = pl.multiple_of(chunk * CHUNK, CHUNK)
        keys = cache_ref[pl.ds(start, CHUNK), pl.ds(key_col, HD)]
        values = cache_ref[pl.ds(start, CHUNK), pl.ds(value_col, HD)]
        scores = lax.dot_general(
            query, keys, (((1,), (1,)), ((), ())), preferred_element_type=jnp.float32
        ) * (HD ** (-0.5))
        rows = start + lax.broadcasted_iota(jnp.int32, (1, CHUNK), 1)
        seen = (rows >= lo) & (rows < hi)
        scores = jnp.where(seen, scores, -jnp.inf)
        old_peak = m_sc[...]
        new_peak = jnp.maximum(old_peak, jnp.max(scores, axis=1, keepdims=True))
        scale = jnp.exp(old_peak - new_peak)
        weights = jnp.exp(scores - new_peak)
        l_sc[...] = scale * l_sc[...] + jnp.sum(weights, axis=1, keepdims=True)
        acc_sc[...] = scale * acc_sc[...] + jnp.dot(
            weights.astype(jnp.bfloat16), values, preferred_element_type=jnp.float32
        )
        m_sc[...] = new_peak
        return carry

    lax.fori_loop(first, last, body, 0)
    mix_ref[...] = acc_sc[...].reshape(heads, tokens, width)
    peak_ref[...] = m_sc[...].reshape(heads, tokens, 1)
    total_ref[...] = l_sc[...].reshape(heads, tokens, 1)


def cache_attention(queries, cache_rows, lo, hi):
    heads, tokens, width = queries.shape
    blocks = tokens // C
    group_size = heads // KVH
    return pl.pallas_call(
        attention_kernel,
        out_shape=(
            jax.ShapeDtypeStruct((heads, tokens, width), jnp.float32),
            jax.ShapeDtypeStruct((heads, tokens, 1), jnp.float32),
            jax.ShapeDtypeStruct((heads, tokens, 1), jnp.float32),
        ),
        grid_spec=pltpu.PrefetchScalarGridSpec(
            num_scalar_prefetch=2,
            grid=(blocks, KVH),
            in_specs=[
                pl.BlockSpec((group_size, C, width), lambda b, j, lo, hi: (j, b, 0)),
                pl.BlockSpec(cache_rows.shape, lambda b, j, lo, hi: (0, 0)),
            ],
            out_specs=[
                pl.BlockSpec((group_size, C, width), lambda b, j, lo, hi: (j, b, 0)),
                pl.BlockSpec((group_size, C, 1), lambda b, j, lo, hi: (j, b, 0)),
                pl.BlockSpec((group_size, C, 1), lambda b, j, lo, hi: (j, b, 0)),
            ],
            scratch_shapes=[
                pltpu.VMEM((group_size * C, 1), jnp.float32),
                pltpu.VMEM((group_size * C, 1), jnp.float32),
                pltpu.VMEM((group_size * C, width), jnp.float32),
            ],
        ),
        compiler_params=pltpu.CompilerParams(vmem_limit_bytes=48 * 1024 * 1024),
    )(lo, hi, queries, cache_rows)


def join_partials(first, second):
    first_mix, first_peak, first_total = first
    second_mix, second_peak, second_total = second
    new_peak = jnp.maximum(first_peak, second_peak)
    first_scale = jnp.exp(first_peak - new_peak)
    second_scale = jnp.exp(second_peak - new_peak)
    joined_mix = first_mix * first_scale[..., None] + second_mix * second_scale[..., None]
    return (joined_mix, new_peak, first_total * first_scale + second_total * second_scale)


def to_partner(tree, flip_mask, groups):
    def branch(mask):
        pairs = [(i, i ^ mask) for i in range(groups)]
        return lambda t: jax.tree.map(lambda a: lax.ppermute(a, "grp", pairs), t)

    return lax.switch(flip_mask - 1, [branch(mask) for mask in range(1, groups)], tree)


def on_device(hidden, norm_gain, w_query, w_keyval, w_out, kv_cache, cache_len, partner):
    group_index = lax.axis_index("grp")
    tp_index = lax.axis_index("tp")
    tp_count = lax.axis_size("tp")
    groups = lax.axis_size("grp")
    local_heads = QH // tp_count
    rows_here = kv_cache.shape[0]
    token_count = hidden.shape[0]
    model_width = w_out.shape[1]
    out_width = model_width // tp_count
    flip_mask = partner[0]

    w_blocks = w_out.reshape(w_out.shape[0], tp_count, out_width).transpose(1, 0, 2)
    w_received = [lax.dynamic_index_in_dim(w_blocks, tp_index, 0, False)]
    for step in range(1, tp_count):
        send = lax.dynamic_index_in_dim(w_blocks, lax.rem(tp_index + step, tp_count), 0, False)
        pairs = [(i, (i + step) % tp_count) for i in range(tp_count)]
        w_received.append(lax.ppermute(send, "tp", pairs))

    float_rows = hidden.astype(jnp.float32)
    normed = (
        float_rows
        * lax.rsqrt(jnp.mean(float_rows * float_rows, -1, keepdims=True) + EPS)
        * norm_gain
    ).astype(jnp.bfloat16)
    query_raw = jnp.dot(normed, w_query, preferred_element_type=jnp.float32).reshape(
        token_count, local_heads, HD
    )
    keyval_part = jnp.dot(normed, w_keyval, preferred_element_type=jnp.float32).astype(jnp.bfloat16)
    lengths = lax.dynamic_slice_in_dim(cache_len, group_index * R, R)
    positions = (lengths[:, None] + jnp.arange(C, dtype=jnp.int32)[None, :]).reshape(token_count)
    query_local = rotate_pairs(query_raw, positions).astype(jnp.bfloat16).transpose(1, 0, 2)
    far_query = to_partner(query_local[:, :C], flip_mask, groups)
    query_ext = jnp.concatenate([query_local, far_query], 1)
    query_got, keyval_got = tp_exchange([query_ext, keyval_part], [True, True], 0)
    queries = query_got.reshape(QH, query_ext.shape[1], HD)
    keyval_all = keyval_got.transpose(1, 0, 2).reshape(token_count, -1)

    stored_first = lengths[0] - lengths[0] // 2
    bound_one = stored_first
    bound_two = stored_first + lengths[1]
    far_count = cache_len[partner[group_index] * R] // 2
    starts = jnp.stack([0, bound_one, bound_two]).astype(jnp.int32)
    ends = jnp.stack([bound_one, bound_two, bound_two + far_count]).astype(jnp.int32)
    offset = tp_index * rows_here
    lo = jnp.clip(starts - offset, 0, rows_here)
    hi = jnp.clip(ends - offset, 0, rows_here)
    mix, peak, total = cache_attention(queries, kv_cache, lo, hi)
    ext_tokens = mix.shape[1]
    mix_got, peak_got, total_got = tp_exchange(
        [
            mix.reshape(tp_count, local_heads, ext_tokens, HD),
            peak.reshape(tp_count, local_heads, ext_tokens),
            total.reshape(tp_count, local_heads, ext_tokens),
        ],
        [False, False, False],
        1,
    )
    top = jnp.max(peak_got, 0)
    scales = jnp.exp(peak_got - top[None])
    mix_c = jnp.sum(mix_got * scales[..., None], 0)
    total_c = jnp.sum(total_got * scales, 0)
    combined = (mix_c, top, total_c)
    far_back = to_partner(
        tuple(piece[:, token_count:] for piece in combined), flip_mask, groups
    )
    front = join_partials(tuple(piece[:, :C] for piece in combined), far_back)
    own = tuple(
        jnp.concatenate([front[i], combined[i][:, C:token_count]], 1) for i in range(3)
    )

    new_keys = rotate_pairs(
        keyval_all[:, : KVH * HD].astype(jnp.float32).reshape(token_count, KVH, HD), positions
    ).astype(jnp.bfloat16)
    new_values = keyval_all[:, KVH * HD :].reshape(token_count, KVH, HD)
    kv_head = (tp_index * local_heads) // (QH // KVH)
    key_rows = lax.dynamic_index_in_dim(new_keys, kv_head, 1, keepdims=False)
    value_rows = lax.dynamic_index_in_dim(new_values, kv_head, 1, keepdims=False)
    token_index = jnp.arange(token_count, dtype=jnp.int32)
    request_of = token_index // C
    within = token_index % C
    self_visible = (request_of[:, None] == request_of[None, :]) & (
        within[None, :] <= within[:, None]
    )
    self_scores = jnp.einsum(
        "htd,sd->hts", query_local, key_rows, preferred_element_type=jnp.float32
    ) * HD ** (-0.5)
    self_scores = jnp.where(self_visible[None], self_scores, -jnp.inf)
    self_peak = jnp.max(self_scores, -1)
    self_weights = jnp.exp(self_scores - self_peak[..., None])
    self_total = jnp.sum(self_weights, -1)
    self_mix = jnp.einsum(
        "hts,sd->htd", self_weights.astype(jnp.bfloat16), value_rows,
        preferred_element_type=jnp.float32,
    )
    final_mix, final_peak, final_total = join_partials(own, (self_mix, self_peak, self_total))
    attention = (final_mix / final_total[..., None]).astype(jnp.bfloat16)
    attention = attention.transpose(1, 0, 2).reshape(token_count, local_heads * HD)
    (attention_got,) = tp_exchange([attention], [True], 2)
    out = None
    for step in range(tp_count):
        source = lax.rem(tp_index - step + tp_count, tp_count)
        piece = jnp.dot(
            lax.dynamic_index_in_dim(attention_got, source, 0, False),
            w_received[step],
            preferred_element_type=jnp.float32,
        )
        out = piece if out is None else out + piece
    return out.astype(jnp.bfloat16)


def solution(mesh):
    placed = (
        P("grp", None),
        P(),
        P(None, "tp"),
        P(None, "tp"),
        P("tp", None),
        P(("grp", "tp"), None),
        P(),
        P(),
    )
    return jax.shard_map(
        on_device, mesh=mesh, in_specs=placed, out_specs=P("grp", "tp"), check_vma=False
    )
```

```python
import functools

import jax
import jax.numpy as jnp
from jax import lax
from jax.experimental import pallas as pl
from jax.experimental.pallas import tpu as pltpu
from jax.sharding import PartitionSpec as P

HD = 128
QH = 16
KVH = 2
C = 128
R = 2

THETA = 5000000.0
EPS = 1e-05
NEG = -1e30
CHUNK = 256
MESH = pl.DeviceIdType.MESH


def rotate_pairs(values, positions):
    width = values.shape[-1]
    half_width = width // 2
    frequency = THETA ** (-2.0 * jnp.arange(half_width, dtype=jnp.float32) / width)
    angles = positions.astype(jnp.float32)[:, None] * frequency[None, :]
    cosine_part = jnp.cos(angles)[:, None, :]
    sine_part = jnp.sin(angles)[:, None, :]
    first_half = values[..., :half_width]
    second_half = values[..., half_width:]
    return jnp.concatenate(
        [
            first_half * cosine_part - second_half * sine_part,
            second_half * cosine_part + first_half * sine_part,
        ],
        -1,
    )


def exchange_kernel(count, stride, modes, *refs):
    arrays = len(modes)
    ins, outs = refs[:arrays], refs[arrays : 2 * arrays]
    send_sem, recv_sem = refs[2 * arrays :]
    me = lax.axis_index("tp")
    grp = lax.axis_index("grp")
    mine = lax.rem(me // stride, count)
    base = me - mine * stride

    def member(step):
        return lax.rem(mine + step, count)

    barrier = pltpu.get_barrier_semaphore()
    for step in range(1, count):
        pl.semaphore_signal(
            barrier, inc=1, device_id=(grp, base + member(step) * stride), device_id_type=MESH
        )
    pl.semaphore_wait(barrier, count - 1)
    copies = []
    for index in range(arrays):
        for step in range(1, count):
            peer = member(step)
            source = ins[index] if modes[index] else ins[index].at[peer]
            copy = pltpu.make_async_remote_copy(
                src_ref=source,
                dst_ref=outs[index].at[mine],
                send_sem=send_sem.at[index, step],
                recv_sem=recv_sem.at[index, step],
                device_id=(grp, base + peer * stride),
                device_id_type=MESH,
            )
            copy.start()
            copies.append(copy)
        if modes[index]:
            outs[index][mine] = ins[index][...]
        else:
            outs[index][mine] = ins[index][mine]
    for copy in copies:
        copy.wait()


def tp_exchange(arrays, modes, collective_id, count=None, stride=1):
    count = lax.axis_size("tp") if count is None else count
    shapes = []
    for array, gather in zip(arrays, modes):
        block = array.shape if gather else array.shape[1:]
        shapes.append(jax.ShapeDtypeStruct((count,) + tuple(block), array.dtype))
    vmem = pl.BlockSpec(memory_space=pltpu.VMEM)
    return pl.pallas_call(
        functools.partial(exchange_kernel, count, stride, tuple(modes)),
        out_shape=tuple(shapes),
        in_specs=[vmem] * len(arrays),
        out_specs=tuple([vmem] * len(arrays)),
        scratch_shapes=[
            pltpu.SemaphoreType.DMA((len(arrays), count)),
            pltpu.SemaphoreType.DMA((len(arrays), count)),
        ],
        compiler_params=pltpu.CompilerParams(
            collective_id=collective_id, has_side_effects=True, vmem_limit_bytes=48 * 1024 * 1024
        ),
    )(*arrays)


def attention_kernel(lo_ref, hi_ref, q_ref, cache_ref, mix_ref, peak_ref, total_ref, m_sc, l_sc, acc_sc):
    block = pl.program_id(0)
    kv_head = pl.program_id(1)
    lo = lo_ref[block]
    hi = hi_ref[block]
    heads, tokens, width = q_ref.shape
    query = q_ref[...].reshape(heads * tokens, width)
    m_sc[...] = jnp.full_like(m_sc, NEG)
    l_sc[...] = jnp.zeros_like(l_sc)
    acc_sc[...] = jnp.zeros_like(acc_sc)
    key_col = pl.multiple_of(kv_head * HD, HD)
    value_col = pl.multiple_of((KVH + kv_head) * HD, HD)
    first = lo // CHUNK
    last = jnp.where(hi > lo, (hi + CHUNK - 1) // CHUNK, first)

    def body(chunk, carry):
        start = pl.multiple_of(chunk * CHUNK, CHUNK)
        keys = cache_ref[pl.ds(start, CHUNK), pl.ds(key_col, HD)]
        values = cache_ref[pl.ds(start, CHUNK), pl.ds(value_col, HD)]
        scores = lax.dot_general(
            query, keys, (((1,), (1,)), ((), ())), preferred_element_type=jnp.float32
        ) * (HD ** (-0.5))
        rows = start + lax.broadcasted_iota(jnp.int32, (1, CHUNK), 1)
        seen = (rows >= lo) & (rows < hi)
        scores = jnp.where(seen, scores, -jnp.inf)
        old_peak = m_sc[...]
        new_peak = jnp.maximum(old_peak, jnp.max(scores, axis=1, keepdims=True))
        scale = jnp.exp(old_peak - new_peak)
        weights = jnp.exp(scores - new_peak)
        l_sc[...] = scale * l_sc[...] + jnp.sum(weights, axis=1, keepdims=True)
        acc_sc[...] = scale * acc_sc[...] + jnp.dot(
            weights.astype(jnp.bfloat16), values, preferred_element_type=jnp.float32
        )
        m_sc[...] = new_peak
        return carry

    lax.fori_loop(first, last, body, 0)
    mix_ref[...] = acc_sc[...].reshape(heads, tokens, width)
    peak_ref[...] = m_sc[...].reshape(heads, tokens, 1)
    total_ref[...] = l_sc[...].reshape(heads, tokens, 1)


def cache_attention(queries, cache_rows, lo, hi):
    heads, tokens, width = queries.shape
    blocks = tokens // C
    group_size = heads // KVH
    return pl.pallas_call(
        attention_kernel,
        out_shape=(
            jax.ShapeDtypeStruct((heads, tokens, width), jnp.float32),
            jax.ShapeDtypeStruct((heads, tokens, 1), jnp.float32),
            jax.ShapeDtypeStruct((heads, tokens, 1), jnp.float32),
        ),
        grid_spec=pltpu.PrefetchScalarGridSpec(
            num_scalar_prefetch=2,
            grid=(blocks, KVH),
            in_specs=[
                pl.BlockSpec((group_size, C, width), lambda b, j, lo, hi: (j, b, 0)),
                pl.BlockSpec(cache_rows.shape, lambda b, j, lo, hi: (0, 0)),
            ],
            out_specs=[
                pl.BlockSpec((group_size, C, width), lambda b, j, lo, hi: (j, b, 0)),
                pl.BlockSpec((group_size, C, 1), lambda b, j, lo, hi: (j, b, 0)),
                pl.BlockSpec((group_size, C, 1), lambda b, j, lo, hi: (j, b, 0)),
            ],
            scratch_shapes=[
                pltpu.VMEM((group_size * C, 1), jnp.float32),
                pltpu.VMEM((group_size * C, 1), jnp.float32),
                pltpu.VMEM((group_size * C, width), jnp.float32),
            ],
        ),
        compiler_params=pltpu.CompilerParams(vmem_limit_bytes=48 * 1024 * 1024),
    )(lo, hi, queries, cache_rows)


def join_partials(first, second):
    first_mix, first_peak, first_total = first
    second_mix, second_peak, second_total = second
    new_peak = jnp.maximum(first_peak, second_peak)
    first_scale = jnp.exp(first_peak - new_peak)
    second_scale = jnp.exp(second_peak - new_peak)
    joined_mix = first_mix * first_scale[..., None] + second_mix * second_scale[..., None]
    return (joined_mix, new_peak, first_total * first_scale + second_total * second_scale)


def to_partner(tree, flip_mask, groups):
    def branch(mask):
        pairs = [(i, i ^ mask) for i in range(groups)]
        return lambda t: jax.tree.map(lambda a: lax.ppermute(a, "grp", pairs), t)

    return lax.switch(flip_mask - 1, [branch(mask) for mask in range(1, groups)], tree)


def on_device(hidden, norm_gain, w_query, w_keyval, w_out, kv_cache, cache_len, partner):
    group_index = lax.axis_index("grp")
    tp_index = lax.axis_index("tp")
    tp_count = lax.axis_size("tp")
    groups = lax.axis_size("grp")
    ring = tp_count // 2
    ring_at = tp_index // 2
    side = tp_index % 2
    local_heads = QH // tp_count
    rows_here = kv_cache.shape[0]
    token_count = hidden.shape[0]
    model_width = w_out.shape[1]
    out_width = model_width // tp_count
    flip_mask = partner[0]

    w_blocks = w_out.reshape(w_out.shape[0], ring, 2 * out_width).transpose(1, 0, 2)
    w_received = [lax.dynamic_index_in_dim(w_blocks, ring_at, 0, False)]
    for step in range(1, ring):
        send = lax.dynamic_index_in_dim(w_blocks, lax.rem(ring_at + step, ring), 0, False)
        pairs = [(i, (i + 2 * step) % tp_count) for i in range(tp_count)]
        w_received.append(lax.ppermute(send, "tp", pairs))

    float_rows = hidden.astype(jnp.float32)
    normed = (
        float_rows
        * lax.rsqrt(jnp.mean(float_rows * float_rows, -1, keepdims=True) + EPS)
        * norm_gain
    ).astype(jnp.bfloat16)
    query_raw = jnp.dot(normed, w_query, preferred_element_type=jnp.float32).reshape(
        token_count, local_heads, HD
    )
    keyval_part = jnp.dot(normed, w_keyval, preferred_element_type=jnp.float32).astype(jnp.bfloat16)
    lengths = lax.dynamic_slice_in_dim(cache_len, group_index * R, R)
    positions = (lengths[:, None] + jnp.arange(C, dtype=jnp.int32)[None, :]).reshape(token_count)
    query_local = rotate_pairs(query_raw, positions).astype(jnp.bfloat16).transpose(1, 0, 2)
    far_query = to_partner(query_local[:, :C], flip_mask, groups)
    query_ext = jnp.concatenate([query_local, far_query], 1)
    ext_tokens = query_ext.shape[1]
    query_pair, keyval_pair = tp_exchange([query_ext, keyval_part], [True, True], 0, 2, 1)
    query_got, keyval_got = tp_exchange([query_pair, keyval_pair], [True, True], 1, ring, 2)
    queries = query_got.reshape(QH, ext_tokens, HD)
    keyval_all = keyval_got.reshape(tp_count, token_count, -1).transpose(1, 0, 2).reshape(
        token_count, -1
    )

    stored_first = lengths[0] - lengths[0] // 2
    bound_one = stored_first
    bound_two = stored_first + lengths[1]
    far_count = cache_len[partner[group_index] * R] // 2
    starts = jnp.stack([0, bound_one, bound_two]).astype(jnp.int32)
    ends = jnp.stack([bound_one, bound_two, bound_two + far_count]).astype(jnp.int32)
    offset = tp_index * rows_here
    lo = jnp.clip(starts - offset, 0, rows_here)
    hi = jnp.clip(ends - offset, 0, rows_here)
    mix, peak, total = cache_attention(queries, kv_cache, lo, hi)
    mix_got, peak_got, total_got = tp_exchange(
        [
            mix.astype(jnp.bfloat16).reshape(tp_count, local_heads, ext_tokens, HD),
            peak.reshape(tp_count, local_heads, ext_tokens),
            total.reshape(tp_count, local_heads, ext_tokens),
        ],
        [False, False, False],
        2,
    )
    top = jnp.max(peak_got, 0)
    scales = jnp.exp(peak_got - top[None])
    mix_c = jnp.sum(mix_got.astype(jnp.float32) * scales[..., None], 0)
    total_c = jnp.sum(total_got * scales, 0)
    far_pack = jnp.concatenate(
        [
            mix_c[:, token_count:],
            top[:, None, token_count:],
            total_c[:, None, token_count:],
        ],
        1,
    )
    far_pack = to_partner(far_pack, flip_mask, groups)
    far_back = (far_pack[:, :C], far_pack[:, C], far_pack[:, C + 1])
    combined = (mix_c[:, :token_count], top[:, :token_count], total_c[:, :token_count])
    front = join_partials(tuple(piece[:, :C] for piece in combined), far_back)
    own = tuple(jnp.concatenate([front[i], combined[i][:, C:]], 1) for i in range(3))

    new_keys = rotate_pairs(
        keyval_all[:, : KVH * HD].astype(jnp.float32).reshape(token_count, KVH, HD), positions
    ).astype(jnp.bfloat16)
    new_values = keyval_all[:, KVH * HD :].reshape(token_count, KVH, HD)
    kv_head = (tp_index * local_heads) // (QH // KVH)
    key_rows = lax.dynamic_index_in_dim(new_keys, kv_head, 1, keepdims=False)
    value_rows = lax.dynamic_index_in_dim(new_values, kv_head, 1, keepdims=False)
    token_index = jnp.arange(token_count, dtype=jnp.int32)
    request_of = token_index // C
    within = token_index % C
    self_visible = (request_of[:, None] == request_of[None, :]) & (
        within[None, :] <= within[:, None]
    )
    self_scores = jnp.einsum(
        "htd,sd->hts", query_local, key_rows, preferred_element_type=jnp.float32
    ) * HD ** (-0.5)
    self_scores = jnp.where(self_visible[None], self_scores, -jnp.inf)
    self_peak = jnp.max(self_scores, -1)
    self_weights = jnp.exp(self_scores - self_peak[..., None])
    self_total = jnp.sum(self_weights, -1)
    self_mix = jnp.einsum(
        "hts,sd->htd", self_weights.astype(jnp.bfloat16), value_rows,
        preferred_element_type=jnp.float32,
    )
    final_mix, final_peak, final_total = join_partials(own, (self_mix, self_peak, self_total))
    attention = (final_mix / final_total[..., None]).astype(jnp.bfloat16)
    attention = attention.transpose(1, 0, 2).reshape(token_count, local_heads * HD)
    (attention_ring,) = tp_exchange([attention], [True], 3, ring, 2)
    sums = None
    for step in range(ring):
        source = lax.rem(ring_at - step + ring, ring)
        piece = jnp.dot(
            lax.dynamic_index_in_dim(attention_ring, source, 0, False),
            w_received[step],
            preferred_element_type=jnp.float32,
        )
        sums = piece if sums is None else sums + piece
    halves = sums.reshape(token_count, 2, out_width).transpose(1, 0, 2)
    (halves_got,) = tp_exchange([halves], [False], 4, 2, 1)
    return (halves_got[0] + halves_got[1]).astype(jnp.bfloat16)


def solution(mesh):
    placed = (
        P("grp", None),
        P(),
        P(None, "tp"),
        P(None, "tp"),
        P("tp", None),
        P(("grp", "tp"), None),
        P(),
        P(),
    )
    return jax.shard_map(
        on_device, mesh=mesh, in_specs=placed, out_specs=P("grp", "tp"), check_vma=False
    )
```

```python
import functools

import jax
import jax.numpy as jnp
from jax import lax
from jax.experimental import pallas as pl
from jax.experimental.pallas import tpu as pltpu
from jax.sharding import PartitionSpec as P

HD = 128
QH = 16
KVH = 2
C = 128
R = 2

THETA = 5000000.0
EPS = 1e-05
NEG = -1e30
CHUNK = 256
MESH = pl.DeviceIdType.MESH


def rotate_pairs(values, positions):
    width = values.shape[-1]
    half_width = width // 2
    frequency = THETA ** (-2.0 * jnp.arange(half_width, dtype=jnp.float32) / width)
    angles = positions.astype(jnp.float32)[:, None] * frequency[None, :]
    cosine_part = jnp.cos(angles)[:, None, :]
    sine_part = jnp.sin(angles)[:, None, :]
    first_half = values[..., :half_width]
    second_half = values[..., half_width:]
    return jnp.concatenate(
        [
            first_half * cosine_part - second_half * sine_part,
            second_half * cosine_part + first_half * sine_part,
        ],
        -1,
    )


def exchange_kernel(count, stride, modes, *refs):
    arrays = len(modes)
    ins, outs = refs[:arrays], refs[arrays : 2 * arrays]
    send_sem, recv_sem = refs[2 * arrays :]
    me = lax.axis_index("tp")
    grp = lax.axis_index("grp")
    mine = lax.rem(me // stride, count)
    base = me - mine * stride

    def member(step):
        return lax.rem(mine + step, count)

    barrier = pltpu.get_barrier_semaphore()
    for step in range(1, count):
        pl.semaphore_signal(
            barrier, inc=1, device_id=(grp, base + member(step) * stride), device_id_type=MESH
        )
    pl.semaphore_wait(barrier, count - 1)
    copies = []
    for index in range(arrays):
        for step in range(1, count):
            peer = member(step)
            source = ins[index] if modes[index] else ins[index].at[peer]
            copy = pltpu.make_async_remote_copy(
                src_ref=source,
                dst_ref=outs[index].at[mine],
                send_sem=send_sem.at[index, step],
                recv_sem=recv_sem.at[index, step],
                device_id=(grp, base + peer * stride),
                device_id_type=MESH,
            )
            copy.start()
            copies.append(copy)
        if modes[index]:
            outs[index][mine] = ins[index][...]
        else:
            outs[index][mine] = ins[index][mine]
    for copy in copies:
        copy.wait()


def tp_exchange(arrays, modes, collective_id, count=None, stride=1):
    count = lax.axis_size("tp") if count is None else count
    shapes = []
    for array, gather in zip(arrays, modes):
        block = array.shape if gather else array.shape[1:]
        shapes.append(jax.ShapeDtypeStruct((count,) + tuple(block), array.dtype))
    vmem = pl.BlockSpec(memory_space=pltpu.VMEM)
    return pl.pallas_call(
        functools.partial(exchange_kernel, count, stride, tuple(modes)),
        out_shape=tuple(shapes),
        in_specs=[vmem] * len(arrays),
        out_specs=tuple([vmem] * len(arrays)),
        scratch_shapes=[
            pltpu.SemaphoreType.DMA((len(arrays), count)),
            pltpu.SemaphoreType.DMA((len(arrays), count)),
        ],
        compiler_params=pltpu.CompilerParams(
            collective_id=collective_id, has_side_effects=True, vmem_limit_bytes=48 * 1024 * 1024
        ),
    )(*arrays)


def attention_kernel(lo_ref, hi_ref, q_ref, cache_ref, mix_ref, peak_ref, total_ref, m_sc, l_sc, acc_sc):
    block = pl.program_id(0)
    kv_head = pl.program_id(1)
    lo = lo_ref[block]
    hi = hi_ref[block]
    heads, tokens, width = q_ref.shape
    query = q_ref[...].reshape(heads * tokens, width)
    m_sc[...] = jnp.full_like(m_sc, NEG)
    l_sc[...] = jnp.zeros_like(l_sc)
    acc_sc[...] = jnp.zeros_like(acc_sc)
    key_col = pl.multiple_of(kv_head * HD, HD)
    value_col = pl.multiple_of((KVH + kv_head) * HD, HD)
    first = lo // CHUNK
    last = jnp.where(hi > lo, (hi + CHUNK - 1) // CHUNK, first)

    def body(chunk, carry):
        start = pl.multiple_of(chunk * CHUNK, CHUNK)
        keys = cache_ref[pl.ds(start, CHUNK), pl.ds(key_col, HD)]
        values = cache_ref[pl.ds(start, CHUNK), pl.ds(value_col, HD)]
        rows = start + lax.broadcasted_iota(jnp.int32, (1, CHUNK), 1)
        bias = jnp.where((rows >= lo) & (rows < hi), 0.0, -jnp.inf)
        scores = lax.dot_general(
            query, keys, (((1,), (1,)), ((), ())), preferred_element_type=jnp.float32
        ) * (HD ** (-0.5)) + bias
        old_peak = m_sc[...]
        new_peak = jnp.maximum(old_peak, jnp.max(scores, axis=1, keepdims=True))
        scale = jnp.exp(old_peak - new_peak)
        weights = jnp.exp(scores - new_peak)
        l_sc[...] = scale * l_sc[...] + jnp.sum(weights, axis=1, keepdims=True)
        acc_sc[...] = scale * acc_sc[...] + jnp.dot(
            weights.astype(jnp.bfloat16), values, preferred_element_type=jnp.float32
        )
        m_sc[...] = new_peak
        return carry

    lax.fori_loop(first, last, body, 0)
    mix_ref[...] = acc_sc[...].reshape(heads, tokens, width)
    peak_ref[...] = m_sc[...].reshape(heads, tokens, 1)
    total_ref[...] = l_sc[...].reshape(heads, tokens, 1)


def cache_attention(queries, cache_rows, lo, hi):
    heads, tokens, width = queries.shape
    blocks = tokens // C
    group_size = heads // KVH
    return pl.pallas_call(
        attention_kernel,
        out_shape=(
            jax.ShapeDtypeStruct((heads, tokens, width), jnp.float32),
            jax.ShapeDtypeStruct((heads, tokens, 1), jnp.float32),
            jax.ShapeDtypeStruct((heads, tokens, 1), jnp.float32),
        ),
        grid_spec=pltpu.PrefetchScalarGridSpec(
            num_scalar_prefetch=2,
            grid=(blocks, KVH),
            in_specs=[
                pl.BlockSpec((group_size, C, width), lambda b, j, lo, hi: (j, b, 0)),
                pl.BlockSpec(cache_rows.shape, lambda b, j, lo, hi: (0, 0)),
            ],
            out_specs=[
                pl.BlockSpec((group_size, C, width), lambda b, j, lo, hi: (j, b, 0)),
                pl.BlockSpec((group_size, C, 1), lambda b, j, lo, hi: (j, b, 0)),
                pl.BlockSpec((group_size, C, 1), lambda b, j, lo, hi: (j, b, 0)),
            ],
            scratch_shapes=[
                pltpu.VMEM((group_size * C, 1), jnp.float32),
                pltpu.VMEM((group_size * C, 1), jnp.float32),
                pltpu.VMEM((group_size * C, width), jnp.float32),
            ],
        ),
        compiler_params=pltpu.CompilerParams(vmem_limit_bytes=48 * 1024 * 1024),
    )(lo, hi, queries, cache_rows)


def join_partials(first, second):
    first_mix, first_peak, first_total = first
    second_mix, second_peak, second_total = second
    new_peak = jnp.maximum(first_peak, second_peak)
    first_scale = jnp.exp(first_peak - new_peak)
    second_scale = jnp.exp(second_peak - new_peak)
    joined_mix = first_mix * first_scale[..., None] + second_mix * second_scale[..., None]
    return (joined_mix, new_peak, first_total * first_scale + second_total * second_scale)


def to_partner(tree, flip_mask, groups):
    def branch(mask):
        pairs = [(i, i ^ mask) for i in range(groups)]
        return lambda t: jax.tree.map(lambda a: lax.ppermute(a, "grp", pairs), t)

    return lax.switch(flip_mask - 1, [branch(mask) for mask in range(1, groups)], tree)


def on_device(hidden, norm_gain, w_query, w_keyval, w_out, kv_cache, cache_len, partner):
    group_index = lax.axis_index("grp")
    tp_index = lax.axis_index("tp")
    tp_count = lax.axis_size("tp")
    groups = lax.axis_size("grp")
    ring = tp_count // 2
    ring_at = tp_index // 2
    side = tp_index % 2
    local_heads = QH // tp_count
    rows_here = kv_cache.shape[0]
    token_count = hidden.shape[0]
    model_width = w_out.shape[1]
    out_width = model_width // tp_count
    flip_mask = partner[0]

    def w_block(member):
        return lax.dynamic_slice_in_dim(w_out, member * 2 * out_width, 2 * out_width, 1)

    w_received = [w_block(ring_at)]
    for step in range(1, ring):
        send = w_block(lax.rem(ring_at + step, ring))
        pairs = [(i, (i + 2 * step) % tp_count) for i in range(tp_count)]
        w_received.append(lax.ppermute(send, "tp", pairs))

    float_rows = hidden.astype(jnp.float32)
    normed = (
        float_rows
        * lax.rsqrt(jnp.mean(float_rows * float_rows, -1, keepdims=True) + EPS)
        * norm_gain
    ).astype(jnp.bfloat16)
    query_raw = jnp.dot(normed, w_query, preferred_element_type=jnp.float32).reshape(
        token_count, local_heads, HD
    )
    keyval_part = jnp.dot(normed, w_keyval, preferred_element_type=jnp.float32).astype(jnp.bfloat16)
    lengths = lax.dynamic_slice_in_dim(cache_len, group_index * R, R)
    positions = (lengths[:, None] + jnp.arange(C, dtype=jnp.int32)[None, :]).reshape(token_count)
    query_local = rotate_pairs(query_raw, positions).astype(jnp.bfloat16).transpose(1, 0, 2)
    far_query = to_partner(query_local[:, :C], flip_mask, groups)
    query_ext = jnp.concatenate([query_local, far_query], 1)
    ext_tokens = query_ext.shape[1]
    query_pair, keyval_pair = tp_exchange([query_ext, keyval_part], [True, True], 0, 2, 1)
    query_got, keyval_got = tp_exchange([query_pair, keyval_pair], [True, True], 1, ring, 2)
    queries = query_got.reshape(QH, ext_tokens, HD)
    keyval_all = keyval_got.reshape(tp_count, token_count, -1).transpose(1, 0, 2).reshape(
        token_count, -1
    )

    stored_first = lengths[0] - lengths[0] // 2
    bound_one = stored_first
    bound_two = stored_first + lengths[1]
    far_count = cache_len[partner[group_index] * R] // 2
    starts = jnp.stack([0, bound_one, bound_two]).astype(jnp.int32)
    ends = jnp.stack([bound_one, bound_two, bound_two + far_count]).astype(jnp.int32)
    offset = tp_index * rows_here
    lo = jnp.clip(starts - offset, 0, rows_here)
    hi = jnp.clip(ends - offset, 0, rows_here)
    mix, peak, total = cache_attention(queries, kv_cache, lo, hi)
    mix_got, peak_got, total_got = tp_exchange(
        [
            mix.astype(jnp.bfloat16).reshape(tp_count, local_heads, ext_tokens, HD),
            peak.reshape(tp_count, local_heads, ext_tokens),
            total.reshape(tp_count, local_heads, ext_tokens),
        ],
        [False, False, False],
        2,
    )
    top = jnp.max(peak_got, 0)
    scales = jnp.exp(peak_got - top[None])
    mix_c = jnp.sum(mix_got.astype(jnp.float32) * scales[..., None], 0)
    total_c = jnp.sum(total_got * scales, 0)
    far_pack = jnp.concatenate(
        [
            mix_c[:, token_count:],
            top[:, None, token_count:],
            total_c[:, None, token_count:],
        ],
        1,
    )
    far_pack = to_partner(far_pack, flip_mask, groups)
    far_back = (far_pack[:, :C], far_pack[:, C], far_pack[:, C + 1])
    combined = (mix_c[:, :token_count], top[:, :token_count], total_c[:, :token_count])
    front = join_partials(tuple(piece[:, :C] for piece in combined), far_back)
    own = tuple(jnp.concatenate([front[i], combined[i][:, C:]], 1) for i in range(3))

    new_keys = rotate_pairs(
        keyval_all[:, : KVH * HD].astype(jnp.float32).reshape(token_count, KVH, HD), positions
    ).astype(jnp.bfloat16)
    new_values = keyval_all[:, KVH * HD :].reshape(token_count, KVH, HD)
    kv_head = (tp_index * local_heads) // (QH // KVH)
    key_rows = lax.dynamic_index_in_dim(new_keys, kv_head, 1, keepdims=False)
    value_rows = lax.dynamic_index_in_dim(new_values, kv_head, 1, keepdims=False)
    token_index = jnp.arange(token_count, dtype=jnp.int32)
    request_of = token_index // C
    within = token_index % C
    self_visible = (request_of[:, None] == request_of[None, :]) & (
        within[None, :] <= within[:, None]
    )
    self_scores = jnp.einsum(
        "htd,sd->hts", query_local, key_rows, preferred_element_type=jnp.float32
    ) * HD ** (-0.5)
    self_scores = jnp.where(self_visible[None], self_scores, -jnp.inf)
    self_peak = jnp.max(self_scores, -1)
    self_weights = jnp.exp(self_scores - self_peak[..., None])
    self_total = jnp.sum(self_weights, -1)
    self_mix = jnp.einsum(
        "hts,sd->htd", self_weights.astype(jnp.bfloat16), value_rows,
        preferred_element_type=jnp.float32,
    )
    final_mix, final_peak, final_total = join_partials(own, (self_mix, self_peak, self_total))
    attention = (final_mix / final_total[..., None]).astype(jnp.bfloat16)
    attention = attention.transpose(1, 0, 2).reshape(token_count, local_heads * HD)
    (attention_ring,) = tp_exchange([attention], [True], 3, ring, 2)
    sums = None
    for step in range(ring):
        source = lax.rem(ring_at - step + ring, ring)
        piece = jnp.dot(
            lax.dynamic_index_in_dim(attention_ring, source, 0, False),
            w_received[step],
            preferred_element_type=jnp.float32,
        )
        sums = piece if sums is None else sums + piece
    halves = sums.reshape(token_count, 2, out_width).transpose(1, 0, 2)
    (halves_got,) = tp_exchange([halves.astype(jnp.bfloat16)], [False], 4, 2, 1)
    mine = lax.dynamic_index_in_dim(halves, side, 0, False)
    other = lax.dynamic_index_in_dim(halves_got, 1 - side, 0, False)
    return (mine + other.astype(jnp.float32)).astype(jnp.bfloat16)


def solution(mesh):
    placed = (
        P("grp", None),
        P(),
        P(None, "tp"),
        P(None, "tp"),
        P("tp", None),
        P(("grp", "tp"), None),
        P(),
        P(),
    )
    return jax.shard_map(
        on_device, mesh=mesh, in_specs=placed, out_specs=P("grp", "tp"), check_vma=False
    )
```

```python
import functools

import jax
import jax.numpy as jnp
from jax import lax
from jax.experimental import pallas as pl
from jax.experimental.pallas import tpu as pltpu
from jax.sharding import PartitionSpec as P

HD = 128
QH = 16
KVH = 2
C = 128
R = 2

THETA = 5000000.0
EPS = 1e-05
NEG = -1e30
CHUNK = 256
MESH = pl.DeviceIdType.MESH


def rotate_pairs(values, positions):
    width = values.shape[-1]
    half_width = width // 2
    frequency = THETA ** (-2.0 * jnp.arange(half_width, dtype=jnp.float32) / width)
    angles = positions.astype(jnp.float32)[:, None] * frequency[None, :]
    cosine_part = jnp.cos(angles)[:, None, :]
    sine_part = jnp.sin(angles)[:, None, :]
    first_half = values[..., :half_width]
    second_half = values[..., half_width:]
    return jnp.concatenate(
        [
            first_half * cosine_part - second_half * sine_part,
            second_half * cosine_part + first_half * sine_part,
        ],
        -1,
    )


def exchange_kernel(count, stride, modes, *refs):
    arrays = len(modes)
    ins, outs = refs[:arrays], refs[arrays : 2 * arrays]
    send_sem, recv_sem = refs[2 * arrays :]
    me = lax.axis_index("tp")
    grp = lax.axis_index("grp")
    mine = lax.rem(me // stride, count)
    base = me - mine * stride

    def member(step):
        return lax.rem(mine + step, count)

    barrier = pltpu.get_barrier_semaphore()
    for step in range(1, count):
        pl.semaphore_signal(
            barrier, inc=1, device_id=(grp, base + member(step) * stride), device_id_type=MESH
        )
    pl.semaphore_wait(barrier, count - 1)
    copies = []
    for index in range(arrays):
        for step in range(1, count):
            peer = member(step)
            source = ins[index] if modes[index] else ins[index].at[peer]
            copy = pltpu.make_async_remote_copy(
                src_ref=source,
                dst_ref=outs[index].at[mine],
                send_sem=send_sem.at[index, step],
                recv_sem=recv_sem.at[index, step],
                device_id=(grp, base + peer * stride),
                device_id_type=MESH,
            )
            copy.start()
            copies.append(copy)
        if modes[index]:
            outs[index][mine] = ins[index][...]
        else:
            outs[index][mine] = ins[index][mine]
    for copy in copies:
        copy.wait()


def tp_exchange(arrays, modes, collective_id, count=None, stride=1):
    count = lax.axis_size("tp") if count is None else count
    shapes = []
    for array, gather in zip(arrays, modes):
        block = array.shape if gather else array.shape[1:]
        shapes.append(jax.ShapeDtypeStruct((count,) + tuple(block), array.dtype))
    vmem = pl.BlockSpec(memory_space=pltpu.VMEM)
    return pl.pallas_call(
        functools.partial(exchange_kernel, count, stride, tuple(modes)),
        out_shape=tuple(shapes),
        in_specs=[vmem] * len(arrays),
        out_specs=tuple([vmem] * len(arrays)),
        scratch_shapes=[
            pltpu.SemaphoreType.DMA((len(arrays), count)),
            pltpu.SemaphoreType.DMA((len(arrays), count)),
        ],
        compiler_params=pltpu.CompilerParams(
            collective_id=collective_id, has_side_effects=True, vmem_limit_bytes=48 * 1024 * 1024
        ),
    )(*arrays)


def relay_kernel(modes, *refs):
    count = len(modes)
    ins, outs, stage = refs[:count], refs[count : 2 * count], refs[2 * count : 3 * count]
    leg_send, leg_recv, hop_send, hop_recv = refs[3 * count :]
    grp = lax.axis_index("grp")
    tp = lax.axis_index("tp")
    z_lo_count = lax.axis_size("grp") // 8
    ring_z = 2 * z_lo_count
    side = tp % 2
    z = side * z_lo_count + grp // 8

    def device(step):
        at = lax.rem(z + step + ring_z, ring_z)
        return (lax.rem(at, z_lo_count) * 8 + grp % 8, (tp // 2) * 2 + at // z_lo_count)

    up, down = device(2), device(-2)
    up_side, down_side = up[1] % 2, down[1] % 2
    barrier = pltpu.get_barrier_semaphore()
    for peer in (up, down):
        pl.semaphore_signal(barrier, inc=1, device_id=peer, device_id_type=MESH)
    pl.semaphore_wait(barrier, 2)
    legs = []
    for index in range(count):
        source = ins[index] if modes[index] else ins[index].at[1 - side]
        half = source.shape[0] // 2
        for slot, peer in ((0, up), (1, down)):
            copy = pltpu.make_async_remote_copy(
                src_ref=source.at[pl.ds(slot * half, half)],
                dst_ref=stage[index].at[slot],
                send_sem=leg_send.at[index, slot],
                recv_sem=leg_recv.at[index, slot],
                device_id=peer,
                device_id_type=MESH,
            )
            copy.start()
            legs.append((index, slot, half, copy))
        if modes[index]:
            outs[index][side] = ins[index][...]
        else:
            outs[index][side] = ins[index][side]
    hops = []
    for index, slot, half, copy in legs:
        copy.wait_recv()
        peer, target = (up, down_side) if slot == 0 else (down, up_side)
        hop = pltpu.make_async_remote_copy(
            src_ref=stage[index].at[slot],
            dst_ref=outs[index].at[target, pl.ds(slot * half, half)],
            send_sem=hop_send.at[index, slot],
            recv_sem=hop_recv.at[index, slot],
            device_id=peer,
            device_id_type=MESH,
        )
        hop.start()
        hops.append(hop)
    for _, _, _, copy in legs:
        copy.wait_send()
    for hop in hops:
        hop.wait()


def pair_exchange(arrays, modes, collective_id):
    shapes, stages = [], []
    for array, gather in zip(arrays, modes):
        block = tuple(array.shape if gather else array.shape[1:])
        shapes.append(jax.ShapeDtypeStruct((2,) + block, array.dtype))
        stages.append(pltpu.VMEM((2, block[0] // 2) + block[1:], array.dtype))
    vmem = pl.BlockSpec(memory_space=pltpu.VMEM)
    count = len(arrays)
    return pl.pallas_call(
        functools.partial(relay_kernel, tuple(modes)),
        out_shape=tuple(shapes),
        in_specs=[vmem] * count,
        out_specs=tuple([vmem] * count),
        scratch_shapes=stages + [pltpu.SemaphoreType.DMA((count, 2))] * 4,
        compiler_params=pltpu.CompilerParams(
            collective_id=collective_id, has_side_effects=True, vmem_limit_bytes=48 * 1024 * 1024
        ),
    )(*arrays)


def attention_kernel(lo_ref, hi_ref, q_ref, cache_ref, mix_ref, peak_ref, total_ref, m_sc, l_sc, acc_sc):
    block = pl.program_id(0)
    kv_head = pl.program_id(1)
    lo = lo_ref[block]
    hi = hi_ref[block]
    heads, tokens, width = q_ref.shape
    query = q_ref[...].reshape(heads * tokens, width)
    m_sc[...] = jnp.full_like(m_sc, NEG)
    l_sc[...] = jnp.zeros_like(l_sc)
    acc_sc[...] = jnp.zeros_like(acc_sc)
    key_col = pl.multiple_of(kv_head * HD, HD)
    value_col = pl.multiple_of((KVH + kv_head) * HD, HD)
    first = lo // CHUNK
    last = jnp.where(hi > lo, (hi + CHUNK - 1) // CHUNK, first)

    def body(chunk, carry):
        start = pl.multiple_of(chunk * CHUNK, CHUNK)
        keys = cache_ref[pl.ds(start, CHUNK), pl.ds(key_col, HD)]
        values = cache_ref[pl.ds(start, CHUNK), pl.ds(value_col, HD)]
        rows = start + lax.broadcasted_iota(jnp.int32, (1, CHUNK), 1)
        bias = jnp.where((rows >= lo) & (rows < hi), 0.0, -jnp.inf)
        scores = lax.dot_general(
            query, keys, (((1,), (1,)), ((), ())), preferred_element_type=jnp.float32
        ) * (HD ** (-0.5)) + bias
        old_peak = m_sc[...]
        new_peak = jnp.maximum(old_peak, jnp.max(scores, axis=1, keepdims=True))
        scale = jnp.exp(old_peak - new_peak)
        weights = jnp.exp(scores - new_peak)
        l_sc[...] = scale * l_sc[...] + jnp.sum(weights, axis=1, keepdims=True)
        acc_sc[...] = scale * acc_sc[...] + jnp.dot(
            weights.astype(jnp.bfloat16), values, preferred_element_type=jnp.float32
        )
        m_sc[...] = new_peak
        return carry

    lax.fori_loop(first, last, body, 0)
    mix_ref[...] = acc_sc[...].reshape(heads, tokens, width)
    peak_ref[...] = m_sc[...].reshape(heads, tokens, 1)
    total_ref[...] = l_sc[...].reshape(heads, tokens, 1)


def cache_attention(queries, cache_rows, lo, hi):
    heads, tokens, width = queries.shape
    blocks = tokens // C
    group_size = heads // KVH
    return pl.pallas_call(
        attention_kernel,
        out_shape=(
            jax.ShapeDtypeStruct((heads, tokens, width), jnp.float32),
            jax.ShapeDtypeStruct((heads, tokens, 1), jnp.float32),
            jax.ShapeDtypeStruct((heads, tokens, 1), jnp.float32),
        ),
        grid_spec=pltpu.PrefetchScalarGridSpec(
            num_scalar_prefetch=2,
            grid=(blocks, KVH),
            in_specs=[
                pl.BlockSpec((group_size, C, width), lambda b, j, lo, hi: (j, b, 0)),
                pl.BlockSpec(cache_rows.shape, lambda b, j, lo, hi: (0, 0)),
            ],
            out_specs=[
                pl.BlockSpec((group_size, C, width), lambda b, j, lo, hi: (j, b, 0)),
                pl.BlockSpec((group_size, C, 1), lambda b, j, lo, hi: (j, b, 0)),
                pl.BlockSpec((group_size, C, 1), lambda b, j, lo, hi: (j, b, 0)),
            ],
            scratch_shapes=[
                pltpu.VMEM((group_size * C, 1), jnp.float32),
                pltpu.VMEM((group_size * C, 1), jnp.float32),
                pltpu.VMEM((group_size * C, width), jnp.float32),
            ],
        ),
        compiler_params=pltpu.CompilerParams(vmem_limit_bytes=48 * 1024 * 1024),
    )(lo, hi, queries, cache_rows)


def join_partials(first, second):
    first_mix, first_peak, first_total = first
    second_mix, second_peak, second_total = second
    new_peak = jnp.maximum(first_peak, second_peak)
    first_scale = jnp.exp(first_peak - new_peak)
    second_scale = jnp.exp(second_peak - new_peak)
    joined_mix = first_mix * first_scale[..., None] + second_mix * second_scale[..., None]
    return (joined_mix, new_peak, first_total * first_scale + second_total * second_scale)


def to_partner(tree, flip_mask, groups):
    def branch(mask):
        pairs = [(i, i ^ mask) for i in range(groups)]
        return lambda t: jax.tree.map(lambda a: lax.ppermute(a, "grp", pairs), t)

    return lax.switch(flip_mask - 1, [branch(mask) for mask in range(1, groups)], tree)


def on_device(hidden, norm_gain, w_query, w_keyval, w_out, kv_cache, cache_len, partner):
    group_index = lax.axis_index("grp")
    tp_index = lax.axis_index("tp")
    tp_count = lax.axis_size("tp")
    groups = lax.axis_size("grp")
    ring = tp_count // 2
    ring_at = tp_index // 2
    side = tp_index % 2
    local_heads = QH // tp_count
    rows_here = kv_cache.shape[0]
    token_count = hidden.shape[0]
    model_width = w_out.shape[1]
    out_width = model_width // tp_count
    flip_mask = partner[0]

    def w_block(member):
        return lax.dynamic_slice_in_dim(w_out, member * 2 * out_width, 2 * out_width, 1)

    w_received = [w_block(ring_at)]
    for step in range(1, ring):
        send = w_block(lax.rem(ring_at + step, ring))
        pairs = [(i, (i + 2 * step) % tp_count) for i in range(tp_count)]
        w_received.append(lax.ppermute(send, "tp", pairs))

    float_rows = hidden.astype(jnp.float32)
    normed = (
        float_rows
        * lax.rsqrt(jnp.mean(float_rows * float_rows, -1, keepdims=True) + EPS)
        * norm_gain
    ).astype(jnp.bfloat16)
    query_raw = jnp.dot(normed, w_query, preferred_element_type=jnp.float32).reshape(
        token_count, local_heads, HD
    )
    keyval_part = jnp.dot(normed, w_keyval, preferred_element_type=jnp.float32).astype(jnp.bfloat16)
    lengths = lax.dynamic_slice_in_dim(cache_len, group_index * R, R)
    positions = (lengths[:, None] + jnp.arange(C, dtype=jnp.int32)[None, :]).reshape(token_count)
    query_local = rotate_pairs(query_raw, positions).astype(jnp.bfloat16).transpose(1, 0, 2)
    far_query = to_partner(query_local[:, :C], flip_mask, groups)
    query_ext = jnp.concatenate([query_local, far_query], 1)
    ext_tokens = query_ext.shape[1]
    query_pair, keyval_pair = pair_exchange([query_ext, keyval_part], [True, True], 0)
    query_got, keyval_got = tp_exchange([query_pair, keyval_pair], [True, True], 1, ring, 2)
    queries = query_got.reshape(QH, ext_tokens, HD)
    keyval_all = keyval_got.reshape(tp_count, token_count, -1).transpose(1, 0, 2).reshape(
        token_count, -1
    )

    stored_first = lengths[0] - lengths[0] // 2
    bound_one = stored_first
    bound_two = stored_first + lengths[1]
    far_count = cache_len[partner[group_index] * R] // 2
    starts = jnp.stack([0, bound_one, bound_two]).astype(jnp.int32)
    ends = jnp.stack([bound_one, bound_two, bound_two + far_count]).astype(jnp.int32)
    offset = tp_index * rows_here
    lo = jnp.clip(starts - offset, 0, rows_here)
    hi = jnp.clip(ends - offset, 0, rows_here)
    mix, peak, total = cache_attention(queries, kv_cache, lo, hi)
    mix_got, peak_got, total_got = tp_exchange(
        [
            mix.astype(jnp.bfloat16).reshape(tp_count, local_heads, ext_tokens, HD),
            peak.reshape(tp_count, local_heads, ext_tokens),
            total.reshape(tp_count, local_heads, ext_tokens),
        ],
        [False, False, False],
        2,
    )
    top = jnp.max(peak_got, 0)
    scales = jnp.exp(peak_got - top[None])
    mix_c = jnp.sum(mix_got.astype(jnp.float32) * scales[..., None], 0)
    total_c = jnp.sum(total_got * scales, 0)
    far_pack = jnp.concatenate(
        [
            mix_c[:, token_count:],
            top[:, None, token_count:],
            total_c[:, None, token_count:],
        ],
        1,
    )
    far_pack = to_partner(far_pack, flip_mask, groups)
    far_back = (far_pack[:, :C], far_pack[:, C], far_pack[:, C + 1])
    combined = (mix_c[:, :token_count], top[:, :token_count], total_c[:, :token_count])
    front = join_partials(tuple(piece[:, :C] for piece in combined), far_back)
    own = tuple(jnp.concatenate([front[i], combined[i][:, C:]], 1) for i in range(3))

    new_keys = rotate_pairs(
        keyval_all[:, : KVH * HD].astype(jnp.float32).reshape(token_count, KVH, HD), positions
    ).astype(jnp.bfloat16)
    new_values = keyval_all[:, KVH * HD :].reshape(token_count, KVH, HD)
    kv_head = (tp_index * local_heads) // (QH // KVH)
    key_rows = lax.dynamic_index_in_dim(new_keys, kv_head, 1, keepdims=False)
    value_rows = lax.dynamic_index_in_dim(new_values, kv_head, 1, keepdims=False)
    token_index = jnp.arange(token_count, dtype=jnp.int32)
    request_of = token_index // C
    within = token_index % C
    self_visible = (request_of[:, None] == request_of[None, :]) & (
        within[None, :] <= within[:, None]
    )
    self_scores = jnp.einsum(
        "htd,sd->hts", query_local, key_rows, preferred_element_type=jnp.float32
    ) * HD ** (-0.5)
    self_scores = jnp.where(self_visible[None], self_scores, -jnp.inf)
    self_peak = jnp.max(self_scores, -1)
    self_weights = jnp.exp(self_scores - self_peak[..., None])
    self_total = jnp.sum(self_weights, -1)
    self_mix = jnp.einsum(
        "hts,sd->htd", self_weights.astype(jnp.bfloat16), value_rows,
        preferred_element_type=jnp.float32,
    )
    final_mix, final_peak, final_total = join_partials(own, (self_mix, self_peak, self_total))
    attention = (final_mix / final_total[..., None]).astype(jnp.bfloat16)
    attention = attention.transpose(1, 0, 2).reshape(token_count, local_heads * HD)
    (attention_ring,) = tp_exchange([attention], [True], 3, ring, 2)
    sums = None
    for step in range(ring):
        source = lax.rem(ring_at - step + ring, ring)
        piece = jnp.dot(
            lax.dynamic_index_in_dim(attention_ring, source, 0, False),
            w_received[step],
            preferred_element_type=jnp.float32,
        )
        sums = piece if sums is None else sums + piece
    halves = sums.reshape(token_count, 2, out_width).transpose(1, 0, 2)
    (halves_got,) = pair_exchange([halves.astype(jnp.bfloat16)], [False], 4)
    mine = lax.dynamic_index_in_dim(halves, side, 0, False)
    other = lax.dynamic_index_in_dim(halves_got, 1 - side, 0, False)
    return (mine + other.astype(jnp.float32)).astype(jnp.bfloat16)


def solution(mesh):
    placed = (
        P("grp", None),
        P(),
        P(None, "tp"),
        P(None, "tp"),
        P("tp", None),
        P(("grp", "tp"), None),
        P(),
        P(),
    )
    return jax.shard_map(
        on_device, mesh=mesh, in_specs=placed, out_specs=P("grp", "tp"), check_vma=False
    )
```

```python
import functools

import jax
import jax.numpy as jnp
from jax import lax
from jax.experimental import pallas as pl
from jax.experimental.pallas import tpu as pltpu
from jax.sharding import PartitionSpec as P

HD = 128
QH = 16
KVH = 2
C = 128
R = 2

THETA = 5000000.0
EPS = 1e-05
NEG = -1e30
CHUNK = 256
MESH = pl.DeviceIdType.MESH


def rotate_pairs(values, positions):
    width = values.shape[-1]
    half_width = width // 2
    frequency = THETA ** (-2.0 * jnp.arange(half_width, dtype=jnp.float32) / width)
    angles = positions.astype(jnp.float32)[:, None] * frequency[None, :]
    cosine_part = jnp.cos(angles)[:, None, :]
    sine_part = jnp.sin(angles)[:, None, :]
    first_half = values[..., :half_width]
    second_half = values[..., half_width:]
    return jnp.concatenate(
        [
            first_half * cosine_part - second_half * sine_part,
            second_half * cosine_part + first_half * sine_part,
        ],
        -1,
    )


def exchange_kernel(count, stride, modes, *refs):
    arrays = len(modes)
    ins, outs = refs[:arrays], refs[arrays : 2 * arrays]
    send_sem, recv_sem = refs[2 * arrays :]
    me = lax.axis_index("tp")
    grp = lax.axis_index("grp")
    mine = lax.rem(me // stride, count)
    base = me - mine * stride

    def member(step):
        return lax.rem(mine + step, count)

    barrier = pltpu.get_barrier_semaphore()
    for step in range(1, count):
        pl.semaphore_signal(
            barrier, inc=1, device_id=(grp, base + member(step) * stride), device_id_type=MESH
        )
    pl.semaphore_wait(barrier, count - 1)
    copies = []
    for index in range(arrays):
        for step in range(1, count):
            peer = member(step)
            source = ins[index] if modes[index] else ins[index].at[peer]
            copy = pltpu.make_async_remote_copy(
                src_ref=source,
                dst_ref=outs[index].at[mine],
                send_sem=send_sem.at[index, step],
                recv_sem=recv_sem.at[index, step],
                device_id=(grp, base + peer * stride),
                device_id_type=MESH,
            )
            copy.start()
            copies.append(copy)
        if modes[index]:
            outs[index][mine] = ins[index][...]
        else:
            outs[index][mine] = ins[index][mine]
    for copy in copies:
        copy.wait()


def tp_exchange(arrays, modes, collective_id, count=None, stride=1):
    count = lax.axis_size("tp") if count is None else count
    shapes = []
    for array, gather in zip(arrays, modes):
        block = array.shape if gather else array.shape[1:]
        shapes.append(jax.ShapeDtypeStruct((count,) + tuple(block), array.dtype))
    vmem = pl.BlockSpec(memory_space=pltpu.VMEM)
    return pl.pallas_call(
        functools.partial(exchange_kernel, count, stride, tuple(modes)),
        out_shape=tuple(shapes),
        in_specs=[vmem] * len(arrays),
        out_specs=tuple([vmem] * len(arrays)),
        scratch_shapes=[
            pltpu.SemaphoreType.DMA((len(arrays), count)),
            pltpu.SemaphoreType.DMA((len(arrays), count)),
        ],
        compiler_params=pltpu.CompilerParams(
            collective_id=collective_id, has_side_effects=True, vmem_limit_bytes=48 * 1024 * 1024
        ),
    )(*arrays)


def attention_kernel(lo_ref, hi_ref, q_ref, cache_ref, mix_ref, peak_ref, total_ref):
    block = pl.program_id(0)
    kv_head = pl.program_id(1)
    lo = lo_ref[block]
    hi = hi_ref[block]
    heads, tokens, width = q_ref.shape
    key_col = pl.multiple_of(kv_head * HD, HD)
    value_col = pl.multiple_of((KVH + kv_head) * HD, HD)
    first = lo // CHUNK
    last = jnp.where(hi > lo, (hi + CHUNK - 1) // CHUNK, first)

    def one_head(head, carry):
        query = q_ref[head]

        def body(chunk, state):
            peak, total, mix = state
            start = pl.multiple_of(chunk * CHUNK, CHUNK)
            keys = cache_ref[pl.ds(start, CHUNK), pl.ds(key_col, HD)]
            values = cache_ref[pl.ds(start, CHUNK), pl.ds(value_col, HD)]
            rows = start + lax.broadcasted_iota(jnp.int32, (1, CHUNK), 1)
            bias = jnp.where((rows >= lo) & (rows < hi), 0.0, -jnp.inf)
            scores = lax.dot_general(
                query, keys, (((1,), (1,)), ((), ())), preferred_element_type=jnp.float32
            ) * (HD ** (-0.5)) + bias
            new_peak = jnp.maximum(peak, jnp.max(scores, axis=1, keepdims=True))
            scale = jnp.exp(peak - new_peak)
            weights = jnp.exp(scores - new_peak)
            total = scale * total + jnp.sum(weights, axis=1, keepdims=True)
            mix = scale * mix + jnp.dot(
                weights.astype(jnp.bfloat16), values, preferred_element_type=jnp.float32
            )
            return new_peak, total, mix

        start_state = (
            jnp.full((tokens, 1), NEG, jnp.float32),
            jnp.zeros((tokens, 1), jnp.float32),
            jnp.zeros((tokens, width), jnp.float32),
        )
        peak, total, mix = lax.fori_loop(first, last, body, start_state)
        mix_ref[head] = mix
        peak_ref[head] = peak
        total_ref[head] = total
        return carry

    lax.fori_loop(0, heads, one_head, 0)


def cache_attention(queries, cache_rows, lo, hi):
    heads, tokens, width = queries.shape
    blocks = tokens // C
    group_size = heads // KVH
    return pl.pallas_call(
        attention_kernel,
        out_shape=(
            jax.ShapeDtypeStruct((heads, tokens, width), jnp.float32),
            jax.ShapeDtypeStruct((heads, tokens, 1), jnp.float32),
            jax.ShapeDtypeStruct((heads, tokens, 1), jnp.float32),
        ),
        grid_spec=pltpu.PrefetchScalarGridSpec(
            num_scalar_prefetch=2,
            grid=(blocks, KVH),
            in_specs=[
                pl.BlockSpec((group_size, C, width), lambda b, j, lo, hi: (j, b, 0)),
                pl.BlockSpec(cache_rows.shape, lambda b, j, lo, hi: (0, 0)),
            ],
            out_specs=[
                pl.BlockSpec((group_size, C, width), lambda b, j, lo, hi: (j, b, 0)),
                pl.BlockSpec((group_size, C, 1), lambda b, j, lo, hi: (j, b, 0)),
                pl.BlockSpec((group_size, C, 1), lambda b, j, lo, hi: (j, b, 0)),
            ],
        ),
        compiler_params=pltpu.CompilerParams(vmem_limit_bytes=48 * 1024 * 1024),
    )(lo, hi, queries, cache_rows)


def join_partials(first, second):
    first_mix, first_peak, first_total = first
    second_mix, second_peak, second_total = second
    new_peak = jnp.maximum(first_peak, second_peak)
    first_scale = jnp.exp(first_peak - new_peak)
    second_scale = jnp.exp(second_peak - new_peak)
    joined_mix = first_mix * first_scale[..., None] + second_mix * second_scale[..., None]
    return (joined_mix, new_peak, first_total * first_scale + second_total * second_scale)


def to_partner(tree, flip_mask, groups):
    def branch(mask):
        pairs = [(i, i ^ mask) for i in range(groups)]
        return lambda t: jax.tree.map(lambda a: lax.ppermute(a, "grp", pairs), t)

    return lax.switch(flip_mask - 1, [branch(mask) for mask in range(1, groups)], tree)


def on_device(hidden, norm_gain, w_query, w_keyval, w_out, kv_cache, cache_len, partner):
    group_index = lax.axis_index("grp")
    tp_index = lax.axis_index("tp")
    tp_count = lax.axis_size("tp")
    groups = lax.axis_size("grp")
    ring = tp_count // 2
    ring_at = tp_index // 2
    side = tp_index % 2
    local_heads = QH // tp_count
    rows_here = kv_cache.shape[0]
    token_count = hidden.shape[0]
    model_width = w_out.shape[1]
    out_width = model_width // tp_count
    flip_mask = partner[0]

    def w_block(member):
        return lax.dynamic_slice_in_dim(w_out, member * 2 * out_width, 2 * out_width, 1)

    w_received = [w_block(ring_at)]
    for step in range(1, ring):
        send = w_block(lax.rem(ring_at + step, ring))
        pairs = [(i, (i + 2 * step) % tp_count) for i in range(tp_count)]
        w_received.append(lax.ppermute(send, "tp", pairs))

    float_rows = hidden.astype(jnp.float32)
    normed = (
        float_rows
        * lax.rsqrt(jnp.mean(float_rows * float_rows, -1, keepdims=True) + EPS)
        * norm_gain
    ).astype(jnp.bfloat16)
    query_raw = jnp.dot(normed, w_query, preferred_element_type=jnp.float32).reshape(
        token_count, local_heads, HD
    )
    keyval_part = jnp.dot(normed, w_keyval, preferred_element_type=jnp.float32).astype(jnp.bfloat16)
    lengths = lax.dynamic_slice_in_dim(cache_len, group_index * R, R)
    positions = (lengths[:, None] + jnp.arange(C, dtype=jnp.int32)[None, :]).reshape(token_count)
    query_local = rotate_pairs(query_raw, positions).astype(jnp.bfloat16).transpose(1, 0, 2)
    far_query = to_partner(query_local[:, :C], flip_mask, groups)
    query_ext = jnp.concatenate([query_local, far_query], 1)
    ext_tokens = query_ext.shape[1]
    query_pair, keyval_pair = tp_exchange([query_ext, keyval_part], [True, True], 0, 2, 1)
    query_got, keyval_got = tp_exchange([query_pair, keyval_pair], [True, True], 1, ring, 2)
    queries = query_got.reshape(QH, ext_tokens, HD)
    keyval_all = keyval_got.reshape(tp_count, token_count, -1).transpose(1, 0, 2).reshape(
        token_count, -1
    )

    stored_first = lengths[0] - lengths[0] // 2
    bound_one = stored_first
    bound_two = stored_first + lengths[1]
    far_count = cache_len[partner[group_index] * R] // 2
    starts = jnp.stack([0, bound_one, bound_two]).astype(jnp.int32)
    ends = jnp.stack([bound_one, bound_two, bound_two + far_count]).astype(jnp.int32)
    offset = tp_index * rows_here
    lo = jnp.clip(starts - offset, 0, rows_here)
    hi = jnp.clip(ends - offset, 0, rows_here)
    mix, peak, total = cache_attention(queries, kv_cache, lo, hi)
    mix_got, peak_got, total_got = tp_exchange(
        [
            mix.astype(jnp.bfloat16).reshape(tp_count, local_heads, ext_tokens, HD),
            peak.reshape(tp_count, local_heads, ext_tokens),
            total.reshape(tp_count, local_heads, ext_tokens),
        ],
        [False, False, False],
        2,
    )
    top = jnp.max(peak_got, 0)
    scales = jnp.exp(peak_got - top[None])
    mix_c = jnp.sum(mix_got.astype(jnp.float32) * scales[..., None], 0)
    total_c = jnp.sum(total_got * scales, 0)
    far_pack = jnp.concatenate(
        [
            mix_c[:, token_count:],
            top[:, None, token_count:],
            total_c[:, None, token_count:],
        ],
        1,
    )
    far_pack = to_partner(far_pack, flip_mask, groups)
    far_back = (far_pack[:, :C], far_pack[:, C], far_pack[:, C + 1])
    combined = (mix_c[:, :token_count], top[:, :token_count], total_c[:, :token_count])
    front = join_partials(tuple(piece[:, :C] for piece in combined), far_back)
    own = tuple(jnp.concatenate([front[i], combined[i][:, C:]], 1) for i in range(3))

    new_keys = rotate_pairs(
        keyval_all[:, : KVH * HD].astype(jnp.float32).reshape(token_count, KVH, HD), positions
    ).astype(jnp.bfloat16)
    new_values = keyval_all[:, KVH * HD :].reshape(token_count, KVH, HD)
    kv_head = (tp_index * local_heads) // (QH // KVH)
    key_rows = lax.dynamic_index_in_dim(new_keys, kv_head, 1, keepdims=False)
    value_rows = lax.dynamic_index_in_dim(new_values, kv_head, 1, keepdims=False)
    token_index = jnp.arange(token_count, dtype=jnp.int32)
    request_of = token_index // C
    within = token_index % C
    self_visible = (request_of[:, None] == request_of[None, :]) & (
        within[None, :] <= within[:, None]
    )
    self_scores = jnp.einsum(
        "htd,sd->hts", query_local, key_rows, preferred_element_type=jnp.float32
    ) * HD ** (-0.5)
    self_scores = jnp.where(self_visible[None], self_scores, -jnp.inf)
    self_peak = jnp.max(self_scores, -1)
    self_weights = jnp.exp(self_scores - self_peak[..., None])
    self_total = jnp.sum(self_weights, -1)
    self_mix = jnp.einsum(
        "hts,sd->htd", self_weights.astype(jnp.bfloat16), value_rows,
        preferred_element_type=jnp.float32,
    )
    final_mix, final_peak, final_total = join_partials(own, (self_mix, self_peak, self_total))
    attention = (final_mix / final_total[..., None]).astype(jnp.bfloat16)
    attention = attention.transpose(1, 0, 2).reshape(token_count, local_heads * HD)
    (attention_ring,) = tp_exchange([attention], [True], 3, ring, 2)
    sums = None
    for step in range(ring):
        source = lax.rem(ring_at - step + ring, ring)
        piece = jnp.dot(
            lax.dynamic_index_in_dim(attention_ring, source, 0, False),
            w_received[step],
            preferred_element_type=jnp.float32,
        )
        sums = piece if sums is None else sums + piece
    halves = sums.reshape(token_count, 2, out_width).transpose(1, 0, 2)
    (halves_got,) = tp_exchange([halves.astype(jnp.bfloat16)], [False], 4, 2, 1)
    mine = lax.dynamic_index_in_dim(halves, side, 0, False)
    other = lax.dynamic_index_in_dim(halves_got, 1 - side, 0, False)
    return (mine + other.astype(jnp.float32)).astype(jnp.bfloat16)


def solution(mesh):
    placed = (
        P("grp", None),
        P(),
        P(None, "tp"),
        P(None, "tp"),
        P("tp", None),
        P(("grp", "tp"), None),
        P(),
        P(),
    )
    return jax.shard_map(
        on_device, mesh=mesh, in_specs=placed, out_specs=P("grp", "tp"), check_vma=False
    )
```

```python
import functools

import jax
import jax.numpy as jnp
from jax import lax
from jax.experimental import pallas as pl
from jax.experimental.pallas import tpu as pltpu
from jax.sharding import PartitionSpec as P

HD = 128
QH = 16
KVH = 2
C = 128
R = 2

THETA = 5000000.0
EPS = 1e-05
NEG = -1e30
CHUNK = 256
MESH = pl.DeviceIdType.MESH


def rotate_pairs(values, positions):
    width = values.shape[-1]
    half_width = width // 2
    frequency = THETA ** (-2.0 * jnp.arange(half_width, dtype=jnp.float32) / width)
    angles = positions.astype(jnp.float32)[:, None] * frequency[None, :]
    cosine_part = jnp.cos(angles)[:, None, :]
    sine_part = jnp.sin(angles)[:, None, :]
    first_half = values[..., :half_width]
    second_half = values[..., half_width:]
    return jnp.concatenate(
        [
            first_half * cosine_part - second_half * sine_part,
            second_half * cosine_part + first_half * sine_part,
        ],
        -1,
    )


def exchange_kernel(count, stride, modes, *refs):
    arrays = len(modes)
    ins, outs = refs[:arrays], refs[arrays : 2 * arrays]
    send_sem, recv_sem = refs[2 * arrays :]
    me = lax.axis_index("tp")
    grp = lax.axis_index("grp")
    mine = lax.rem(me // stride, count)
    base = me - mine * stride

    def member(step):
        return lax.rem(mine + step, count)

    barrier = pltpu.get_barrier_semaphore()
    for step in range(1, count):
        pl.semaphore_signal(
            barrier, inc=1, device_id=(grp, base + member(step) * stride), device_id_type=MESH
        )
    pl.semaphore_wait(barrier, count - 1)
    copies = []
    for index in range(arrays):
        for step in range(1, count):
            peer = member(step)
            source = ins[index] if modes[index] else ins[index].at[peer]
            copy = pltpu.make_async_remote_copy(
                src_ref=source,
                dst_ref=outs[index].at[mine],
                send_sem=send_sem.at[index, step],
                recv_sem=recv_sem.at[index, step],
                device_id=(grp, base + peer * stride),
                device_id_type=MESH,
            )
            copy.start()
            copies.append(copy)
        if modes[index]:
            outs[index][mine] = ins[index][...]
        else:
            outs[index][mine] = ins[index][mine]
    for copy in copies:
        copy.wait()


def tp_exchange(arrays, modes, collective_id, count=None, stride=1):
    count = lax.axis_size("tp") if count is None else count
    shapes = []
    for array, gather in zip(arrays, modes):
        block = array.shape if gather else array.shape[1:]
        shapes.append(jax.ShapeDtypeStruct((count,) + tuple(block), array.dtype))
    vmem = pl.BlockSpec(memory_space=pltpu.VMEM)
    return pl.pallas_call(
        functools.partial(exchange_kernel, count, stride, tuple(modes)),
        out_shape=tuple(shapes),
        in_specs=[vmem] * len(arrays),
        out_specs=tuple([vmem] * len(arrays)),
        scratch_shapes=[
            pltpu.SemaphoreType.DMA((len(arrays), count)),
            pltpu.SemaphoreType.DMA((len(arrays), count)),
        ],
        compiler_params=pltpu.CompilerParams(
            collective_id=collective_id, has_side_effects=True, vmem_limit_bytes=48 * 1024 * 1024
        ),
    )(*arrays)


def attention_kernel(lo_ref, hi_ref, q_ref, cache_ref, mix_ref, peak_ref, total_ref):
    block = pl.program_id(0)
    kv_head = pl.program_id(1)
    lo = lo_ref[block]
    hi = hi_ref[block]
    heads, tokens, width = q_ref.shape
    key_col = pl.multiple_of(kv_head * HD, HD)
    value_col = pl.multiple_of((KVH + kv_head) * HD, HD)
    first = lo // CHUNK
    last = jnp.where(hi > lo, (hi + CHUNK - 1) // CHUNK, first)

    def one_head(head, carry):
        query = q_ref[head]

        def body(chunk, state):
            peak, total, mix = state
            start = pl.multiple_of(chunk * CHUNK, CHUNK)
            keys = cache_ref[pl.ds(start, CHUNK), pl.ds(key_col, HD)]
            values = cache_ref[pl.ds(start, CHUNK), pl.ds(value_col, HD)]
            rows = start + lax.broadcasted_iota(jnp.int32, (1, CHUNK), 1)
            bias = jnp.where((rows >= lo) & (rows < hi), 0.0, -jnp.inf)
            scores = lax.dot_general(
                query, keys, (((1,), (1,)), ((), ())), preferred_element_type=jnp.float32
            ) * (HD ** (-0.5)) + bias
            new_peak = jnp.maximum(peak, jnp.max(scores, axis=1, keepdims=True))
            scale = jnp.exp(peak - new_peak)
            weights = jnp.exp(scores - new_peak)
            total = scale * total + jnp.sum(weights, axis=1, keepdims=True)
            mix = scale * mix + jnp.dot(
                weights.astype(jnp.bfloat16), values, preferred_element_type=jnp.float32
            )
            return new_peak, total, mix

        start_state = (
            jnp.full((tokens, 1), NEG, jnp.float32),
            jnp.zeros((tokens, 1), jnp.float32),
            jnp.zeros((tokens, width), jnp.float32),
        )
        peak, total, mix = lax.fori_loop(first, last, body, start_state)
        mix_ref[head] = mix
        peak_ref[head] = peak
        total_ref[head] = total
        return carry

    lax.fori_loop(0, heads, one_head, 0)


def cache_attention(queries, cache_rows, lo, hi):
    heads, tokens, width = queries.shape
    blocks = tokens // C
    group_size = heads // KVH
    return pl.pallas_call(
        attention_kernel,
        out_shape=(
            jax.ShapeDtypeStruct((heads, tokens, width), jnp.float32),
            jax.ShapeDtypeStruct((heads, tokens, 1), jnp.float32),
            jax.ShapeDtypeStruct((heads, tokens, 1), jnp.float32),
        ),
        grid_spec=pltpu.PrefetchScalarGridSpec(
            num_scalar_prefetch=2,
            grid=(blocks, KVH),
            in_specs=[
                pl.BlockSpec((group_size, C, width), lambda b, j, lo, hi: (j, b, 0)),
                pl.BlockSpec(cache_rows.shape, lambda b, j, lo, hi: (0, 0)),
            ],
            out_specs=[
                pl.BlockSpec((group_size, C, width), lambda b, j, lo, hi: (j, b, 0)),
                pl.BlockSpec((group_size, C, 1), lambda b, j, lo, hi: (j, b, 0)),
                pl.BlockSpec((group_size, C, 1), lambda b, j, lo, hi: (j, b, 0)),
            ],
        ),
        compiler_params=pltpu.CompilerParams(vmem_limit_bytes=48 * 1024 * 1024),
    )(lo, hi, queries, cache_rows)


def combine_many(mix, peak, total):
    top = jnp.max(peak, 0)
    scales = jnp.exp(peak - top[None])
    joined = jnp.sum(mix.astype(jnp.float32) * scales[..., None], 0)
    return joined, top, jnp.sum(total * scales, 0)


def join_partials(first, second):
    first_mix, first_peak, first_total = first
    second_mix, second_peak, second_total = second
    new_peak = jnp.maximum(first_peak, second_peak)
    first_scale = jnp.exp(first_peak - new_peak)
    second_scale = jnp.exp(second_peak - new_peak)
    joined_mix = first_mix * first_scale[..., None] + second_mix * second_scale[..., None]
    return (joined_mix, new_peak, first_total * first_scale + second_total * second_scale)


def to_partner(tree, flip_mask, groups):
    def branch(mask):
        pairs = [(i, i ^ mask) for i in range(groups)]
        return lambda t: jax.tree.map(lambda a: lax.ppermute(a, "grp", pairs), t)

    return lax.switch(flip_mask - 1, [branch(mask) for mask in range(1, groups)], tree)


def on_device(hidden, norm_gain, w_query, w_keyval, w_out, kv_cache, cache_len, partner):
    group_index = lax.axis_index("grp")
    tp_index = lax.axis_index("tp")
    tp_count = lax.axis_size("tp")
    groups = lax.axis_size("grp")
    ring = tp_count // 2
    ring_at = tp_index // 2
    side = tp_index % 2
    local_heads = QH // tp_count
    rows_here = kv_cache.shape[0]
    token_count = hidden.shape[0]
    model_width = w_out.shape[1]
    out_width = model_width // tp_count
    flip_mask = partner[0]

    def w_block(member):
        first = lax.dynamic_slice_in_dim(w_out, (2 * member + side) * out_width, out_width, 1)
        second = lax.dynamic_slice_in_dim(w_out, (2 * member + 1 - side) * out_width, out_width, 1)
        return jnp.concatenate([first, second], 1)

    w_received = [w_block(ring_at)]
    for step in range(1, ring):
        send = w_block(lax.rem(ring_at + step, ring))
        pairs = [(i, (i + 2 * step) % tp_count) for i in range(tp_count)]
        w_received.append(lax.ppermute(send, "tp", pairs))

    float_rows = hidden.astype(jnp.float32)
    normed = (
        float_rows
        * lax.rsqrt(jnp.mean(float_rows * float_rows, -1, keepdims=True) + EPS)
        * norm_gain
    ).astype(jnp.bfloat16)
    query_raw = jnp.dot(normed, w_query, preferred_element_type=jnp.float32).reshape(
        token_count, local_heads, HD
    )
    keyval_part = jnp.dot(normed, w_keyval, preferred_element_type=jnp.float32).astype(jnp.bfloat16)
    lengths = lax.dynamic_slice_in_dim(cache_len, group_index * R, R)
    positions = (lengths[:, None] + jnp.arange(C, dtype=jnp.int32)[None, :]).reshape(token_count)
    query_local = rotate_pairs(query_raw, positions).astype(jnp.bfloat16).transpose(1, 0, 2)
    far_query = to_partner(query_local[:, :C], flip_mask, groups)
    query_ext = jnp.concatenate([query_local, far_query], 1)
    ext_tokens = query_ext.shape[1]
    query_pair, keyval_pair = tp_exchange([query_ext, keyval_part], [True, True], 0, 2, 1)
    query_got, keyval_got = tp_exchange([query_pair, keyval_pair], [True, True], 1, ring, 2)
    queries = query_got.reshape(QH, ext_tokens, HD)
    keyval_all = keyval_got.reshape(tp_count, token_count, -1).transpose(1, 0, 2).reshape(
        token_count, -1
    )

    stored_first = lengths[0] - lengths[0] // 2
    bound_one = stored_first
    bound_two = stored_first + lengths[1]
    far_count = cache_len[partner[group_index] * R] // 2
    starts = jnp.stack([0, bound_one, bound_two]).astype(jnp.int32)
    ends = jnp.stack([bound_one, bound_two, bound_two + far_count]).astype(jnp.int32)
    offset = tp_index * rows_here
    lo = jnp.clip(starts - offset, 0, rows_here)
    hi = jnp.clip(ends - offset, 0, rows_here)
    mix, peak, total = cache_attention(queries, kv_cache, lo, hi)
    quad = 2 * local_heads
    ring_parts = tp_exchange(
        [
            mix.astype(jnp.bfloat16).reshape(ring, quad, ext_tokens, HD),
            peak.reshape(ring, quad, ext_tokens),
            total.reshape(ring, quad, ext_tokens),
        ],
        [False, False, False],
        2,
        ring,
        2,
    )
    ring_mix, ring_peak, ring_total = combine_many(*ring_parts)
    pair_parts = tp_exchange(
        [
            ring_mix.astype(jnp.bfloat16).reshape(2, local_heads, ext_tokens, HD),
            ring_peak.reshape(2, local_heads, ext_tokens),
            ring_total.reshape(2, local_heads, ext_tokens),
        ],
        [False, False, False],
        5,
        2,
        1,
    )
    own_part = tuple(
        lax.dynamic_index_in_dim(piece.reshape((2, local_heads) + piece.shape[1:]), side, 0, True)
        for piece in (ring_mix, ring_peak, ring_total)
    )
    far_part = tuple(
        lax.dynamic_index_in_dim(piece, 1 - side, 0, True).astype(jnp.float32) for piece in pair_parts
    )
    mix_c, top, total_c = combine_many(
        *(jnp.concatenate([a, b], 0) for a, b in zip(own_part, far_part))
    )
    far_pack = jnp.concatenate(
        [
            mix_c[:, token_count:],
            top[:, None, token_count:],
            total_c[:, None, token_count:],
        ],
        1,
    )
    far_pack = to_partner(far_pack, flip_mask, groups)
    far_back = (far_pack[:, :C], far_pack[:, C], far_pack[:, C + 1])
    combined = (mix_c[:, :token_count], top[:, :token_count], total_c[:, :token_count])
    front = join_partials(tuple(piece[:, :C] for piece in combined), far_back)
    own = tuple(jnp.concatenate([front[i], combined[i][:, C:]], 1) for i in range(3))

    new_keys = rotate_pairs(
        keyval_all[:, : KVH * HD].astype(jnp.float32).reshape(token_count, KVH, HD), positions
    ).astype(jnp.bfloat16)
    new_values = keyval_all[:, KVH * HD :].reshape(token_count, KVH, HD)
    kv_head = (tp_index * local_heads) // (QH // KVH)
    key_rows = lax.dynamic_index_in_dim(new_keys, kv_head, 1, keepdims=False)
    value_rows = lax.dynamic_index_in_dim(new_values, kv_head, 1, keepdims=False)
    token_index = jnp.arange(token_count, dtype=jnp.int32)
    request_of = token_index // C
    within = token_index % C
    self_visible = (request_of[:, None] == request_of[None, :]) & (
        within[None, :] <= within[:, None]
    )
    self_scores = jnp.einsum(
        "htd,sd->hts", query_local, key_rows, preferred_element_type=jnp.float32
    ) * HD ** (-0.5)
    self_scores = jnp.where(self_visible[None], self_scores, -jnp.inf)
    self_peak = jnp.max(self_scores, -1)
    self_weights = jnp.exp(self_scores - self_peak[..., None])
    self_total = jnp.sum(self_weights, -1)
    self_mix = jnp.einsum(
        "hts,sd->htd", self_weights.astype(jnp.bfloat16), value_rows,
        preferred_element_type=jnp.float32,
    )
    final_mix, final_peak, final_total = join_partials(own, (self_mix, self_peak, self_total))
    attention = (final_mix / final_total[..., None]).astype(jnp.bfloat16)
    attention = attention.transpose(1, 0, 2).reshape(token_count, local_heads * HD)
    (attention_ring,) = tp_exchange([attention], [True], 3, ring, 2)
    sums = None
    for step in range(ring):
        source = lax.rem(ring_at - step + ring, ring)
        piece = jnp.dot(
            lax.dynamic_index_in_dim(attention_ring, source, 0, False),
            w_received[step],
            preferred_element_type=jnp.float32,
        )
        sums = piece if sums is None else sums + piece
    (other_got,) = tp_exchange([sums[:, out_width:].astype(jnp.bfloat16)], [True], 4, 2, 1)
    other = lax.dynamic_index_in_dim(other_got, 1 - side, 0, False)
    return (sums[:, :out_width] + other.astype(jnp.float32)).astype(jnp.bfloat16)


def solution(mesh):
    placed = (
        P("grp", None),
        P(),
        P(None, "tp"),
        P(None, "tp"),
        P("tp", None),
        P(("grp", "tp"), None),
        P(),
        P(),
    )
    return jax.shard_map(
        on_device, mesh=mesh, in_specs=placed, out_specs=P("grp", "tp"), check_vma=False
    )
```

```python
import functools

import jax
import jax.numpy as jnp
from jax import lax
from jax.experimental import pallas as pl
from jax.experimental.pallas import tpu as pltpu
from jax.sharding import PartitionSpec as P

HD = 128
QH = 16
KVH = 2
C = 128
R = 2

THETA = 5000000.0
EPS = 1e-05
NEG = -1e30
CHUNK = 256
MESH = pl.DeviceIdType.MESH


def rotate_pairs(values, positions):
    width = values.shape[-1]
    half_width = width // 2
    frequency = THETA ** (-2.0 * jnp.arange(half_width, dtype=jnp.float32) / width)
    angles = positions.astype(jnp.float32)[:, None] * frequency[None, :]
    cosine_part = jnp.cos(angles)[:, None, :]
    sine_part = jnp.sin(angles)[:, None, :]
    first_half = values[..., :half_width]
    second_half = values[..., half_width:]
    return jnp.concatenate(
        [
            first_half * cosine_part - second_half * sine_part,
            second_half * cosine_part + first_half * sine_part,
        ],
        -1,
    )


def exchange_kernel(count, stride, modes, *refs):
    arrays = len(modes)
    ins, outs = refs[:arrays], refs[arrays : 2 * arrays]
    send_sem, recv_sem = refs[2 * arrays :]
    me = lax.axis_index("tp")
    grp = lax.axis_index("grp")
    mine = lax.rem(me // stride, count)
    base = me - mine * stride

    def member(step):
        return lax.rem(mine + step, count)

    barrier = pltpu.get_barrier_semaphore()
    for step in range(1, count):
        pl.semaphore_signal(
            barrier, inc=1, device_id=(grp, base + member(step) * stride), device_id_type=MESH
        )
    pl.semaphore_wait(barrier, count - 1)
    copies = []
    for index in range(arrays):
        for step in range(1, count):
            peer = member(step)
            source = ins[index] if modes[index] else ins[index].at[peer]
            copy = pltpu.make_async_remote_copy(
                src_ref=source,
                dst_ref=outs[index].at[mine],
                send_sem=send_sem.at[index, step],
                recv_sem=recv_sem.at[index, step],
                device_id=(grp, base + peer * stride),
                device_id_type=MESH,
            )
            copy.start()
            copies.append(copy)
        if modes[index]:
            outs[index][mine] = ins[index][...]
        else:
            outs[index][mine] = ins[index][mine]
    for copy in copies:
        copy.wait()


def tp_exchange(arrays, modes, collective_id, count=None, stride=1):
    count = lax.axis_size("tp") if count is None else count
    shapes = []
    for array, gather in zip(arrays, modes):
        block = array.shape if gather else array.shape[1:]
        shapes.append(jax.ShapeDtypeStruct((count,) + tuple(block), array.dtype))
    vmem = pl.BlockSpec(memory_space=pltpu.VMEM)
    return pl.pallas_call(
        functools.partial(exchange_kernel, count, stride, tuple(modes)),
        out_shape=tuple(shapes),
        in_specs=[vmem] * len(arrays),
        out_specs=tuple([vmem] * len(arrays)),
        scratch_shapes=[
            pltpu.SemaphoreType.DMA((len(arrays), count)),
            pltpu.SemaphoreType.DMA((len(arrays), count)),
        ],
        compiler_params=pltpu.CompilerParams(
            collective_id=collective_id, has_side_effects=True, vmem_limit_bytes=48 * 1024 * 1024
        ),
    )(*arrays)


def permute_exchange(arrays, modes, count, stride):
    size = lax.axis_size("tp")
    me = lax.axis_index("tp")
    mine = lax.rem(me // stride, count)

    def target(i, step):
        member = (i // stride) % count
        return i - member * stride + ((member + step) % count) * stride

    results = []
    for array, gather in zip(arrays, modes):
        own = array if gather else lax.dynamic_index_in_dim(array, mine, 0, False)
        relative = [own]
        for step in range(1, count):
            pairs = [(i, target(i, step)) for i in range(size)]
            block = array if gather else lax.dynamic_index_in_dim(
                array, lax.rem(mine + step, count), 0, False
            )
            relative.append(lax.ppermute(block, "tp", pairs))
        stacked = jnp.stack(relative, 0)
        order = lax.rem(mine - jnp.arange(count, dtype=jnp.int32) + count, count)
        results.append(jnp.take(stacked, order, axis=0))
    return tuple(results)


def attention_kernel(lo_ref, hi_ref, q_ref, cache_ref, mix_ref, peak_ref, total_ref):
    block = pl.program_id(0)
    kv_head = pl.program_id(1)
    lo = lo_ref[block]
    hi = hi_ref[block]
    heads, tokens, width = q_ref.shape
    key_col = pl.multiple_of(kv_head * HD, HD)
    value_col = pl.multiple_of((KVH + kv_head) * HD, HD)
    first = lo // CHUNK
    last = jnp.where(hi > lo, (hi + CHUNK - 1) // CHUNK, first)

    def one_head(head, carry):
        query = q_ref[head]

        def body(chunk, state):
            peak, total, mix = state
            start = pl.multiple_of(chunk * CHUNK, CHUNK)
            keys = cache_ref[pl.ds(start, CHUNK), pl.ds(key_col, HD)]
            values = cache_ref[pl.ds(start, CHUNK), pl.ds(value_col, HD)]
            rows = start + lax.broadcasted_iota(jnp.int32, (1, CHUNK), 1)
            bias = jnp.where((rows >= lo) & (rows < hi), 0.0, -jnp.inf)
            scores = lax.dot_general(
                query, keys, (((1,), (1,)), ((), ())), preferred_element_type=jnp.float32
            ) * (HD ** (-0.5)) + bias
            new_peak = jnp.maximum(peak, jnp.max(scores, axis=1, keepdims=True))
            scale = jnp.exp(peak - new_peak)
            weights = jnp.exp(scores - new_peak)
            total = scale * total + jnp.sum(weights, axis=1, keepdims=True)
            mix = scale * mix + jnp.dot(
                weights.astype(jnp.bfloat16), values, preferred_element_type=jnp.float32
            )
            return new_peak, total, mix

        start_state = (
            jnp.full((tokens, 1), NEG, jnp.float32),
            jnp.zeros((tokens, 1), jnp.float32),
            jnp.zeros((tokens, width), jnp.float32),
        )
        peak, total, mix = lax.fori_loop(first, last, body, start_state)
        mix_ref[head] = mix
        peak_ref[head] = peak
        total_ref[head] = total
        return carry

    lax.fori_loop(0, heads, one_head, 0)


def cache_attention(queries, cache_rows, lo, hi):
    heads, tokens, width = queries.shape
    blocks = tokens // C
    group_size = heads // KVH
    return pl.pallas_call(
        attention_kernel,
        out_shape=(
            jax.ShapeDtypeStruct((heads, tokens, width), jnp.float32),
            jax.ShapeDtypeStruct((heads, tokens, 1), jnp.float32),
            jax.ShapeDtypeStruct((heads, tokens, 1), jnp.float32),
        ),
        grid_spec=pltpu.PrefetchScalarGridSpec(
            num_scalar_prefetch=2,
            grid=(blocks, KVH),
            in_specs=[
                pl.BlockSpec((group_size, C, width), lambda b, j, lo, hi: (j, b, 0)),
                pl.BlockSpec(cache_rows.shape, lambda b, j, lo, hi: (0, 0)),
            ],
            out_specs=[
                pl.BlockSpec((group_size, C, width), lambda b, j, lo, hi: (j, b, 0)),
                pl.BlockSpec((group_size, C, 1), lambda b, j, lo, hi: (j, b, 0)),
                pl.BlockSpec((group_size, C, 1), lambda b, j, lo, hi: (j, b, 0)),
            ],
        ),
        compiler_params=pltpu.CompilerParams(vmem_limit_bytes=48 * 1024 * 1024),
    )(lo, hi, queries, cache_rows)


def combine_many(mix, peak, total):
    top = jnp.max(peak, 0)
    scales = jnp.exp(peak - top[None])
    joined = jnp.sum(mix.astype(jnp.float32) * scales[..., None], 0)
    return joined, top, jnp.sum(total * scales, 0)


def join_partials(first, second):
    first_mix, first_peak, first_total = first
    second_mix, second_peak, second_total = second
    new_peak = jnp.maximum(first_peak, second_peak)
    first_scale = jnp.exp(first_peak - new_peak)
    second_scale = jnp.exp(second_peak - new_peak)
    joined_mix = first_mix * first_scale[..., None] + second_mix * second_scale[..., None]
    return (joined_mix, new_peak, first_total * first_scale + second_total * second_scale)


def to_partner(tree, flip_mask, groups):
    def branch(mask):
        pairs = [(i, i ^ mask) for i in range(groups)]
        return lambda t: jax.tree.map(lambda a: lax.ppermute(a, "grp", pairs), t)

    return lax.switch(flip_mask - 1, [branch(mask) for mask in range(1, groups)], tree)


def on_device(hidden, norm_gain, w_query, w_keyval, w_out, kv_cache, cache_len, partner):
    group_index = lax.axis_index("grp")
    tp_index = lax.axis_index("tp")
    tp_count = lax.axis_size("tp")
    groups = lax.axis_size("grp")
    ring = tp_count // 2
    ring_at = tp_index // 2
    side = tp_index % 2
    local_heads = QH // tp_count
    rows_here = kv_cache.shape[0]
    token_count = hidden.shape[0]
    model_width = w_out.shape[1]
    out_width = model_width // tp_count
    flip_mask = partner[0]

    def w_block(member):
        first = lax.dynamic_slice_in_dim(w_out, (2 * member + side) * out_width, out_width, 1)
        second = lax.dynamic_slice_in_dim(w_out, (2 * member + 1 - side) * out_width, out_width, 1)
        return jnp.concatenate([first, second], 1)

    w_received = [w_block(ring_at)]
    for step in range(1, ring):
        send = w_block(lax.rem(ring_at + step, ring))
        pairs = [(i, (i + 2 * step) % tp_count) for i in range(tp_count)]
        w_received.append(lax.ppermute(send, "tp", pairs))

    float_rows = hidden.astype(jnp.float32)
    normed = (
        float_rows
        * lax.rsqrt(jnp.mean(float_rows * float_rows, -1, keepdims=True) + EPS)
        * norm_gain
    ).astype(jnp.bfloat16)
    query_raw = jnp.dot(normed, w_query, preferred_element_type=jnp.float32).reshape(
        token_count, local_heads, HD
    )
    keyval_part = jnp.dot(normed, w_keyval, preferred_element_type=jnp.float32).astype(jnp.bfloat16)
    lengths = lax.dynamic_slice_in_dim(cache_len, group_index * R, R)
    positions = (lengths[:, None] + jnp.arange(C, dtype=jnp.int32)[None, :]).reshape(token_count)
    query_local = rotate_pairs(query_raw, positions).astype(jnp.bfloat16).transpose(1, 0, 2)
    far_query = to_partner(query_local[:, :C], flip_mask, groups)
    query_ext = jnp.concatenate([query_local, far_query], 1)
    ext_tokens = query_ext.shape[1]
    query_pair, keyval_pair = permute_exchange([query_ext, keyval_part], [True, True], 2, 1)
    query_got, keyval_got = permute_exchange([query_pair, keyval_pair], [True, True], ring, 2)
    queries = query_got.reshape(QH, ext_tokens, HD)
    keyval_all = keyval_got.reshape(tp_count, token_count, -1).transpose(1, 0, 2).reshape(
        token_count, -1
    )

    stored_first = lengths[0] - lengths[0] // 2
    bound_one = stored_first
    bound_two = stored_first + lengths[1]
    far_count = cache_len[partner[group_index] * R] // 2
    starts = jnp.stack([0, bound_one, bound_two]).astype(jnp.int32)
    ends = jnp.stack([bound_one, bound_two, bound_two + far_count]).astype(jnp.int32)
    offset = tp_index * rows_here
    lo = jnp.clip(starts - offset, 0, rows_here)
    hi = jnp.clip(ends - offset, 0, rows_here)
    mix, peak, total = cache_attention(queries, kv_cache, lo, hi)
    quad = 2 * local_heads
    ring_parts = permute_exchange(
        [
            mix.astype(jnp.bfloat16).reshape(ring, quad, ext_tokens, HD),
            peak.reshape(ring, quad, ext_tokens),
            total.reshape(ring, quad, ext_tokens),
        ],
        [False, False, False],
        ring,
        2,
    )
    ring_mix, ring_peak, ring_total = combine_many(*ring_parts)
    pair_parts = permute_exchange(
        [
            ring_mix.astype(jnp.bfloat16).reshape(2, local_heads, ext_tokens, HD),
            ring_peak.reshape(2, local_heads, ext_tokens),
            ring_total.reshape(2, local_heads, ext_tokens),
        ],
        [False, False, False],
        2,
        1,
    )
    own_part = tuple(
        lax.dynamic_index_in_dim(piece.reshape((2, local_heads) + piece.shape[1:]), side, 0, True)
        for piece in (ring_mix, ring_peak, ring_total)
    )
    far_part = tuple(
        lax.dynamic_index_in_dim(piece, 1 - side, 0, True).astype(jnp.float32) for piece in pair_parts
    )
    mix_c, top, total_c = combine_many(
        *(jnp.concatenate([a, b], 0) for a, b in zip(own_part, far_part))
    )
    far_pack = jnp.concatenate(
        [
            mix_c[:, token_count:],
            top[:, None, token_count:],
            total_c[:, None, token_count:],
        ],
        1,
    )
    far_pack = to_partner(far_pack, flip_mask, groups)
    far_back = (far_pack[:, :C], far_pack[:, C], far_pack[:, C + 1])
    combined = (mix_c[:, :token_count], top[:, :token_count], total_c[:, :token_count])
    front = join_partials(tuple(piece[:, :C] for piece in combined), far_back)
    own = tuple(jnp.concatenate([front[i], combined[i][:, C:]], 1) for i in range(3))

    new_keys = rotate_pairs(
        keyval_all[:, : KVH * HD].astype(jnp.float32).reshape(token_count, KVH, HD), positions
    ).astype(jnp.bfloat16)
    new_values = keyval_all[:, KVH * HD :].reshape(token_count, KVH, HD)
    kv_head = (tp_index * local_heads) // (QH // KVH)
    key_rows = lax.dynamic_index_in_dim(new_keys, kv_head, 1, keepdims=False)
    value_rows = lax.dynamic_index_in_dim(new_values, kv_head, 1, keepdims=False)
    token_index = jnp.arange(token_count, dtype=jnp.int32)
    request_of = token_index // C
    within = token_index % C
    self_visible = (request_of[:, None] == request_of[None, :]) & (
        within[None, :] <= within[:, None]
    )
    self_scores = jnp.einsum(
        "htd,sd->hts", query_local, key_rows, preferred_element_type=jnp.float32
    ) * HD ** (-0.5)
    self_scores = jnp.where(self_visible[None], self_scores, -jnp.inf)
    self_peak = jnp.max(self_scores, -1)
    self_weights = jnp.exp(self_scores - self_peak[..., None])
    self_total = jnp.sum(self_weights, -1)
    self_mix = jnp.einsum(
        "hts,sd->htd", self_weights.astype(jnp.bfloat16), value_rows,
        preferred_element_type=jnp.float32,
    )
    final_mix, final_peak, final_total = join_partials(own, (self_mix, self_peak, self_total))
    attention = (final_mix / final_total[..., None]).astype(jnp.bfloat16)
    attention = attention.transpose(1, 0, 2).reshape(token_count, local_heads * HD)
    (attention_ring,) = permute_exchange([attention], [True], ring, 2)
    sums = None
    for step in range(ring):
        source = lax.rem(ring_at - step + ring, ring)
        piece = jnp.dot(
            lax.dynamic_index_in_dim(attention_ring, source, 0, False),
            w_received[step],
            preferred_element_type=jnp.float32,
        )
        sums = piece if sums is None else sums + piece
    (other_got,) = permute_exchange([sums[:, out_width:].astype(jnp.bfloat16)], [True], 2, 1)
    other = lax.dynamic_index_in_dim(other_got, 1 - side, 0, False)
    return (sums[:, :out_width] + other.astype(jnp.float32)).astype(jnp.bfloat16)


def solution(mesh):
    placed = (
        P("grp", None),
        P(),
        P(None, "tp"),
        P(None, "tp"),
        P("tp", None),
        P(("grp", "tp"), None),
        P(),
        P(),
    )
    return jax.shard_map(
        on_device, mesh=mesh, in_specs=placed, out_specs=P("grp", "tp"), check_vma=False
    )
```

```python
import functools

import jax
import jax.numpy as jnp
from jax import lax
from jax.experimental import pallas as pl
from jax.experimental.pallas import tpu as pltpu
from jax.sharding import PartitionSpec as P

HD = 128
QH = 16
KVH = 2
C = 128
R = 2

THETA = 5000000.0
EPS = 1e-05
NEG = -1e30
CHUNK = 256
MESH = pl.DeviceIdType.MESH


def rotate_pairs(values, positions):
    width = values.shape[-1]
    half_width = width // 2
    frequency = THETA ** (-2.0 * jnp.arange(half_width, dtype=jnp.float32) / width)
    angles = positions.astype(jnp.float32)[:, None] * frequency[None, :]
    cosine_part = jnp.cos(angles)[:, None, :]
    sine_part = jnp.sin(angles)[:, None, :]
    first_half = values[..., :half_width]
    second_half = values[..., half_width:]
    return jnp.concatenate(
        [
            first_half * cosine_part - second_half * sine_part,
            second_half * cosine_part + first_half * sine_part,
        ],
        -1,
    )


def exchange_kernel(count, stride, modes, *refs):
    arrays = len(modes)
    ins, outs = refs[:arrays], refs[arrays : 2 * arrays]
    send_sem, recv_sem = refs[2 * arrays :]
    me = lax.axis_index("tp")
    grp = lax.axis_index("grp")
    mine = lax.rem(me // stride, count)
    base = me - mine * stride

    def member(step):
        return lax.rem(mine + step, count)

    barrier = pltpu.get_barrier_semaphore()
    for step in range(1, count):
        pl.semaphore_signal(
            barrier, inc=1, device_id=(grp, base + member(step) * stride), device_id_type=MESH
        )
    pl.semaphore_wait(barrier, count - 1)
    copies = []
    for index in range(arrays):
        for step in range(1, count):
            peer = member(step)
            source = ins[index] if modes[index] else ins[index].at[peer]
            copy = pltpu.make_async_remote_copy(
                src_ref=source,
                dst_ref=outs[index].at[mine],
                send_sem=send_sem.at[index, step],
                recv_sem=recv_sem.at[index, step],
                device_id=(grp, base + peer * stride),
                device_id_type=MESH,
            )
            copy.start()
            copies.append(copy)
        if modes[index]:
            outs[index][mine] = ins[index][...]
        else:
            outs[index][mine] = ins[index][mine]
    for copy in copies:
        copy.wait()


def tp_exchange(arrays, modes, collective_id, count=None, stride=1):
    count = lax.axis_size("tp") if count is None else count
    shapes = []
    for array, gather in zip(arrays, modes):
        block = array.shape if gather else array.shape[1:]
        shapes.append(jax.ShapeDtypeStruct((count,) + tuple(block), array.dtype))
    vmem = pl.BlockSpec(memory_space=pltpu.VMEM)
    return pl.pallas_call(
        functools.partial(exchange_kernel, count, stride, tuple(modes)),
        out_shape=tuple(shapes),
        in_specs=[vmem] * len(arrays),
        out_specs=tuple([vmem] * len(arrays)),
        scratch_shapes=[
            pltpu.SemaphoreType.DMA((len(arrays), count)),
            pltpu.SemaphoreType.DMA((len(arrays), count)),
        ],
        compiler_params=pltpu.CompilerParams(
            collective_id=collective_id, has_side_effects=True, vmem_limit_bytes=48 * 1024 * 1024
        ),
    )(*arrays)


def gather_kernel(arrays, *refs):
    ins, outs = refs[:arrays], refs[arrays : 2 * arrays]
    pair_send, pair_recv, ring_send, ring_recv, hop_send, hop_recv = refs[2 * arrays :]
    me = lax.axis_index("tp")
    grp = lax.axis_index("grp")
    ring = lax.axis_size("tp") // 2
    side = me % 2
    ring_at = me // 2
    partner = (grp, ring_at * 2 + 1 - side)

    def member(step):
        return (grp, lax.rem(ring_at + step, ring) * 2 + side)

    barrier = pltpu.get_barrier_semaphore()
    pl.semaphore_signal(barrier, inc=1, device_id=partner, device_id_type=MESH)
    for step in range(1, ring):
        pl.semaphore_signal(barrier, inc=1, device_id=member(step), device_id_type=MESH)
    pl.semaphore_wait(barrier, ring)
    pairs, direct = [], []
    for index in range(arrays):
        copy = pltpu.make_async_remote_copy(
            src_ref=ins[index],
            dst_ref=outs[index].at[ring_at, side],
            send_sem=pair_send.at[index],
            recv_sem=pair_recv.at[index],
            device_id=partner,
            device_id_type=MESH,
        )
        copy.start()
        pairs.append(copy)
        for step in range(1, ring):
            copy = pltpu.make_async_remote_copy(
                src_ref=ins[index],
                dst_ref=outs[index].at[ring_at, side],
                send_sem=ring_send.at[index, step],
                recv_sem=ring_recv.at[index, step],
                device_id=member(step),
                device_id_type=MESH,
            )
            copy.start()
            direct.append(copy)
        outs[index][ring_at, side] = ins[index][...]
    hops = []
    for index in range(arrays):
        pairs[index].wait_recv()
        for step in range(1, ring):
            copy = pltpu.make_async_remote_copy(
                src_ref=outs[index].at[ring_at, 1 - side],
                dst_ref=outs[index].at[ring_at, 1 - side],
                send_sem=hop_send.at[index, step],
                recv_sem=hop_recv.at[index, step],
                device_id=member(step),
                device_id_type=MESH,
            )
            copy.start()
            hops.append(copy)
    for copy in pairs:
        copy.wait_send()
    for copy in direct + hops:
        copy.wait()


def group_gather(arrays, collective_id):
    ring = lax.axis_size("tp") // 2
    count = len(arrays)
    shapes = [jax.ShapeDtypeStruct((ring, 2) + a.shape, a.dtype) for a in arrays]
    vmem = pl.BlockSpec(memory_space=pltpu.VMEM)
    return pl.pallas_call(
        functools.partial(gather_kernel, count),
        out_shape=tuple(shapes),
        in_specs=[vmem] * count,
        out_specs=tuple([vmem] * count),
        scratch_shapes=[
            pltpu.SemaphoreType.DMA((count,)),
            pltpu.SemaphoreType.DMA((count,)),
            pltpu.SemaphoreType.DMA((count, ring)),
            pltpu.SemaphoreType.DMA((count, ring)),
            pltpu.SemaphoreType.DMA((count, ring)),
            pltpu.SemaphoreType.DMA((count, ring)),
        ],
        compiler_params=pltpu.CompilerParams(
            collective_id=collective_id, has_side_effects=True, vmem_limit_bytes=48 * 1024 * 1024
        ),
    )(*arrays)


def attention_kernel(lo_ref, hi_ref, q_ref, cache_ref, mix_ref, peak_ref, total_ref):
    block = pl.program_id(0)
    kv_head = pl.program_id(1)
    lo = lo_ref[block]
    hi = hi_ref[block]
    heads, tokens, width = q_ref.shape
    key_col = pl.multiple_of(kv_head * HD, HD)
    value_col = pl.multiple_of((KVH + kv_head) * HD, HD)
    first = lo // CHUNK
    last = jnp.where(hi > lo, (hi + CHUNK - 1) // CHUNK, first)

    def one_head(head, carry):
        query = q_ref[head]

        def body(chunk, state):
            peak, total, mix = state
            start = pl.multiple_of(chunk * CHUNK, CHUNK)
            keys = cache_ref[pl.ds(start, CHUNK), pl.ds(key_col, HD)]
            values = cache_ref[pl.ds(start, CHUNK), pl.ds(value_col, HD)]
            rows = start + lax.broadcasted_iota(jnp.int32, (1, CHUNK), 1)
            bias = jnp.where((rows >= lo) & (rows < hi), 0.0, -jnp.inf)
            scores = lax.dot_general(
                query, keys, (((1,), (1,)), ((), ())), preferred_element_type=jnp.float32
            ) * (HD ** (-0.5)) + bias
            new_peak = jnp.maximum(peak, jnp.max(scores, axis=1, keepdims=True))
            scale = jnp.exp(peak - new_peak)
            weights = jnp.exp(scores - new_peak)
            total = scale * total + jnp.sum(weights, axis=1, keepdims=True)
            mix = scale * mix + jnp.dot(
                weights.astype(jnp.bfloat16), values, preferred_element_type=jnp.float32
            )
            return new_peak, total, mix

        start_state = (
            jnp.full((tokens, 1), NEG, jnp.float32),
            jnp.zeros((tokens, 1), jnp.float32),
            jnp.zeros((tokens, width), jnp.float32),
        )
        peak, total, mix = lax.fori_loop(first, last, body, start_state)
        mix_ref[head] = mix
        peak_ref[head] = peak
        total_ref[head] = total
        return carry

    lax.fori_loop(0, heads, one_head, 0)


def cache_attention(queries, cache_rows, lo, hi):
    heads, tokens, width = queries.shape
    blocks = tokens // C
    group_size = heads // KVH
    return pl.pallas_call(
        attention_kernel,
        out_shape=(
            jax.ShapeDtypeStruct((heads, tokens, width), jnp.float32),
            jax.ShapeDtypeStruct((heads, tokens, 1), jnp.float32),
            jax.ShapeDtypeStruct((heads, tokens, 1), jnp.float32),
        ),
        grid_spec=pltpu.PrefetchScalarGridSpec(
            num_scalar_prefetch=2,
            grid=(blocks, KVH),
            in_specs=[
                pl.BlockSpec((group_size, C, width), lambda b, j, lo, hi: (j, b, 0)),
                pl.BlockSpec(cache_rows.shape, lambda b, j, lo, hi: (0, 0)),
            ],
            out_specs=[
                pl.BlockSpec((group_size, C, width), lambda b, j, lo, hi: (j, b, 0)),
                pl.BlockSpec((group_size, C, 1), lambda b, j, lo, hi: (j, b, 0)),
                pl.BlockSpec((group_size, C, 1), lambda b, j, lo, hi: (j, b, 0)),
            ],
        ),
        compiler_params=pltpu.CompilerParams(vmem_limit_bytes=48 * 1024 * 1024),
    )(lo, hi, queries, cache_rows)


def join_partials(first, second):
    first_mix, first_peak, first_total = first
    second_mix, second_peak, second_total = second
    new_peak = jnp.maximum(first_peak, second_peak)
    first_scale = jnp.exp(first_peak - new_peak)
    second_scale = jnp.exp(second_peak - new_peak)
    joined_mix = first_mix * first_scale[..., None] + second_mix * second_scale[..., None]
    return (joined_mix, new_peak, first_total * first_scale + second_total * second_scale)


def to_partner(tree, flip_mask, groups):
    def branch(mask):
        pairs = [(i, i ^ mask) for i in range(groups)]
        return lambda t: jax.tree.map(lambda a: lax.ppermute(a, "grp", pairs), t)

    return lax.switch(flip_mask - 1, [branch(mask) for mask in range(1, groups)], tree)


def on_device(hidden, norm_gain, w_query, w_keyval, w_out, kv_cache, cache_len, partner):
    group_index = lax.axis_index("grp")
    tp_index = lax.axis_index("tp")
    tp_count = lax.axis_size("tp")
    groups = lax.axis_size("grp")
    ring = tp_count // 2
    ring_at = tp_index // 2
    side = tp_index % 2
    local_heads = QH // tp_count
    rows_here = kv_cache.shape[0]
    token_count = hidden.shape[0]
    model_width = w_out.shape[1]
    out_width = model_width // tp_count
    flip_mask = partner[0]

    def w_block(member):
        return lax.dynamic_slice_in_dim(w_out, member * 2 * out_width, 2 * out_width, 1)

    w_received = [w_block(ring_at)]
    for step in range(1, ring):
        send = w_block(lax.rem(ring_at + step, ring))
        pairs = [(i, (i + 2 * step) % tp_count) for i in range(tp_count)]
        w_received.append(lax.ppermute(send, "tp", pairs))

    float_rows = hidden.astype(jnp.float32)
    normed = (
        float_rows
        * lax.rsqrt(jnp.mean(float_rows * float_rows, -1, keepdims=True) + EPS)
        * norm_gain
    ).astype(jnp.bfloat16)
    query_raw = jnp.dot(normed, w_query, preferred_element_type=jnp.float32).reshape(
        token_count, local_heads, HD
    )
    keyval_part = jnp.dot(normed, w_keyval, preferred_element_type=jnp.float32).astype(jnp.bfloat16)
    lengths = lax.dynamic_slice_in_dim(cache_len, group_index * R, R)
    positions = (lengths[:, None] + jnp.arange(C, dtype=jnp.int32)[None, :]).reshape(token_count)
    query_local = rotate_pairs(query_raw, positions).astype(jnp.bfloat16).transpose(1, 0, 2)
    far_query = to_partner(query_local[:, :C], flip_mask, groups)
    query_ext = jnp.concatenate([query_local, far_query], 1)
    ext_tokens = query_ext.shape[1]
    query_got, keyval_got = group_gather([query_ext, keyval_part], 0)
    queries = query_got.reshape(QH, ext_tokens, HD)
    keyval_all = keyval_got.reshape(tp_count, token_count, -1).transpose(1, 0, 2).reshape(
        token_count, -1
    )

    stored_first = lengths[0] - lengths[0] // 2
    bound_one = stored_first
    bound_two = stored_first + lengths[1]
    far_count = cache_len[partner[group_index] * R] // 2
    starts = jnp.stack([0, bound_one, bound_two]).astype(jnp.int32)
    ends = jnp.stack([bound_one, bound_two, bound_two + far_count]).astype(jnp.int32)
    offset = tp_index * rows_here
    lo = jnp.clip(starts - offset, 0, rows_here)
    hi = jnp.clip(ends - offset, 0, rows_here)
    mix, peak, total = cache_attention(queries, kv_cache, lo, hi)
    mix_got, peak_got, total_got = tp_exchange(
        [
            mix.astype(jnp.bfloat16).reshape(tp_count, local_heads, ext_tokens, HD),
            peak.reshape(tp_count, local_heads, ext_tokens),
            total.reshape(tp_count, local_heads, ext_tokens),
        ],
        [False, False, False],
        2,
    )
    top = jnp.max(peak_got, 0)
    scales = jnp.exp(peak_got - top[None])
    mix_c = jnp.sum(mix_got.astype(jnp.float32) * scales[..., None], 0)
    total_c = jnp.sum(total_got * scales, 0)
    far_pack = jnp.concatenate(
        [
            mix_c[:, token_count:],
            top[:, None, token_count:],
            total_c[:, None, token_count:],
        ],
        1,
    )
    far_pack = to_partner(far_pack, flip_mask, groups)
    far_back = (far_pack[:, :C], far_pack[:, C], far_pack[:, C + 1])
    combined = (mix_c[:, :token_count], top[:, :token_count], total_c[:, :token_count])
    front = join_partials(tuple(piece[:, :C] for piece in combined), far_back)
    own = tuple(jnp.concatenate([front[i], combined[i][:, C:]], 1) for i in range(3))

    new_keys = rotate_pairs(
        keyval_all[:, : KVH * HD].astype(jnp.float32).reshape(token_count, KVH, HD), positions
    ).astype(jnp.bfloat16)
    new_values = keyval_all[:, KVH * HD :].reshape(token_count, KVH, HD)
    kv_head = (tp_index * local_heads) // (QH // KVH)
    key_rows = lax.dynamic_index_in_dim(new_keys, kv_head, 1, keepdims=False)
    value_rows = lax.dynamic_index_in_dim(new_values, kv_head, 1, keepdims=False)
    token_index = jnp.arange(token_count, dtype=jnp.int32)
    request_of = token_index // C
    within = token_index % C
    self_visible = (request_of[:, None] == request_of[None, :]) & (
        within[None, :] <= within[:, None]
    )
    self_scores = jnp.einsum(
        "htd,sd->hts", query_local, key_rows, preferred_element_type=jnp.float32
    ) * HD ** (-0.5)
    self_scores = jnp.where(self_visible[None], self_scores, -jnp.inf)
    self_peak = jnp.max(self_scores, -1)
    self_weights = jnp.exp(self_scores - self_peak[..., None])
    self_total = jnp.sum(self_weights, -1)
    self_mix = jnp.einsum(
        "hts,sd->htd", self_weights.astype(jnp.bfloat16), value_rows,
        preferred_element_type=jnp.float32,
    )
    final_mix, final_peak, final_total = join_partials(own, (self_mix, self_peak, self_total))
    attention = (final_mix / final_total[..., None]).astype(jnp.bfloat16)
    attention = attention.transpose(1, 0, 2).reshape(token_count, local_heads * HD)
    (attention_ring,) = tp_exchange([attention], [True], 3, ring, 2)
    sums = None
    for step in range(ring):
        source = lax.rem(ring_at - step + ring, ring)
        piece = jnp.dot(
            lax.dynamic_index_in_dim(attention_ring, source, 0, False),
            w_received[step],
            preferred_element_type=jnp.float32,
        )
        sums = piece if sums is None else sums + piece
    halves = sums.reshape(token_count, 2, out_width).transpose(1, 0, 2)
    (halves_got,) = tp_exchange([halves.astype(jnp.bfloat16)], [False], 4, 2, 1)
    mine = lax.dynamic_index_in_dim(halves, side, 0, False)
    other = lax.dynamic_index_in_dim(halves_got, 1 - side, 0, False)
    return (mine + other.astype(jnp.float32)).astype(jnp.bfloat16)


def solution(mesh):
    placed = (
        P("grp", None),
        P(),
        P(None, "tp"),
        P(None, "tp"),
        P("tp", None),
        P(("grp", "tp"), None),
        P(),
        P(),
    )
    return jax.shard_map(
        on_device, mesh=mesh, in_specs=placed, out_specs=P("grp", "tp"), check_vma=False
    )
```

```python
import functools

import jax
import jax.numpy as jnp
from jax import lax
from jax.experimental import pallas as pl
from jax.experimental.pallas import tpu as pltpu
from jax.sharding import PartitionSpec as P

HD = 128
QH = 16
KVH = 2
C = 128
R = 2

THETA = 5000000.0
EPS = 1e-05
NEG = -1e30
CHUNK = 256
MESH = pl.DeviceIdType.MESH


def rotate_pairs(values, positions):
    width = values.shape[-1]
    half_width = width // 2
    frequency = THETA ** (-2.0 * jnp.arange(half_width, dtype=jnp.float32) / width)
    angles = positions.astype(jnp.float32)[:, None] * frequency[None, :]
    cosine_part = jnp.cos(angles)[:, None, :]
    sine_part = jnp.sin(angles)[:, None, :]
    first_half = values[..., :half_width]
    second_half = values[..., half_width:]
    return jnp.concatenate(
        [
            first_half * cosine_part - second_half * sine_part,
            second_half * cosine_part + first_half * sine_part,
        ],
        -1,
    )


def exchange_kernel(count, stride, modes, *refs):
    arrays = len(modes)
    ins, outs = refs[:arrays], refs[arrays : 2 * arrays]
    send_sem, recv_sem = refs[2 * arrays :]
    me = lax.axis_index("tp")
    grp = lax.axis_index("grp")
    mine = lax.rem(me // stride, count)
    base = me - mine * stride

    def member(step):
        return lax.rem(mine + step, count)

    barrier = pltpu.get_barrier_semaphore()
    for step in range(1, count):
        pl.semaphore_signal(
            barrier, inc=1, device_id=(grp, base + member(step) * stride), device_id_type=MESH
        )
    pl.semaphore_wait(barrier, count - 1)
    copies = []
    for index in range(arrays):
        for step in range(1, count):
            peer = member(step)
            source = ins[index] if modes[index] else ins[index].at[peer]
            copy = pltpu.make_async_remote_copy(
                src_ref=source,
                dst_ref=outs[index].at[mine],
                send_sem=send_sem.at[index, step],
                recv_sem=recv_sem.at[index, step],
                device_id=(grp, base + peer * stride),
                device_id_type=MESH,
            )
            copy.start()
            copies.append(copy)
        if modes[index]:
            outs[index][mine] = ins[index][...]
        else:
            outs[index][mine] = ins[index][mine]
    for copy in copies:
        copy.wait()


def tp_exchange(arrays, modes, collective_id, count=None, stride=1):
    count = lax.axis_size("tp") if count is None else count
    shapes = []
    for array, gather in zip(arrays, modes):
        block = array.shape if gather else array.shape[1:]
        shapes.append(jax.ShapeDtypeStruct((count,) + tuple(block), array.dtype))
    vmem = pl.BlockSpec(memory_space=pltpu.VMEM)
    return pl.pallas_call(
        functools.partial(exchange_kernel, count, stride, tuple(modes)),
        out_shape=tuple(shapes),
        in_specs=[vmem] * len(arrays),
        out_specs=tuple([vmem] * len(arrays)),
        scratch_shapes=[
            pltpu.SemaphoreType.DMA((len(arrays), count)),
            pltpu.SemaphoreType.DMA((len(arrays), count)),
        ],
        compiler_params=pltpu.CompilerParams(
            collective_id=collective_id, has_side_effects=True, vmem_limit_bytes=48 * 1024 * 1024
        ),
    )(*arrays)


def gather_kernel(arrays, *refs):
    ins, outs = refs[:arrays], refs[arrays : 2 * arrays]
    pair_send, pair_recv, ring_send, ring_recv, hop_send, hop_recv = refs[2 * arrays :]
    me = lax.axis_index("tp")
    grp = lax.axis_index("grp")
    ring = lax.axis_size("tp") // 2
    side = me % 2
    ring_at = me // 2
    partner = (grp, ring_at * 2 + 1 - side)

    def member(step):
        return (grp, lax.rem(ring_at + step, ring) * 2 + side)

    barrier = pltpu.get_barrier_semaphore()
    pl.semaphore_signal(barrier, inc=1, device_id=partner, device_id_type=MESH)
    for step in range(1, ring):
        pl.semaphore_signal(barrier, inc=1, device_id=member(step), device_id_type=MESH)
    pl.semaphore_wait(barrier, ring)
    pairs, direct = [], []
    for index in range(arrays):
        copy = pltpu.make_async_remote_copy(
            src_ref=ins[index],
            dst_ref=outs[index].at[ring_at, side],
            send_sem=pair_send.at[index],
            recv_sem=pair_recv.at[index],
            device_id=partner,
            device_id_type=MESH,
        )
        copy.start()
        pairs.append(copy)
        for step in range(1, ring):
            copy = pltpu.make_async_remote_copy(
                src_ref=ins[index],
                dst_ref=outs[index].at[ring_at, side],
                send_sem=ring_send.at[index, step],
                recv_sem=ring_recv.at[index, step],
                device_id=member(step),
                device_id_type=MESH,
            )
            copy.start()
            direct.append(copy)
        outs[index][ring_at, side] = ins[index][...]
    hops = []
    for index in range(arrays):
        pairs[index].wait_recv()
        for step in range(1, ring):
            copy = pltpu.make_async_remote_copy(
                src_ref=outs[index].at[ring_at, 1 - side],
                dst_ref=outs[index].at[ring_at, 1 - side],
                send_sem=hop_send.at[index, step],
                recv_sem=hop_recv.at[index, step],
                device_id=member(step),
                device_id_type=MESH,
            )
            copy.start()
            hops.append(copy)
    for copy in pairs:
        copy.wait_send()
    for copy in direct + hops:
        copy.wait()


def group_gather(arrays, collective_id):
    ring = lax.axis_size("tp") // 2
    count = len(arrays)
    shapes = [jax.ShapeDtypeStruct((ring, 2) + a.shape, a.dtype) for a in arrays]
    vmem = pl.BlockSpec(memory_space=pltpu.VMEM)
    return pl.pallas_call(
        functools.partial(gather_kernel, count),
        out_shape=tuple(shapes),
        in_specs=[vmem] * count,
        out_specs=tuple([vmem] * count),
        scratch_shapes=[
            pltpu.SemaphoreType.DMA((count,)),
            pltpu.SemaphoreType.DMA((count,)),
            pltpu.SemaphoreType.DMA((count, ring)),
            pltpu.SemaphoreType.DMA((count, ring)),
            pltpu.SemaphoreType.DMA((count, ring)),
            pltpu.SemaphoreType.DMA((count, ring)),
        ],
        compiler_params=pltpu.CompilerParams(
            collective_id=collective_id, has_side_effects=True, vmem_limit_bytes=48 * 1024 * 1024
        ),
    )(*arrays)


def attention_kernel(lo_ref, hi_ref, q_ref, cache_ref, mix_ref, peak_ref, total_ref):
    block = pl.program_id(0)
    kv_head = pl.program_id(1)
    lo = lo_ref[block]
    hi = hi_ref[block]
    heads, tokens, width = q_ref.shape
    key_col = pl.multiple_of(kv_head * HD, HD)
    value_col = pl.multiple_of((KVH + kv_head) * HD, HD)
    first = lo // CHUNK
    last = jnp.where(hi > lo, (hi + CHUNK - 1) // CHUNK, first)

    def one_head(head, carry):
        query = q_ref[head]

        def body(chunk, state):
            peak, total, mix = state
            start = pl.multiple_of(chunk * CHUNK, CHUNK)
            keys = cache_ref[pl.ds(start, CHUNK), pl.ds(key_col, HD)]
            values = cache_ref[pl.ds(start, CHUNK), pl.ds(value_col, HD)]
            rows = start + lax.broadcasted_iota(jnp.int32, (1, CHUNK), 1)
            bias = jnp.where((rows >= lo) & (rows < hi), 0.0, -jnp.inf)
            scores = lax.dot_general(
                query, keys, (((1,), (1,)), ((), ())), preferred_element_type=jnp.float32
            ) * (HD ** (-0.5)) + bias
            new_peak = jnp.maximum(peak, jnp.max(scores, axis=1, keepdims=True))
            scale = jnp.exp(peak - new_peak)
            weights = jnp.exp(scores - new_peak)
            total = scale * total + jnp.sum(weights, axis=1, keepdims=True)
            mix = scale * mix + jnp.dot(
                weights.astype(jnp.bfloat16), values, preferred_element_type=jnp.float32
            )
            return new_peak, total, mix

        start_state = (
            jnp.full((tokens, 1), NEG, jnp.float32),
            jnp.zeros((tokens, 1), jnp.float32),
            jnp.zeros((tokens, width), jnp.float32),
        )
        peak, total, mix = lax.fori_loop(first, last, body, start_state)
        mix_ref[head] = mix
        peak_ref[head] = peak
        total_ref[head] = total
        return carry

    lax.fori_loop(0, heads, one_head, 0)


def cache_attention(queries, cache_rows, lo, hi):
    heads, tokens, width = queries.shape
    blocks = tokens // C
    group_size = heads // KVH
    return pl.pallas_call(
        attention_kernel,
        out_shape=(
            jax.ShapeDtypeStruct((heads, tokens, width), jnp.float32),
            jax.ShapeDtypeStruct((heads, tokens, 1), jnp.float32),
            jax.ShapeDtypeStruct((heads, tokens, 1), jnp.float32),
        ),
        grid_spec=pltpu.PrefetchScalarGridSpec(
            num_scalar_prefetch=2,
            grid=(blocks, KVH),
            in_specs=[
                pl.BlockSpec((group_size, C, width), lambda b, j, lo, hi: (j, b, 0)),
                pl.BlockSpec(cache_rows.shape, lambda b, j, lo, hi: (0, 0)),
            ],
            out_specs=[
                pl.BlockSpec((group_size, C, width), lambda b, j, lo, hi: (j, b, 0)),
                pl.BlockSpec((group_size, C, 1), lambda b, j, lo, hi: (j, b, 0)),
                pl.BlockSpec((group_size, C, 1), lambda b, j, lo, hi: (j, b, 0)),
            ],
        ),
        compiler_params=pltpu.CompilerParams(vmem_limit_bytes=48 * 1024 * 1024),
    )(lo, hi, queries, cache_rows)


def join_partials(first, second):
    first_mix, first_peak, first_total = first
    second_mix, second_peak, second_total = second
    new_peak = jnp.maximum(first_peak, second_peak)
    first_scale = jnp.exp(first_peak - new_peak)
    second_scale = jnp.exp(second_peak - new_peak)
    joined_mix = first_mix * first_scale[..., None] + second_mix * second_scale[..., None]
    return (joined_mix, new_peak, first_total * first_scale + second_total * second_scale)


def to_partner(tree, flip_mask, groups):
    def branch(mask):
        pairs = [(i, i ^ mask) for i in range(groups)]
        return lambda t: jax.tree.map(lambda a: lax.ppermute(a, "grp", pairs), t)

    return lax.switch(flip_mask - 1, [branch(mask) for mask in range(1, groups)], tree)


def on_device(hidden, norm_gain, w_query, w_keyval, w_out, kv_cache, cache_len, partner):
    group_index = lax.axis_index("grp")
    tp_index = lax.axis_index("tp")
    tp_count = lax.axis_size("tp")
    groups = lax.axis_size("grp")
    ring = tp_count // 2
    ring_at = tp_index // 2
    side = tp_index % 2
    local_heads = QH // tp_count
    rows_here = kv_cache.shape[0]
    token_count = hidden.shape[0]
    model_width = w_out.shape[1]
    out_width = model_width // tp_count
    flip_mask = partner[0]

    def w_block(member):
        first = lax.dynamic_slice_in_dim(w_out, (2 * member + side) * out_width, out_width, 1)
        second = lax.dynamic_slice_in_dim(w_out, (2 * member + 1 - side) * out_width, out_width, 1)
        return jnp.concatenate([first, second], 1)

    w_received = [w_block(ring_at)]
    for step in range(1, ring):
        send = w_block(lax.rem(ring_at + step, ring))
        pairs = [(i, (i + 2 * step) % tp_count) for i in range(tp_count)]
        w_received.append(lax.ppermute(send, "tp", pairs))

    float_rows = hidden.astype(jnp.float32)
    normed = (
        float_rows
        * lax.rsqrt(jnp.mean(float_rows * float_rows, -1, keepdims=True) + EPS)
        * norm_gain
    ).astype(jnp.bfloat16)
    query_raw = jnp.dot(normed, w_query, preferred_element_type=jnp.float32).reshape(
        token_count, local_heads, HD
    )
    keyval_part = jnp.dot(normed, w_keyval, preferred_element_type=jnp.float32).astype(jnp.bfloat16)
    lengths = lax.dynamic_slice_in_dim(cache_len, group_index * R, R)
    positions = (lengths[:, None] + jnp.arange(C, dtype=jnp.int32)[None, :]).reshape(token_count)
    query_local = rotate_pairs(query_raw, positions).astype(jnp.bfloat16).transpose(1, 0, 2)
    far_query = to_partner(query_local[:, :C], flip_mask, groups)
    query_ext = jnp.concatenate([query_local, far_query], 1)
    ext_tokens = query_ext.shape[1]
    query_got, keyval_got = group_gather([query_ext, keyval_part], 0)
    queries = query_got.reshape(QH, ext_tokens, HD)
    keyval_all = keyval_got.reshape(tp_count, token_count, -1).transpose(1, 0, 2).reshape(
        token_count, -1
    )

    stored_first = lengths[0] - lengths[0] // 2
    bound_one = stored_first
    bound_two = stored_first + lengths[1]
    far_count = cache_len[partner[group_index] * R] // 2
    starts = jnp.stack([0, bound_one, bound_two]).astype(jnp.int32)
    ends = jnp.stack([bound_one, bound_two, bound_two + far_count]).astype(jnp.int32)
    offset = tp_index * rows_here
    lo = jnp.clip(starts - offset, 0, rows_here)
    hi = jnp.clip(ends - offset, 0, rows_here)
    mix, peak, total = cache_attention(queries, kv_cache, lo, hi)
    mix_got, peak_got, total_got = tp_exchange(
        [
            mix.astype(jnp.bfloat16).reshape(tp_count, local_heads, ext_tokens, HD),
            peak.reshape(tp_count, local_heads, ext_tokens),
            total.reshape(tp_count, local_heads, ext_tokens),
        ],
        [False, False, False],
        2,
    )
    top = jnp.max(peak_got, 0)
    scales = jnp.exp(peak_got - top[None])
    mix_c = jnp.sum(mix_got.astype(jnp.float32) * scales[..., None], 0)
    total_c = jnp.sum(total_got * scales, 0)
    far_pack = jnp.concatenate(
        [
            mix_c[:, token_count:],
            top[:, None, token_count:],
            total_c[:, None, token_count:],
        ],
        1,
    )
    far_pack = to_partner(far_pack, flip_mask, groups)
    far_back = (far_pack[:, :C], far_pack[:, C], far_pack[:, C + 1])
    combined = (mix_c[:, :token_count], top[:, :token_count], total_c[:, :token_count])
    front = join_partials(tuple(piece[:, :C] for piece in combined), far_back)
    own = tuple(jnp.concatenate([front[i], combined[i][:, C:]], 1) for i in range(3))

    new_keys = rotate_pairs(
        keyval_all[:, : KVH * HD].astype(jnp.float32).reshape(token_count, KVH, HD), positions
    ).astype(jnp.bfloat16)
    new_values = keyval_all[:, KVH * HD :].reshape(token_count, KVH, HD)
    kv_head = (tp_index * local_heads) // (QH // KVH)
    key_rows = lax.dynamic_index_in_dim(new_keys, kv_head, 1, keepdims=False)
    value_rows = lax.dynamic_index_in_dim(new_values, kv_head, 1, keepdims=False)
    token_index = jnp.arange(token_count, dtype=jnp.int32)
    request_of = token_index // C
    within = token_index % C
    self_visible = (request_of[:, None] == request_of[None, :]) & (
        within[None, :] <= within[:, None]
    )
    self_scores = jnp.einsum(
        "htd,sd->hts", query_local, key_rows, preferred_element_type=jnp.float32
    ) * HD ** (-0.5)
    self_scores = jnp.where(self_visible[None], self_scores, -jnp.inf)
    self_peak = jnp.max(self_scores, -1)
    self_weights = jnp.exp(self_scores - self_peak[..., None])
    self_total = jnp.sum(self_weights, -1)
    self_mix = jnp.einsum(
        "hts,sd->htd", self_weights.astype(jnp.bfloat16), value_rows,
        preferred_element_type=jnp.float32,
    )
    final_mix, final_peak, final_total = join_partials(own, (self_mix, self_peak, self_total))
    attention = (final_mix / final_total[..., None]).astype(jnp.bfloat16)
    attention = attention.transpose(1, 0, 2).reshape(token_count, local_heads * HD)
    (attention_ring,) = tp_exchange([attention], [True], 3, ring, 2)
    sums = None
    for step in range(ring):
        source = lax.rem(ring_at - step + ring, ring)
        piece = jnp.dot(
            lax.dynamic_index_in_dim(attention_ring, source, 0, False),
            w_received[step],
            preferred_element_type=jnp.float32,
        )
        sums = piece if sums is None else sums + piece
    (other_got,) = tp_exchange([sums[:, out_width:].astype(jnp.bfloat16)], [True], 4, 2, 1)
    other = lax.dynamic_index_in_dim(other_got, 1 - side, 0, False)
    return (sums[:, :out_width] + other.astype(jnp.float32)).astype(jnp.bfloat16)


def solution(mesh):
    placed = (
        P("grp", None),
        P(),
        P(None, "tp"),
        P(None, "tp"),
        P("tp", None),
        P(("grp", "tp"), None),
        P(),
        P(),
    )
    return jax.shard_map(
        on_device, mesh=mesh, in_specs=placed, out_specs=P("grp", "tp"), check_vma=False
    )
```

```python
import functools

import jax
import jax.numpy as jnp
from jax import lax
from jax.experimental import pallas as pl
from jax.experimental.pallas import tpu as pltpu
from jax.sharding import PartitionSpec as P

HD = 128
QH = 16
KVH = 2
C = 128
R = 2

THETA = 5000000.0
EPS = 1e-05
NEG = -1e30
CHUNK = 256
MESH = pl.DeviceIdType.MESH


def rotate_pairs(values, positions):
    width = values.shape[-1]
    half_width = width // 2
    frequency = THETA ** (-2.0 * jnp.arange(half_width, dtype=jnp.float32) / width)
    angles = positions.astype(jnp.float32)[:, None] * frequency[None, :]
    cosine_part = jnp.cos(angles)[:, None, :]
    sine_part = jnp.sin(angles)[:, None, :]
    first_half = values[..., :half_width]
    second_half = values[..., half_width:]
    return jnp.concatenate(
        [
            first_half * cosine_part - second_half * sine_part,
            second_half * cosine_part + first_half * sine_part,
        ],
        -1,
    )


def exchange_kernel(count, stride, modes, *refs):
    arrays = len(modes)
    ins, outs = refs[:arrays], refs[arrays : 2 * arrays]
    send_sem, recv_sem = refs[2 * arrays :]
    me = lax.axis_index("tp")
    grp = lax.axis_index("grp")
    mine = lax.rem(me // stride, count)
    base = me - mine * stride

    def member(step):
        return lax.rem(mine + step, count)

    barrier = pltpu.get_barrier_semaphore()
    for step in range(1, count):
        pl.semaphore_signal(
            barrier, inc=1, device_id=(grp, base + member(step) * stride), device_id_type=MESH
        )
    pl.semaphore_wait(barrier, count - 1)
    copies = []
    for index in range(arrays):
        for step in range(1, count):
            peer = member(step)
            source = ins[index] if modes[index] else ins[index].at[peer]
            copy = pltpu.make_async_remote_copy(
                src_ref=source,
                dst_ref=outs[index].at[mine],
                send_sem=send_sem.at[index, step],
                recv_sem=recv_sem.at[index, step],
                device_id=(grp, base + peer * stride),
                device_id_type=MESH,
            )
            copy.start()
            copies.append(copy)
        if modes[index]:
            outs[index][mine] = ins[index][...]
        else:
            outs[index][mine] = ins[index][mine]
    for copy in copies:
        copy.wait()


def tp_exchange(arrays, modes, collective_id, count=None, stride=1):
    count = lax.axis_size("tp") if count is None else count
    shapes = []
    for array, gather in zip(arrays, modes):
        block = array.shape if gather else array.shape[1:]
        shapes.append(jax.ShapeDtypeStruct((count,) + tuple(block), array.dtype))
    vmem = pl.BlockSpec(memory_space=pltpu.VMEM)
    return pl.pallas_call(
        functools.partial(exchange_kernel, count, stride, tuple(modes)),
        out_shape=tuple(shapes),
        in_specs=[vmem] * len(arrays),
        out_specs=tuple([vmem] * len(arrays)),
        scratch_shapes=[
            pltpu.SemaphoreType.DMA((len(arrays), count)),
            pltpu.SemaphoreType.DMA((len(arrays), count)),
        ],
        compiler_params=pltpu.CompilerParams(
            collective_id=collective_id, has_side_effects=True, vmem_limit_bytes=48 * 1024 * 1024
        ),
    )(*arrays)


def gather_kernel(arrays, *refs):
    ins, outs = refs[:arrays], refs[arrays : 2 * arrays]
    pair_send, pair_recv, ring_send, ring_recv, hop_send, hop_recv = refs[2 * arrays :]
    me = lax.axis_index("tp")
    grp = lax.axis_index("grp")
    ring = lax.axis_size("tp") // 2
    side = me % 2
    ring_at = me // 2
    partner = (grp, ring_at * 2 + 1 - side)

    def member(step):
        return (grp, lax.rem(ring_at + step, ring) * 2 + side)

    barrier = pltpu.get_barrier_semaphore()
    pl.semaphore_signal(barrier, inc=1, device_id=partner, device_id_type=MESH)
    for step in range(1, ring):
        pl.semaphore_signal(barrier, inc=1, device_id=member(step), device_id_type=MESH)
    pl.semaphore_wait(barrier, ring)
    pairs, direct = [], []
    for index in range(arrays):
        copy = pltpu.make_async_remote_copy(
            src_ref=ins[index],
            dst_ref=outs[index].at[ring_at, side],
            send_sem=pair_send.at[index],
            recv_sem=pair_recv.at[index],
            device_id=partner,
            device_id_type=MESH,
        )
        copy.start()
        pairs.append(copy)
        for step in range(1, ring):
            copy = pltpu.make_async_remote_copy(
                src_ref=ins[index],
                dst_ref=outs[index].at[ring_at, side],
                send_sem=ring_send.at[index, step],
                recv_sem=ring_recv.at[index, step],
                device_id=member(step),
                device_id_type=MESH,
            )
            copy.start()
            direct.append(copy)
        outs[index][ring_at, side] = ins[index][...]
    hops = []
    for index in range(arrays):
        pairs[index].wait_recv()
        for step in range(1, ring):
            copy = pltpu.make_async_remote_copy(
                src_ref=outs[index].at[ring_at, 1 - side],
                dst_ref=outs[index].at[ring_at, 1 - side],
                send_sem=hop_send.at[index, step],
                recv_sem=hop_recv.at[index, step],
                device_id=member(step),
                device_id_type=MESH,
            )
            copy.start()
            hops.append(copy)
    for copy in pairs:
        copy.wait_send()
    for copy in direct + hops:
        copy.wait()


def group_gather(arrays, collective_id):
    ring = lax.axis_size("tp") // 2
    count = len(arrays)
    shapes = [jax.ShapeDtypeStruct((ring, 2) + a.shape, a.dtype) for a in arrays]
    vmem = pl.BlockSpec(memory_space=pltpu.VMEM)
    return pl.pallas_call(
        functools.partial(gather_kernel, count),
        out_shape=tuple(shapes),
        in_specs=[vmem] * count,
        out_specs=tuple([vmem] * count),
        scratch_shapes=[
            pltpu.SemaphoreType.DMA((count,)),
            pltpu.SemaphoreType.DMA((count,)),
            pltpu.SemaphoreType.DMA((count, ring)),
            pltpu.SemaphoreType.DMA((count, ring)),
            pltpu.SemaphoreType.DMA((count, ring)),
            pltpu.SemaphoreType.DMA((count, ring)),
        ],
        compiler_params=pltpu.CompilerParams(
            collective_id=collective_id, has_side_effects=True, vmem_limit_bytes=48 * 1024 * 1024
        ),
    )(*arrays)


def attention_kernel(lo_ref, hi_ref, q_ref, cache_ref, mix_ref, peak_ref, total_ref):
    block = pl.program_id(0)
    kv_head = pl.program_id(1)
    lo = lo_ref[block]
    hi = hi_ref[block]
    heads, tokens, width = q_ref.shape
    key_col = pl.multiple_of(kv_head * HD, HD)
    value_col = pl.multiple_of((KVH + kv_head) * HD, HD)
    first = lo // CHUNK
    last = jnp.where(hi > lo, (hi + CHUNK - 1) // CHUNK, first)

    def one_head(head, carry):
        query = q_ref[head]

        def body(chunk, state):
            peak, total, mix = state
            start = pl.multiple_of(chunk * CHUNK, CHUNK)
            keys = cache_ref[pl.ds(start, CHUNK), pl.ds(key_col, HD)]
            values = cache_ref[pl.ds(start, CHUNK), pl.ds(value_col, HD)]
            rows = start + lax.broadcasted_iota(jnp.int32, (1, CHUNK), 1)
            bias = jnp.where((rows >= lo) & (rows < hi), 0.0, -jnp.inf)
            scores = lax.dot_general(
                query, keys, (((1,), (1,)), ((), ())), preferred_element_type=jnp.float32
            ) * (HD ** (-0.5)) + bias
            new_peak = jnp.maximum(peak, jnp.max(scores, axis=1, keepdims=True))
            scale = jnp.exp(peak - new_peak)
            weights = jnp.exp(scores - new_peak)
            total = scale * total + jnp.sum(weights, axis=1, keepdims=True)
            mix = scale * mix + jnp.dot(
                weights.astype(jnp.bfloat16), values, preferred_element_type=jnp.float32
            )
            return new_peak, total, mix

        start_state = (
            jnp.full((tokens, 1), NEG, jnp.float32),
            jnp.zeros((tokens, 1), jnp.float32),
            jnp.zeros((tokens, width), jnp.float32),
        )
        peak, total, mix = lax.fori_loop(first, last, body, start_state)
        mix_ref[head] = mix
        peak_ref[head] = peak
        total_ref[head] = total
        return carry

    lax.fori_loop(0, heads, one_head, 0)


def cache_attention(queries, cache_rows, lo, hi):
    heads, tokens, width = queries.shape
    blocks = tokens // C
    group_size = heads // KVH
    return pl.pallas_call(
        attention_kernel,
        out_shape=(
            jax.ShapeDtypeStruct((heads, tokens, width), jnp.float32),
            jax.ShapeDtypeStruct((heads, tokens, 1), jnp.float32),
            jax.ShapeDtypeStruct((heads, tokens, 1), jnp.float32),
        ),
        grid_spec=pltpu.PrefetchScalarGridSpec(
            num_scalar_prefetch=2,
            grid=(blocks, KVH),
            in_specs=[
                pl.BlockSpec((group_size, C, width), lambda b, j, lo, hi: (j, b, 0)),
                pl.BlockSpec(cache_rows.shape, lambda b, j, lo, hi: (0, 0)),
            ],
            out_specs=[
                pl.BlockSpec((group_size, C, width), lambda b, j, lo, hi: (j, b, 0)),
                pl.BlockSpec((group_size, C, 1), lambda b, j, lo, hi: (j, b, 0)),
                pl.BlockSpec((group_size, C, 1), lambda b, j, lo, hi: (j, b, 0)),
            ],
        ),
        compiler_params=pltpu.CompilerParams(vmem_limit_bytes=48 * 1024 * 1024),
    )(lo, hi, queries, cache_rows)


def join_partials(first, second):
    first_mix, first_peak, first_total = first
    second_mix, second_peak, second_total = second
    new_peak = jnp.maximum(first_peak, second_peak)
    first_scale = jnp.exp(first_peak - new_peak)
    second_scale = jnp.exp(second_peak - new_peak)
    joined_mix = first_mix * first_scale[..., None] + second_mix * second_scale[..., None]
    return (joined_mix, new_peak, first_total * first_scale + second_total * second_scale)


def to_partner(tree, flip_mask, groups):
    def branch(mask):
        pairs = [(i, i ^ mask) for i in range(groups)]
        return lambda t: jax.tree.map(lambda a: lax.ppermute(a, "grp", pairs), t)

    return lax.switch(flip_mask - 1, [branch(mask) for mask in range(1, groups)], tree)


def on_device(hidden, norm_gain, w_query, w_keyval, w_out, kv_cache, cache_len, partner):
    group_index = lax.axis_index("grp")
    tp_index = lax.axis_index("tp")
    tp_count = lax.axis_size("tp")
    groups = lax.axis_size("grp")
    ring = tp_count // 2
    ring_at = tp_index // 2
    side = tp_index % 2
    local_heads = QH // tp_count
    rows_here = kv_cache.shape[0]
    token_count = hidden.shape[0]
    model_width = w_out.shape[1]
    out_width = model_width // tp_count
    flip_mask = partner[0]

    float_rows = hidden.astype(jnp.float32)
    normed = (
        float_rows
        * lax.rsqrt(jnp.mean(float_rows * float_rows, -1, keepdims=True) + EPS)
        * norm_gain
    ).astype(jnp.bfloat16)
    query_raw = jnp.dot(normed, w_query, preferred_element_type=jnp.float32).reshape(
        token_count, local_heads, HD
    )
    keyval_part = jnp.dot(normed, w_keyval, preferred_element_type=jnp.float32).astype(jnp.bfloat16)
    lengths = lax.dynamic_slice_in_dim(cache_len, group_index * R, R)
    positions = (lengths[:, None] + jnp.arange(C, dtype=jnp.int32)[None, :]).reshape(token_count)
    query_local = rotate_pairs(query_raw, positions).astype(jnp.bfloat16).transpose(1, 0, 2)
    far_query = to_partner(query_local[:, :C], flip_mask, groups)
    query_ext = jnp.concatenate([query_local, far_query], 1)
    ext_tokens = query_ext.shape[1]
    query_got, keyval_got = group_gather([query_ext, keyval_part], 0)
    w_source, query_got = lax.optimization_barrier((w_out, query_got))
    def w_block(member):
        first = lax.dynamic_slice_in_dim(w_source, (2 * member + side) * out_width, out_width, 1)
        second = lax.dynamic_slice_in_dim(w_source, (2 * member + 1 - side) * out_width, out_width, 1)
        return jnp.concatenate([first, second], 1)

    w_received = [w_block(ring_at)]
    for step in range(1, ring):
        send = w_block(lax.rem(ring_at + step, ring))
        pairs = [(i, (i + 2 * step) % tp_count) for i in range(tp_count)]
        w_received.append(lax.ppermute(send, "tp", pairs))

    queries = query_got.reshape(QH, ext_tokens, HD)
    keyval_all = keyval_got.reshape(tp_count, token_count, -1).transpose(1, 0, 2).reshape(
        token_count, -1
    )

    stored_first = lengths[0] - lengths[0] // 2
    bound_one = stored_first
    bound_two = stored_first + lengths[1]
    far_count = cache_len[partner[group_index] * R] // 2
    starts = jnp.stack([0, bound_one, bound_two]).astype(jnp.int32)
    ends = jnp.stack([bound_one, bound_two, bound_two + far_count]).astype(jnp.int32)
    offset = tp_index * rows_here
    lo = jnp.clip(starts - offset, 0, rows_here)
    hi = jnp.clip(ends - offset, 0, rows_here)
    mix, peak, total = cache_attention(queries, kv_cache, lo, hi)
    mix_got, peak_got, total_got = tp_exchange(
        [
            mix.astype(jnp.bfloat16).reshape(tp_count, local_heads, ext_tokens, HD),
            peak.reshape(tp_count, local_heads, ext_tokens),
            total.reshape(tp_count, local_heads, ext_tokens),
        ],
        [False, False, False],
        2,
    )
    top = jnp.max(peak_got, 0)
    scales = jnp.exp(peak_got - top[None])
    mix_c = jnp.sum(mix_got.astype(jnp.float32) * scales[..., None], 0)
    total_c = jnp.sum(total_got * scales, 0)
    far_pack = jnp.concatenate(
        [
            mix_c[:, token_count:],
            top[:, None, token_count:],
            total_c[:, None, token_count:],
        ],
        1,
    )
    far_pack = to_partner(far_pack, flip_mask, groups)
    far_back = (far_pack[:, :C], far_pack[:, C], far_pack[:, C + 1])
    combined = (mix_c[:, :token_count], top[:, :token_count], total_c[:, :token_count])
    front = join_partials(tuple(piece[:, :C] for piece in combined), far_back)
    own = tuple(jnp.concatenate([front[i], combined[i][:, C:]], 1) for i in range(3))

    new_keys = rotate_pairs(
        keyval_all[:, : KVH * HD].astype(jnp.float32).reshape(token_count, KVH, HD), positions
    ).astype(jnp.bfloat16)
    new_values = keyval_all[:, KVH * HD :].reshape(token_count, KVH, HD)
    kv_head = (tp_index * local_heads) // (QH // KVH)
    key_rows = lax.dynamic_index_in_dim(new_keys, kv_head, 1, keepdims=False)
    value_rows = lax.dynamic_index_in_dim(new_values, kv_head, 1, keepdims=False)
    token_index = jnp.arange(token_count, dtype=jnp.int32)
    request_of = token_index // C
    within = token_index % C
    self_visible = (request_of[:, None] == request_of[None, :]) & (
        within[None, :] <= within[:, None]
    )
    self_scores = jnp.einsum(
        "htd,sd->hts", query_local, key_rows, preferred_element_type=jnp.float32
    ) * HD ** (-0.5)
    self_scores = jnp.where(self_visible[None], self_scores, -jnp.inf)
    self_peak = jnp.max(self_scores, -1)
    self_weights = jnp.exp(self_scores - self_peak[..., None])
    self_total = jnp.sum(self_weights, -1)
    self_mix = jnp.einsum(
        "hts,sd->htd", self_weights.astype(jnp.bfloat16), value_rows,
        preferred_element_type=jnp.float32,
    )
    final_mix, final_peak, final_total = join_partials(own, (self_mix, self_peak, self_total))
    attention = (final_mix / final_total[..., None]).astype(jnp.bfloat16)
    attention = attention.transpose(1, 0, 2).reshape(token_count, local_heads * HD)
    (attention_ring,) = tp_exchange([attention], [True], 3, ring, 2)
    sums = None
    for step in range(ring):
        source = lax.rem(ring_at - step + ring, ring)
        piece = jnp.dot(
            lax.dynamic_index_in_dim(attention_ring, source, 0, False),
            w_received[step],
            preferred_element_type=jnp.float32,
        )
        sums = piece if sums is None else sums + piece
    (other_got,) = tp_exchange([sums[:, out_width:].astype(jnp.bfloat16)], [True], 4, 2, 1)
    other = lax.dynamic_index_in_dim(other_got, 1 - side, 0, False)
    return (sums[:, :out_width] + other.astype(jnp.float32)).astype(jnp.bfloat16)


def solution(mesh):
    placed = (
        P("grp", None),
        P(),
        P(None, "tp"),
        P(None, "tp"),
        P("tp", None),
        P(("grp", "tp"), None),
        P(),
        P(),
    )
    return jax.shard_map(
        on_device, mesh=mesh, in_specs=placed, out_specs=P("grp", "tp"), check_vma=False
    )
```

```python
import functools

import jax
import jax.numpy as jnp
from jax import lax
from jax.experimental import pallas as pl
from jax.experimental.pallas import tpu as pltpu
from jax.sharding import PartitionSpec as P

HD = 128
QH = 16
KVH = 2
C = 128
R = 2

THETA = 5000000.0
EPS = 1e-05
NEG = -1e30
CHUNK = 256
MESH = pl.DeviceIdType.MESH


def rotate_pairs(values, positions):
    width = values.shape[-1]
    half_width = width // 2
    frequency = THETA ** (-2.0 * jnp.arange(half_width, dtype=jnp.float32) / width)
    angles = positions.astype(jnp.float32)[:, None] * frequency[None, :]
    cosine_part = jnp.cos(angles)[:, None, :]
    sine_part = jnp.sin(angles)[:, None, :]
    first_half = values[..., :half_width]
    second_half = values[..., half_width:]
    return jnp.concatenate(
        [
            first_half * cosine_part - second_half * sine_part,
            second_half * cosine_part + first_half * sine_part,
        ],
        -1,
    )


def exchange_kernel(count, stride, modes, *refs):
    arrays = len(modes)
    ins, outs = refs[:arrays], refs[arrays : 2 * arrays]
    send_sem, recv_sem = refs[2 * arrays :]
    me = lax.axis_index("tp")
    grp = lax.axis_index("grp")
    mine = lax.rem(me // stride, count)
    base = me - mine * stride

    def member(step):
        return lax.rem(mine + step, count)

    barrier = pltpu.get_barrier_semaphore()
    for step in range(1, count):
        pl.semaphore_signal(
            barrier, inc=1, device_id=(grp, base + member(step) * stride), device_id_type=MESH
        )
    pl.semaphore_wait(barrier, count - 1)
    copies = []
    for index in range(arrays):
        for step in range(1, count):
            peer = member(step)
            source = ins[index] if modes[index] else ins[index].at[peer]
            copy = pltpu.make_async_remote_copy(
                src_ref=source,
                dst_ref=outs[index].at[mine],
                send_sem=send_sem.at[index, step],
                recv_sem=recv_sem.at[index, step],
                device_id=(grp, base + peer * stride),
                device_id_type=MESH,
            )
            copy.start()
            copies.append(copy)
        if modes[index]:
            outs[index][mine] = ins[index][...]
        else:
            outs[index][mine] = ins[index][mine]
    for copy in copies:
        copy.wait()


def tp_exchange(arrays, modes, collective_id, count=None, stride=1):
    count = lax.axis_size("tp") if count is None else count
    shapes = []
    for array, gather in zip(arrays, modes):
        block = array.shape if gather else array.shape[1:]
        shapes.append(jax.ShapeDtypeStruct((count,) + tuple(block), array.dtype))
    vmem = pl.BlockSpec(memory_space=pltpu.VMEM)
    return pl.pallas_call(
        functools.partial(exchange_kernel, count, stride, tuple(modes)),
        out_shape=tuple(shapes),
        in_specs=[vmem] * len(arrays),
        out_specs=tuple([vmem] * len(arrays)),
        scratch_shapes=[
            pltpu.SemaphoreType.DMA((len(arrays), count)),
            pltpu.SemaphoreType.DMA((len(arrays), count)),
        ],
        compiler_params=pltpu.CompilerParams(
            collective_id=collective_id, has_side_effects=True, vmem_limit_bytes=48 * 1024 * 1024
        ),
    )(*arrays)


def gather_kernel(arrays, *refs):
    ins, outs = refs[:arrays], refs[arrays : 2 * arrays]
    pair_send, pair_recv, ring_send, ring_recv, hop_send, hop_recv = refs[2 * arrays :]
    me = lax.axis_index("tp")
    grp = lax.axis_index("grp")
    ring = lax.axis_size("tp") // 2
    side = me % 2
    ring_at = me // 2
    partner = (grp, ring_at * 2 + 1 - side)

    def member(step):
        return (grp, lax.rem(ring_at + step, ring) * 2 + side)

    barrier = pltpu.get_barrier_semaphore()
    pl.semaphore_signal(barrier, inc=1, device_id=partner, device_id_type=MESH)
    for step in range(1, ring):
        pl.semaphore_signal(barrier, inc=1, device_id=member(step), device_id_type=MESH)
    pl.semaphore_wait(barrier, ring)
    pairs, direct = [], []
    for index in range(arrays):
        copy = pltpu.make_async_remote_copy(
            src_ref=ins[index],
            dst_ref=outs[index].at[ring_at, side],
            send_sem=pair_send.at[index],
            recv_sem=pair_recv.at[index],
            device_id=partner,
            device_id_type=MESH,
        )
        copy.start()
        pairs.append(copy)
        for step in range(1, ring):
            copy = pltpu.make_async_remote_copy(
                src_ref=ins[index],
                dst_ref=outs[index].at[ring_at, side],
                send_sem=ring_send.at[index, step],
                recv_sem=ring_recv.at[index, step],
                device_id=member(step),
                device_id_type=MESH,
            )
            copy.start()
            direct.append(copy)
        outs[index][ring_at, side] = ins[index][...]
    hops = []
    for index in range(arrays):
        pairs[index].wait_recv()
        for step in range(1, ring):
            copy = pltpu.make_async_remote_copy(
                src_ref=outs[index].at[ring_at, 1 - side],
                dst_ref=outs[index].at[ring_at, 1 - side],
                send_sem=hop_send.at[index, step],
                recv_sem=hop_recv.at[index, step],
                device_id=member(step),
                device_id_type=MESH,
            )
            copy.start()
            hops.append(copy)
    for copy in pairs:
        copy.wait_send()
    for copy in direct + hops:
        copy.wait()


def group_gather(arrays, collective_id):
    ring = lax.axis_size("tp") // 2
    count = len(arrays)
    shapes = [jax.ShapeDtypeStruct((ring, 2) + a.shape, a.dtype) for a in arrays]
    vmem = pl.BlockSpec(memory_space=pltpu.VMEM)
    return pl.pallas_call(
        functools.partial(gather_kernel, count),
        out_shape=tuple(shapes),
        in_specs=[vmem] * count,
        out_specs=tuple([vmem] * count),
        scratch_shapes=[
            pltpu.SemaphoreType.DMA((count,)),
            pltpu.SemaphoreType.DMA((count,)),
            pltpu.SemaphoreType.DMA((count, ring)),
            pltpu.SemaphoreType.DMA((count, ring)),
            pltpu.SemaphoreType.DMA((count, ring)),
            pltpu.SemaphoreType.DMA((count, ring)),
        ],
        compiler_params=pltpu.CompilerParams(
            collective_id=collective_id, has_side_effects=True, vmem_limit_bytes=48 * 1024 * 1024
        ),
    )(*arrays)


def attention_kernel(lo_ref, hi_ref, q_ref, cache_ref, mix_ref, peak_ref, total_ref):
    block = pl.program_id(0)
    kv_head = pl.program_id(1)
    lo = lo_ref[block]
    hi = hi_ref[block]
    heads, tokens, width = q_ref.shape
    key_col = pl.multiple_of(kv_head * HD, HD)
    value_col = pl.multiple_of((KVH + kv_head) * HD, HD)
    first = lo // CHUNK
    last = jnp.where(hi > lo, (hi + CHUNK - 1) // CHUNK, first)

    def one_head(head, carry):
        query = q_ref[head]

        def body(chunk, state):
            peak, total, mix = state
            start = pl.multiple_of(chunk * CHUNK, CHUNK)
            keys = cache_ref[pl.ds(start, CHUNK), pl.ds(key_col, HD)]
            values = cache_ref[pl.ds(start, CHUNK), pl.ds(value_col, HD)]
            rows = start + lax.broadcasted_iota(jnp.int32, (1, CHUNK), 1)
            bias = jnp.where((rows >= lo) & (rows < hi), 0.0, -jnp.inf)
            scores = lax.dot_general(
                query, keys, (((1,), (1,)), ((), ())), preferred_element_type=jnp.float32
            ) * (HD ** (-0.5)) + bias
            new_peak = jnp.maximum(peak, jnp.max(scores, axis=1, keepdims=True))
            scale = jnp.exp(peak - new_peak)
            weights = jnp.exp(scores - new_peak)
            total = scale * total + jnp.sum(weights, axis=1, keepdims=True)
            mix = scale * mix + jnp.dot(
                weights.astype(jnp.bfloat16), values, preferred_element_type=jnp.float32
            )
            return new_peak, total, mix

        start_state = (
            jnp.full((tokens, 1), NEG, jnp.float32),
            jnp.zeros((tokens, 1), jnp.float32),
            jnp.zeros((tokens, width), jnp.float32),
        )
        peak, total, mix = lax.fori_loop(first, last, body, start_state)
        mix_ref[head] = mix
        peak_ref[head] = peak
        total_ref[head] = total
        return carry

    lax.fori_loop(0, heads, one_head, 0)


def cache_attention(queries, cache_rows, lo, hi):
    heads, tokens, width = queries.shape
    blocks = tokens // C
    group_size = heads // KVH
    return pl.pallas_call(
        attention_kernel,
        out_shape=(
            jax.ShapeDtypeStruct((heads, tokens, width), jnp.float32),
            jax.ShapeDtypeStruct((heads, tokens, 1), jnp.float32),
            jax.ShapeDtypeStruct((heads, tokens, 1), jnp.float32),
        ),
        grid_spec=pltpu.PrefetchScalarGridSpec(
            num_scalar_prefetch=2,
            grid=(blocks, KVH),
            in_specs=[
                pl.BlockSpec((group_size, C, width), lambda b, j, lo, hi: (j, b, 0)),
                pl.BlockSpec(cache_rows.shape, lambda b, j, lo, hi: (0, 0)),
            ],
            out_specs=[
                pl.BlockSpec((group_size, C, width), lambda b, j, lo, hi: (j, b, 0)),
                pl.BlockSpec((group_size, C, 1), lambda b, j, lo, hi: (j, b, 0)),
                pl.BlockSpec((group_size, C, 1), lambda b, j, lo, hi: (j, b, 0)),
            ],
        ),
        compiler_params=pltpu.CompilerParams(vmem_limit_bytes=48 * 1024 * 1024),
    )(lo, hi, queries, cache_rows)


def join_partials(first, second):
    first_mix, first_peak, first_total = first
    second_mix, second_peak, second_total = second
    new_peak = jnp.maximum(first_peak, second_peak)
    first_scale = jnp.exp(first_peak - new_peak)
    second_scale = jnp.exp(second_peak - new_peak)
    joined_mix = first_mix * first_scale[..., None] + second_mix * second_scale[..., None]
    return (joined_mix, new_peak, first_total * first_scale + second_total * second_scale)


def to_partner(tree, flip_mask, groups):
    def branch(mask):
        pairs = [(i, i ^ mask) for i in range(groups)]
        return lambda t: jax.tree.map(lambda a: lax.ppermute(a, "grp", pairs), t)

    low_count = 8
    low = lax.rem(flip_mask, low_count)
    high = flip_mask // low_count
    tree = lax.switch(low, [lambda t: t] + [branch(mask) for mask in range(1, low_count)], tree)
    high_masks = range(low_count, groups, low_count)
    return lax.switch(high, [lambda t: t] + [branch(mask) for mask in high_masks], tree)


def on_device(hidden, norm_gain, w_query, w_keyval, w_out, kv_cache, cache_len, partner):
    group_index = lax.axis_index("grp")
    tp_index = lax.axis_index("tp")
    tp_count = lax.axis_size("tp")
    groups = lax.axis_size("grp")
    ring = tp_count // 2
    ring_at = tp_index // 2
    side = tp_index % 2
    local_heads = QH // tp_count
    rows_here = kv_cache.shape[0]
    token_count = hidden.shape[0]
    model_width = w_out.shape[1]
    out_width = model_width // tp_count
    flip_mask = partner[0]

    def w_block(member):
        first = lax.dynamic_slice_in_dim(w_out, (2 * member + side) * out_width, out_width, 1)
        second = lax.dynamic_slice_in_dim(w_out, (2 * member + 1 - side) * out_width, out_width, 1)
        return jnp.concatenate([first, second], 1)

    w_received = [w_block(ring_at)]
    for step in range(1, ring):
        send = w_block(lax.rem(ring_at + step, ring))
        pairs = [(i, (i + 2 * step) % tp_count) for i in range(tp_count)]
        w_received.append(lax.ppermute(send, "tp", pairs))

    float_rows = hidden.astype(jnp.float32)
    normed = (
        float_rows
        * lax.rsqrt(jnp.mean(float_rows * float_rows, -1, keepdims=True) + EPS)
        * norm_gain
    ).astype(jnp.bfloat16)
    query_raw = jnp.dot(normed, w_query, preferred_element_type=jnp.float32).reshape(
        token_count, local_heads, HD
    )
    keyval_part = jnp.dot(normed, w_keyval, preferred_element_type=jnp.float32).astype(jnp.bfloat16)
    lengths = lax.dynamic_slice_in_dim(cache_len, group_index * R, R)
    positions = (lengths[:, None] + jnp.arange(C, dtype=jnp.int32)[None, :]).reshape(token_count)
    query_local = rotate_pairs(query_raw, positions).astype(jnp.bfloat16).transpose(1, 0, 2)
    far_query = to_partner(query_local[:, :C], flip_mask, groups)
    query_ext = jnp.concatenate([query_local, far_query], 1)
    ext_tokens = query_ext.shape[1]
    query_got, keyval_got = group_gather([query_ext, keyval_part], 0)
    queries = query_got.reshape(QH, ext_tokens, HD)
    keyval_all = keyval_got.reshape(tp_count, token_count, -1).transpose(1, 0, 2).reshape(
        token_count, -1
    )

    stored_first = lengths[0] - lengths[0] // 2
    bound_one = stored_first
    bound_two = stored_first + lengths[1]
    far_count = cache_len[partner[group_index] * R] // 2
    starts = jnp.stack([0, bound_one, bound_two]).astype(jnp.int32)
    ends = jnp.stack([bound_one, bound_two, bound_two + far_count]).astype(jnp.int32)
    offset = tp_index * rows_here
    lo = jnp.clip(starts - offset, 0, rows_here)
    hi = jnp.clip(ends - offset, 0, rows_here)
    mix, peak, total = cache_attention(queries, kv_cache, lo, hi)
    mix_got, peak_got, total_got = tp_exchange(
        [
            mix.astype(jnp.bfloat16).reshape(tp_count, local_heads, ext_tokens, HD),
            peak.reshape(tp_count, local_heads, ext_tokens),
            total.reshape(tp_count, local_heads, ext_tokens),
        ],
        [False, False, False],
        2,
    )
    top = jnp.max(peak_got, 0)
    scales = jnp.exp(peak_got - top[None])
    mix_c = jnp.sum(mix_got.astype(jnp.float32) * scales[..., None], 0)
    total_c = jnp.sum(total_got * scales, 0)
    far_pack = jnp.concatenate(
        [
            mix_c[:, token_count:],
            top[:, None, token_count:],
            total_c[:, None, token_count:],
        ],
        1,
    )
    far_pack = to_partner(far_pack, flip_mask, groups)
    far_back = (far_pack[:, :C], far_pack[:, C], far_pack[:, C + 1])
    combined = (mix_c[:, :token_count], top[:, :token_count], total_c[:, :token_count])
    front = join_partials(tuple(piece[:, :C] for piece in combined), far_back)
    own = tuple(jnp.concatenate([front[i], combined[i][:, C:]], 1) for i in range(3))

    new_keys = rotate_pairs(
        keyval_all[:, : KVH * HD].astype(jnp.float32).reshape(token_count, KVH, HD), positions
    ).astype(jnp.bfloat16)
    new_values = keyval_all[:, KVH * HD :].reshape(token_count, KVH, HD)
    kv_head = (tp_index * local_heads) // (QH // KVH)
    key_rows = lax.dynamic_index_in_dim(new_keys, kv_head, 1, keepdims=False)
    value_rows = lax.dynamic_index_in_dim(new_values, kv_head, 1, keepdims=False)
    token_index = jnp.arange(token_count, dtype=jnp.int32)
    request_of = token_index // C
    within = token_index % C
    self_visible = (request_of[:, None] == request_of[None, :]) & (
        within[None, :] <= within[:, None]
    )
    self_scores = jnp.einsum(
        "htd,sd->hts", query_local, key_rows, preferred_element_type=jnp.float32
    ) * HD ** (-0.5)
    self_scores = jnp.where(self_visible[None], self_scores, -jnp.inf)
    self_peak = jnp.max(self_scores, -1)
    self_weights = jnp.exp(self_scores - self_peak[..., None])
    self_total = jnp.sum(self_weights, -1)
    self_mix = jnp.einsum(
        "hts,sd->htd", self_weights.astype(jnp.bfloat16), value_rows,
        preferred_element_type=jnp.float32,
    )
    final_mix, final_peak, final_total = join_partials(own, (self_mix, self_peak, self_total))
    attention = (final_mix / final_total[..., None]).astype(jnp.bfloat16)
    attention = attention.transpose(1, 0, 2).reshape(token_count, local_heads * HD)
    (attention_ring,) = tp_exchange([attention], [True], 3, ring, 2)
    sums = None
    for step in range(ring):
        source = lax.rem(ring_at - step + ring, ring)
        piece = jnp.dot(
            lax.dynamic_index_in_dim(attention_ring, source, 0, False),
            w_received[step],
            preferred_element_type=jnp.float32,
        )
        sums = piece if sums is None else sums + piece
    (other_got,) = tp_exchange([sums[:, out_width:].astype(jnp.bfloat16)], [True], 4, 2, 1)
    other = lax.dynamic_index_in_dim(other_got, 1 - side, 0, False)
    return (sums[:, :out_width] + other.astype(jnp.float32)).astype(jnp.bfloat16)


def solution(mesh):
    placed = (
        P("grp", None),
        P(),
        P(None, "tp"),
        P(None, "tp"),
        P("tp", None),
        P(("grp", "tp"), None),
        P(),
        P(),
    )
    return jax.shard_map(
        on_device, mesh=mesh, in_specs=placed, out_specs=P("grp", "tp"), check_vma=False
    )
```

```python
import functools

import jax
import jax.numpy as jnp
from jax import lax
from jax.experimental import pallas as pl
from jax.experimental.pallas import tpu as pltpu
from jax.sharding import PartitionSpec as P

HD = 128
QH = 16
KVH = 2
C = 128
R = 2

THETA = 5000000.0
EPS = 1e-05
NEG = -1e30
CHUNK = 128
MESH = pl.DeviceIdType.MESH


def rotate_pairs(values, positions):
    width = values.shape[-1]
    half_width = width // 2
    frequency = THETA ** (-2.0 * jnp.arange(half_width, dtype=jnp.float32) / width)
    angles = positions.astype(jnp.float32)[:, None] * frequency[None, :]
    cosine_part = jnp.cos(angles)[:, None, :]
    sine_part = jnp.sin(angles)[:, None, :]
    first_half = values[..., :half_width]
    second_half = values[..., half_width:]
    return jnp.concatenate(
        [
            first_half * cosine_part - second_half * sine_part,
            second_half * cosine_part + first_half * sine_part,
        ],
        -1,
    )


def exchange_kernel(count, stride, modes, *refs):
    arrays = len(modes)
    ins, outs = refs[:arrays], refs[arrays : 2 * arrays]
    send_sem, recv_sem = refs[2 * arrays :]
    me = lax.axis_index("tp")
    grp = lax.axis_index("grp")
    mine = lax.rem(me // stride, count)
    base = me - mine * stride

    def member(step):
        return lax.rem(mine + step, count)

    barrier = pltpu.get_barrier_semaphore()
    for step in range(1, count):
        pl.semaphore_signal(
            barrier, inc=1, device_id=(grp, base + member(step) * stride), device_id_type=MESH
        )
    pl.semaphore_wait(barrier, count - 1)
    copies = []
    for index in range(arrays):
        for step in range(1, count):
            peer = member(step)
            source = ins[index] if modes[index] else ins[index].at[peer]
            copy = pltpu.make_async_remote_copy(
                src_ref=source,
                dst_ref=outs[index].at[mine],
                send_sem=send_sem.at[index, step],
                recv_sem=recv_sem.at[index, step],
                device_id=(grp, base + peer * stride),
                device_id_type=MESH,
            )
            copy.start()
            copies.append(copy)
        if modes[index]:
            outs[index][mine] = ins[index][...]
        else:
            outs[index][mine] = ins[index][mine]
    for copy in copies:
        copy.wait()


def tp_exchange(arrays, modes, collective_id, count=None, stride=1):
    count = lax.axis_size("tp") if count is None else count
    shapes = []
    for array, gather in zip(arrays, modes):
        block = array.shape if gather else array.shape[1:]
        shapes.append(jax.ShapeDtypeStruct((count,) + tuple(block), array.dtype))
    vmem = pl.BlockSpec(memory_space=pltpu.VMEM)
    return pl.pallas_call(
        functools.partial(exchange_kernel, count, stride, tuple(modes)),
        out_shape=tuple(shapes),
        in_specs=[vmem] * len(arrays),
        out_specs=tuple([vmem] * len(arrays)),
        scratch_shapes=[
            pltpu.SemaphoreType.DMA((len(arrays), count)),
            pltpu.SemaphoreType.DMA((len(arrays), count)),
        ],
        compiler_params=pltpu.CompilerParams(
            collective_id=collective_id, has_side_effects=True, vmem_limit_bytes=48 * 1024 * 1024
        ),
    )(*arrays)


def gather_kernel(arrays, *refs):
    ins, outs = refs[:arrays], refs[arrays : 2 * arrays]
    pair_send, pair_recv, ring_send, ring_recv, hop_send, hop_recv = refs[2 * arrays :]
    me = lax.axis_index("tp")
    grp = lax.axis_index("grp")
    ring = lax.axis_size("tp") // 2
    side = me % 2
    ring_at = me // 2
    partner = (grp, ring_at * 2 + 1 - side)

    def member(step):
        return (grp, lax.rem(ring_at + step, ring) * 2 + side)

    barrier = pltpu.get_barrier_semaphore()
    pl.semaphore_signal(barrier, inc=1, device_id=partner, device_id_type=MESH)
    for step in range(1, ring):
        pl.semaphore_signal(barrier, inc=1, device_id=member(step), device_id_type=MESH)
    pl.semaphore_wait(barrier, ring)
    pairs, direct = [], []
    for index in range(arrays):
        copy = pltpu.make_async_remote_copy(
            src_ref=ins[index],
            dst_ref=outs[index].at[ring_at, side],
            send_sem=pair_send.at[index],
            recv_sem=pair_recv.at[index],
            device_id=partner,
            device_id_type=MESH,
        )
        copy.start()
        pairs.append(copy)
        for step in range(1, ring):
            copy = pltpu.make_async_remote_copy(
                src_ref=ins[index],
                dst_ref=outs[index].at[ring_at, side],
                send_sem=ring_send.at[index, step],
                recv_sem=ring_recv.at[index, step],
                device_id=member(step),
                device_id_type=MESH,
            )
            copy.start()
            direct.append(copy)
        outs[index][ring_at, side] = ins[index][...]
    hops = []
    for index in range(arrays):
        pairs[index].wait_recv()
        for step in range(1, ring):
            copy = pltpu.make_async_remote_copy(
                src_ref=outs[index].at[ring_at, 1 - side],
                dst_ref=outs[index].at[ring_at, 1 - side],
                send_sem=hop_send.at[index, step],
                recv_sem=hop_recv.at[index, step],
                device_id=member(step),
                device_id_type=MESH,
            )
            copy.start()
            hops.append(copy)
    for copy in pairs:
        copy.wait_send()
    for copy in direct + hops:
        copy.wait()


def group_gather(arrays, collective_id):
    ring = lax.axis_size("tp") // 2
    count = len(arrays)
    shapes = [jax.ShapeDtypeStruct((ring, 2) + a.shape, a.dtype) for a in arrays]
    vmem = pl.BlockSpec(memory_space=pltpu.VMEM)
    return pl.pallas_call(
        functools.partial(gather_kernel, count),
        out_shape=tuple(shapes),
        in_specs=[vmem] * count,
        out_specs=tuple([vmem] * count),
        scratch_shapes=[
            pltpu.SemaphoreType.DMA((count,)),
            pltpu.SemaphoreType.DMA((count,)),
            pltpu.SemaphoreType.DMA((count, ring)),
            pltpu.SemaphoreType.DMA((count, ring)),
            pltpu.SemaphoreType.DMA((count, ring)),
            pltpu.SemaphoreType.DMA((count, ring)),
        ],
        compiler_params=pltpu.CompilerParams(
            collective_id=collective_id, has_side_effects=True, vmem_limit_bytes=48 * 1024 * 1024
        ),
    )(*arrays)


def attention_kernel(lo_ref, hi_ref, q_ref, cache_ref, mix_ref, peak_ref, total_ref):
    block = pl.program_id(0)
    kv_head = pl.program_id(1)
    lo = lo_ref[block]
    hi = hi_ref[block]
    heads, tokens, width = q_ref.shape
    key_col = pl.multiple_of(kv_head * HD, HD)
    value_col = pl.multiple_of((KVH + kv_head) * HD, HD)
    first = lo // CHUNK
    last = jnp.where(hi > lo, (hi + CHUNK - 1) // CHUNK, first)

    def one_head(head, carry):
        query = q_ref[head]

        def body(chunk, state):
            peak, total, mix = state
            start = pl.multiple_of(chunk * CHUNK, CHUNK)
            keys = cache_ref[pl.ds(start, CHUNK), pl.ds(key_col, HD)]
            values = cache_ref[pl.ds(start, CHUNK), pl.ds(value_col, HD)]
            rows = start + lax.broadcasted_iota(jnp.int32, (1, CHUNK), 1)
            bias = jnp.where((rows >= lo) & (rows < hi), 0.0, -jnp.inf)
            scores = lax.dot_general(
                query, keys, (((1,), (1,)), ((), ())), preferred_element_type=jnp.float32
            ) * (HD ** (-0.5)) + bias
            new_peak = jnp.maximum(peak, jnp.max(scores, axis=1, keepdims=True))
            scale = jnp.exp(peak - new_peak)
            weights = jnp.exp(scores - new_peak)
            total = scale * total + jnp.sum(weights, axis=1, keepdims=True)
            mix = scale * mix + jnp.dot(
                weights.astype(jnp.bfloat16), values, preferred_element_type=jnp.float32
            )
            return new_peak, total, mix

        start_state = (
            jnp.full((tokens, 1), NEG, jnp.float32),
            jnp.zeros((tokens, 1), jnp.float32),
            jnp.zeros((tokens, width), jnp.float32),
        )
        peak, total, mix = lax.fori_loop(first, last, body, start_state)
        mix_ref[head] = mix
        peak_ref[head] = peak
        total_ref[head] = total
        return carry

    lax.fori_loop(0, heads, one_head, 0)


def cache_attention(queries, cache_rows, lo, hi):
    heads, tokens, width = queries.shape
    blocks = tokens // C
    group_size = heads // KVH
    return pl.pallas_call(
        attention_kernel,
        out_shape=(
            jax.ShapeDtypeStruct((heads, tokens, width), jnp.float32),
            jax.ShapeDtypeStruct((heads, tokens, 1), jnp.float32),
            jax.ShapeDtypeStruct((heads, tokens, 1), jnp.float32),
        ),
        grid_spec=pltpu.PrefetchScalarGridSpec(
            num_scalar_prefetch=2,
            grid=(blocks, KVH),
            in_specs=[
                pl.BlockSpec((group_size, C, width), lambda b, j, lo, hi: (j, b, 0)),
                pl.BlockSpec(cache_rows.shape, lambda b, j, lo, hi: (0, 0)),
            ],
            out_specs=[
                pl.BlockSpec((group_size, C, width), lambda b, j, lo, hi: (j, b, 0)),
                pl.BlockSpec((group_size, C, 1), lambda b, j, lo, hi: (j, b, 0)),
                pl.BlockSpec((group_size, C, 1), lambda b, j, lo, hi: (j, b, 0)),
            ],
        ),
        compiler_params=pltpu.CompilerParams(vmem_limit_bytes=48 * 1024 * 1024),
    )(lo, hi, queries, cache_rows)


def join_partials(first, second):
    first_mix, first_peak, first_total = first
    second_mix, second_peak, second_total = second
    new_peak = jnp.maximum(first_peak, second_peak)
    first_scale = jnp.exp(first_peak - new_peak)
    second_scale = jnp.exp(second_peak - new_peak)
    joined_mix = first_mix * first_scale[..., None] + second_mix * second_scale[..., None]
    return (joined_mix, new_peak, first_total * first_scale + second_total * second_scale)


def to_partner(tree, flip_mask, groups):
    def branch(mask):
        pairs = [(i, i ^ mask) for i in range(groups)]
        return lambda t: jax.tree.map(lambda a: lax.ppermute(a, "grp", pairs), t)

    low_count = 8
    low = lax.rem(flip_mask, low_count)
    high = flip_mask // low_count
    tree = lax.switch(low, [lambda t: t] + [branch(mask) for mask in range(1, low_count)], tree)
    high_masks = range(low_count, groups, low_count)
    return lax.switch(high, [lambda t: t] + [branch(mask) for mask in high_masks], tree)


def on_device(hidden, norm_gain, w_query, w_keyval, w_out, kv_cache, cache_len, partner):
    group_index = lax.axis_index("grp")
    tp_index = lax.axis_index("tp")
    tp_count = lax.axis_size("tp")
    groups = lax.axis_size("grp")
    ring = tp_count // 2
    ring_at = tp_index // 2
    side = tp_index % 2
    local_heads = QH // tp_count
    rows_here = kv_cache.shape[0]
    token_count = hidden.shape[0]
    model_width = w_out.shape[1]
    out_width = model_width // tp_count
    flip_mask = partner[0]

    def w_block(member):
        first = lax.dynamic_slice_in_dim(w_out, (2 * member + side) * out_width, out_width, 1)
        second = lax.dynamic_slice_in_dim(w_out, (2 * member + 1 - side) * out_width, out_width, 1)
        return jnp.concatenate([first, second], 1)

    w_received = [w_block(ring_at)]
    for step in range(1, ring):
        send = w_block(lax.rem(ring_at + step, ring))
        pairs = [(i, (i + 2 * step) % tp_count) for i in range(tp_count)]
        w_received.append(lax.ppermute(send, "tp", pairs))

    float_rows = hidden.astype(jnp.float32)
    normed = (
        float_rows
        * lax.rsqrt(jnp.mean(float_rows * float_rows, -1, keepdims=True) + EPS)
        * norm_gain
    ).astype(jnp.bfloat16)
    query_raw = jnp.dot(normed, w_query, preferred_element_type=jnp.float32).reshape(
        token_count, local_heads, HD
    )
    keyval_part = jnp.dot(normed, w_keyval, preferred_element_type=jnp.float32).astype(jnp.bfloat16)
    lengths = lax.dynamic_slice_in_dim(cache_len, group_index * R, R)
    positions = (lengths[:, None] + jnp.arange(C, dtype=jnp.int32)[None, :]).reshape(token_count)
    query_local = rotate_pairs(query_raw, positions).astype(jnp.bfloat16).transpose(1, 0, 2)
    far_query = to_partner(query_local[:, :C], flip_mask, groups)
    query_ext = jnp.concatenate([query_local, far_query], 1)
    ext_tokens = query_ext.shape[1]
    query_got, keyval_got = group_gather([query_ext, keyval_part], 0)
    queries = query_got.reshape(QH, ext_tokens, HD)
    keyval_all = keyval_got.reshape(tp_count, token_count, -1).transpose(1, 0, 2).reshape(
        token_count, -1
    )

    stored_first = lengths[0] - lengths[0] // 2
    bound_one = stored_first
    bound_two = stored_first + lengths[1]
    far_count = cache_len[partner[group_index] * R] // 2
    starts = jnp.stack([0, bound_one, bound_two]).astype(jnp.int32)
    ends = jnp.stack([bound_one, bound_two, bound_two + far_count]).astype(jnp.int32)
    offset = tp_index * rows_here
    lo = jnp.clip(starts - offset, 0, rows_here)
    hi = jnp.clip(ends - offset, 0, rows_here)
    mix, peak, total = cache_attention(queries, kv_cache, lo, hi)
    mix_got, peak_got, total_got = tp_exchange(
        [
            mix.astype(jnp.bfloat16).reshape(tp_count, local_heads, ext_tokens, HD),
            peak.reshape(tp_count, local_heads, ext_tokens),
            total.reshape(tp_count, local_heads, ext_tokens),
        ],
        [False, False, False],
        2,
    )
    top = jnp.max(peak_got, 0)
    scales = jnp.exp(peak_got - top[None])
    mix_c = jnp.sum(mix_got.astype(jnp.float32) * scales[..., None], 0)
    total_c = jnp.sum(total_got * scales, 0)
    far_pack = jnp.concatenate(
        [
            mix_c[:, token_count:],
            top[:, None, token_count:],
            total_c[:, None, token_count:],
        ],
        1,
    )
    far_pack = to_partner(far_pack, flip_mask, groups)
    far_back = (far_pack[:, :C], far_pack[:, C], far_pack[:, C + 1])
    combined = (mix_c[:, :token_count], top[:, :token_count], total_c[:, :token_count])
    front = join_partials(tuple(piece[:, :C] for piece in combined), far_back)
    own = tuple(jnp.concatenate([front[i], combined[i][:, C:]], 1) for i in range(3))

    new_keys = rotate_pairs(
        keyval_all[:, : KVH * HD].astype(jnp.float32).reshape(token_count, KVH, HD), positions
    ).astype(jnp.bfloat16)
    new_values = keyval_all[:, KVH * HD :].reshape(token_count, KVH, HD)
    kv_head = (tp_index * local_heads) // (QH // KVH)
    key_rows = lax.dynamic_index_in_dim(new_keys, kv_head, 1, keepdims=False)
    value_rows = lax.dynamic_index_in_dim(new_values, kv_head, 1, keepdims=False)
    token_index = jnp.arange(token_count, dtype=jnp.int32)
    request_of = token_index // C
    within = token_index % C
    self_visible = (request_of[:, None] == request_of[None, :]) & (
        within[None, :] <= within[:, None]
    )
    self_scores = jnp.einsum(
        "htd,sd->hts", query_local, key_rows, preferred_element_type=jnp.float32
    ) * HD ** (-0.5)
    self_scores = jnp.where(self_visible[None], self_scores, -jnp.inf)
    self_peak = jnp.max(self_scores, -1)
    self_weights = jnp.exp(self_scores - self_peak[..., None])
    self_total = jnp.sum(self_weights, -1)
    self_mix = jnp.einsum(
        "hts,sd->htd", self_weights.astype(jnp.bfloat16), value_rows,
        preferred_element_type=jnp.float32,
    )
    final_mix, final_peak, final_total = join_partials(own, (self_mix, self_peak, self_total))
    attention = (final_mix / final_total[..., None]).astype(jnp.bfloat16)
    attention = attention.transpose(1, 0, 2).reshape(token_count, local_heads * HD)
    (attention_ring,) = tp_exchange([attention], [True], 3, ring, 2)
    sums = None
    for step in range(ring):
        source = lax.rem(ring_at - step + ring, ring)
        piece = jnp.dot(
            lax.dynamic_index_in_dim(attention_ring, source, 0, False),
            w_received[step],
            preferred_element_type=jnp.float32,
        )
        sums = piece if sums is None else sums + piece
    (other_got,) = tp_exchange([sums[:, out_width:].astype(jnp.bfloat16)], [True], 4, 2, 1)
    other = lax.dynamic_index_in_dim(other_got, 1 - side, 0, False)
    return (sums[:, :out_width] + other.astype(jnp.float32)).astype(jnp.bfloat16)


def solution(mesh):
    placed = (
        P("grp", None),
        P(),
        P(None, "tp"),
        P(None, "tp"),
        P("tp", None),
        P(("grp", "tp"), None),
        P(),
        P(),
    )
    return jax.shard_map(
        on_device, mesh=mesh, in_specs=placed, out_specs=P("grp", "tp"), check_vma=False
    )
```

```python
import functools

import jax
import jax.numpy as jnp
from jax import lax
from jax.experimental import pallas as pl
from jax.experimental.pallas import tpu as pltpu
from jax.sharding import PartitionSpec as P

HD = 128
QH = 16
KVH = 2
C = 128
R = 2

THETA = 5000000.0
EPS = 1e-05
NEG = -1e30
CHUNK = 640
MESH = pl.DeviceIdType.MESH


def rotate_pairs(values, positions):
    width = values.shape[-1]
    half_width = width // 2
    frequency = THETA ** (-2.0 * jnp.arange(half_width, dtype=jnp.float32) / width)
    angles = positions.astype(jnp.float32)[:, None] * frequency[None, :]
    cosine_part = jnp.cos(angles)[:, None, :]
    sine_part = jnp.sin(angles)[:, None, :]
    first_half = values[..., :half_width]
    second_half = values[..., half_width:]
    return jnp.concatenate(
        [
            first_half * cosine_part - second_half * sine_part,
            second_half * cosine_part + first_half * sine_part,
        ],
        -1,
    )


def exchange_kernel(count, stride, modes, *refs):
    arrays = len(modes)
    ins, outs = refs[:arrays], refs[arrays : 2 * arrays]
    send_sem, recv_sem = refs[2 * arrays :]
    me = lax.axis_index("tp")
    grp = lax.axis_index("grp")
    mine = lax.rem(me // stride, count)
    base = me - mine * stride

    def member(step):
        return lax.rem(mine + step, count)

    barrier = pltpu.get_barrier_semaphore()
    for step in range(1, count):
        pl.semaphore_signal(
            barrier, inc=1, device_id=(grp, base + member(step) * stride), device_id_type=MESH
        )
    pl.semaphore_wait(barrier, count - 1)
    copies = []
    for index in range(arrays):
        for step in range(1, count):
            peer = member(step)
            source = ins[index] if modes[index] else ins[index].at[peer]
            copy = pltpu.make_async_remote_copy(
                src_ref=source,
                dst_ref=outs[index].at[mine],
                send_sem=send_sem.at[index, step],
                recv_sem=recv_sem.at[index, step],
                device_id=(grp, base + peer * stride),
                device_id_type=MESH,
            )
            copy.start()
            copies.append(copy)
        if modes[index]:
            outs[index][mine] = ins[index][...]
        else:
            outs[index][mine] = ins[index][mine]
    for copy in copies:
        copy.wait()


def tp_exchange(arrays, modes, collective_id, count=None, stride=1):
    count = lax.axis_size("tp") if count is None else count
    shapes = []
    for array, gather in zip(arrays, modes):
        block = array.shape if gather else array.shape[1:]
        shapes.append(jax.ShapeDtypeStruct((count,) + tuple(block), array.dtype))
    vmem = pl.BlockSpec(memory_space=pltpu.VMEM)
    return pl.pallas_call(
        functools.partial(exchange_kernel, count, stride, tuple(modes)),
        out_shape=tuple(shapes),
        in_specs=[vmem] * len(arrays),
        out_specs=tuple([vmem] * len(arrays)),
        scratch_shapes=[
            pltpu.SemaphoreType.DMA((len(arrays), count)),
            pltpu.SemaphoreType.DMA((len(arrays), count)),
        ],
        compiler_params=pltpu.CompilerParams(
            collective_id=collective_id, has_side_effects=True, vmem_limit_bytes=48 * 1024 * 1024
        ),
    )(*arrays)


def gather_kernel(arrays, *refs):
    ins, outs = refs[:arrays], refs[arrays : 2 * arrays]
    pair_send, pair_recv, ring_send, ring_recv, hop_send, hop_recv = refs[2 * arrays :]
    me = lax.axis_index("tp")
    grp = lax.axis_index("grp")
    ring = lax.axis_size("tp") // 2
    side = me % 2
    ring_at = me // 2
    partner = (grp, ring_at * 2 + 1 - side)

    def member(step):
        return (grp, lax.rem(ring_at + step, ring) * 2 + side)

    barrier = pltpu.get_barrier_semaphore()
    pl.semaphore_signal(barrier, inc=1, device_id=partner, device_id_type=MESH)
    for step in range(1, ring):
        pl.semaphore_signal(barrier, inc=1, device_id=member(step), device_id_type=MESH)
    pl.semaphore_wait(barrier, ring)
    pairs, direct = [], []
    for index in range(arrays):
        copy = pltpu.make_async_remote_copy(
            src_ref=ins[index],
            dst_ref=outs[index].at[ring_at, side],
            send_sem=pair_send.at[index],
            recv_sem=pair_recv.at[index],
            device_id=partner,
            device_id_type=MESH,
        )
        copy.start()
        pairs.append(copy)
        for step in range(1, ring):
            copy = pltpu.make_async_remote_copy(
                src_ref=ins[index],
                dst_ref=outs[index].at[ring_at, side],
                send_sem=ring_send.at[index, step],
                recv_sem=ring_recv.at[index, step],
                device_id=member(step),
                device_id_type=MESH,
            )
            copy.start()
            direct.append(copy)
        outs[index][ring_at, side] = ins[index][...]
    hops = []
    for index in range(arrays):
        pairs[index].wait_recv()
        for step in range(1, ring):
            copy = pltpu.make_async_remote_copy(
                src_ref=outs[index].at[ring_at, 1 - side],
                dst_ref=outs[index].at[ring_at, 1 - side],
                send_sem=hop_send.at[index, step],
                recv_sem=hop_recv.at[index, step],
                device_id=member(step),
                device_id_type=MESH,
            )
            copy.start()
            hops.append(copy)
    for copy in pairs:
        copy.wait_send()
    for copy in direct + hops:
        copy.wait()


def group_gather(arrays, collective_id):
    ring = lax.axis_size("tp") // 2
    count = len(arrays)
    shapes = [jax.ShapeDtypeStruct((ring, 2) + a.shape, a.dtype) for a in arrays]
    vmem = pl.BlockSpec(memory_space=pltpu.VMEM)
    return pl.pallas_call(
        functools.partial(gather_kernel, count),
        out_shape=tuple(shapes),
        in_specs=[vmem] * count,
        out_specs=tuple([vmem] * count),
        scratch_shapes=[
            pltpu.SemaphoreType.DMA((count,)),
            pltpu.SemaphoreType.DMA((count,)),
            pltpu.SemaphoreType.DMA((count, ring)),
            pltpu.SemaphoreType.DMA((count, ring)),
            pltpu.SemaphoreType.DMA((count, ring)),
            pltpu.SemaphoreType.DMA((count, ring)),
        ],
        compiler_params=pltpu.CompilerParams(
            collective_id=collective_id, has_side_effects=True, vmem_limit_bytes=48 * 1024 * 1024
        ),
    )(*arrays)


def attention_kernel(lo_ref, hi_ref, q_ref, cache_ref, mix_ref, peak_ref, total_ref):
    block = pl.program_id(0)
    kv_head = pl.program_id(1)
    lo = lo_ref[block]
    hi = hi_ref[block]
    heads, tokens, width = q_ref.shape
    key_col = pl.multiple_of(kv_head * HD, HD)
    value_col = pl.multiple_of((KVH + kv_head) * HD, HD)
    first = lo // CHUNK
    last = jnp.where(hi > lo, (hi + CHUNK - 1) // CHUNK, first)

    def one_head(head, carry):
        query = q_ref[head]

        def body(chunk, state):
            peak, total, mix = state
            start = pl.multiple_of(chunk * CHUNK, CHUNK)
            keys = cache_ref[pl.ds(start, CHUNK), pl.ds(key_col, HD)]
            values = cache_ref[pl.ds(start, CHUNK), pl.ds(value_col, HD)]
            rows = start + lax.broadcasted_iota(jnp.int32, (1, CHUNK), 1)
            bias = jnp.where((rows >= lo) & (rows < hi), 0.0, -jnp.inf)
            scores = lax.dot_general(
                query, keys, (((1,), (1,)), ((), ())), preferred_element_type=jnp.float32
            ) * (HD ** (-0.5)) + bias
            new_peak = jnp.maximum(peak, jnp.max(scores, axis=1, keepdims=True))
            scale = jnp.exp(peak - new_peak)
            weights = jnp.exp(scores - new_peak)
            total = scale * total + jnp.sum(weights, axis=1, keepdims=True)
            mix = scale * mix + jnp.dot(
                weights.astype(jnp.bfloat16), values, preferred_element_type=jnp.float32
            )
            return new_peak, total, mix

        start_state = (
            jnp.full((tokens, 1), NEG, jnp.float32),
            jnp.zeros((tokens, 1), jnp.float32),
            jnp.zeros((tokens, width), jnp.float32),
        )
        peak, total, mix = lax.fori_loop(first, last, body, start_state)
        mix_ref[head] = mix
        peak_ref[head] = peak
        total_ref[head] = total
        return carry

    lax.fori_loop(0, heads, one_head, 0)


def cache_attention(queries, cache_rows, lo, hi):
    heads, tokens, width = queries.shape
    blocks = tokens // C
    group_size = heads // KVH
    return pl.pallas_call(
        attention_kernel,
        out_shape=(
            jax.ShapeDtypeStruct((heads, tokens, width), jnp.float32),
            jax.ShapeDtypeStruct((heads, tokens, 1), jnp.float32),
            jax.ShapeDtypeStruct((heads, tokens, 1), jnp.float32),
        ),
        grid_spec=pltpu.PrefetchScalarGridSpec(
            num_scalar_prefetch=2,
            grid=(blocks, KVH),
            in_specs=[
                pl.BlockSpec((group_size, C, width), lambda b, j, lo, hi: (j, b, 0)),
                pl.BlockSpec(cache_rows.shape, lambda b, j, lo, hi: (0, 0)),
            ],
            out_specs=[
                pl.BlockSpec((group_size, C, width), lambda b, j, lo, hi: (j, b, 0)),
                pl.BlockSpec((group_size, C, 1), lambda b, j, lo, hi: (j, b, 0)),
                pl.BlockSpec((group_size, C, 1), lambda b, j, lo, hi: (j, b, 0)),
            ],
        ),
        compiler_params=pltpu.CompilerParams(vmem_limit_bytes=48 * 1024 * 1024),
    )(lo, hi, queries, cache_rows)


def join_partials(first, second):
    first_mix, first_peak, first_total = first
    second_mix, second_peak, second_total = second
    new_peak = jnp.maximum(first_peak, second_peak)
    first_scale = jnp.exp(first_peak - new_peak)
    second_scale = jnp.exp(second_peak - new_peak)
    joined_mix = first_mix * first_scale[..., None] + second_mix * second_scale[..., None]
    return (joined_mix, new_peak, first_total * first_scale + second_total * second_scale)


def to_partner(tree, flip_mask, groups):
    def branch(mask):
        pairs = [(i, i ^ mask) for i in range(groups)]
        return lambda t: jax.tree.map(lambda a: lax.ppermute(a, "grp", pairs), t)

    low_count = 8
    low = lax.rem(flip_mask, low_count)
    high = flip_mask // low_count
    tree = lax.switch(low, [lambda t: t] + [branch(mask) for mask in range(1, low_count)], tree)
    high_masks = range(low_count, groups, low_count)
    return lax.switch(high, [lambda t: t] + [branch(mask) for mask in high_masks], tree)


def on_device(hidden, norm_gain, w_query, w_keyval, w_out, kv_cache, cache_len, partner):
    group_index = lax.axis_index("grp")
    tp_index = lax.axis_index("tp")
    tp_count = lax.axis_size("tp")
    groups = lax.axis_size("grp")
    ring = tp_count // 2
    ring_at = tp_index // 2
    side = tp_index % 2
    local_heads = QH // tp_count
    rows_here = kv_cache.shape[0]
    token_count = hidden.shape[0]
    model_width = w_out.shape[1]
    out_width = model_width // tp_count
    flip_mask = partner[0]

    def w_block(member):
        first = lax.dynamic_slice_in_dim(w_out, (2 * member + side) * out_width, out_width, 1)
        second = lax.dynamic_slice_in_dim(w_out, (2 * member + 1 - side) * out_width, out_width, 1)
        return jnp.concatenate([first, second], 1)

    w_received = [w_block(ring_at)]
    for step in range(1, ring):
        send = w_block(lax.rem(ring_at + step, ring))
        pairs = [(i, (i + 2 * step) % tp_count) for i in range(tp_count)]
        w_received.append(lax.ppermute(send, "tp", pairs))

    float_rows = hidden.astype(jnp.float32)
    normed = (
        float_rows
        * lax.rsqrt(jnp.mean(float_rows * float_rows, -1, keepdims=True) + EPS)
        * norm_gain
    ).astype(jnp.bfloat16)
    query_raw = jnp.dot(normed, w_query, preferred_element_type=jnp.float32).reshape(
        token_count, local_heads, HD
    )
    keyval_part = jnp.dot(normed, w_keyval, preferred_element_type=jnp.float32).astype(jnp.bfloat16)
    lengths = lax.dynamic_slice_in_dim(cache_len, group_index * R, R)
    positions = (lengths[:, None] + jnp.arange(C, dtype=jnp.int32)[None, :]).reshape(token_count)
    query_local = rotate_pairs(query_raw, positions).astype(jnp.bfloat16).transpose(1, 0, 2)
    far_query = to_partner(query_local[:, :C], flip_mask, groups)
    query_ext = jnp.concatenate([query_local, far_query], 1)
    ext_tokens = query_ext.shape[1]
    query_got, keyval_got = group_gather([query_ext, keyval_part], 0)
    queries = query_got.reshape(QH, ext_tokens, HD)
    keyval_all = keyval_got.reshape(tp_count, token_count, -1).transpose(1, 0, 2).reshape(
        token_count, -1
    )

    stored_first = lengths[0] - lengths[0] // 2
    bound_one = stored_first
    bound_two = stored_first + lengths[1]
    far_count = cache_len[partner[group_index] * R] // 2
    starts = jnp.stack([0, bound_one, bound_two]).astype(jnp.int32)
    ends = jnp.stack([bound_one, bound_two, bound_two + far_count]).astype(jnp.int32)
    offset = tp_index * rows_here
    lo = jnp.clip(starts - offset, 0, rows_here)
    hi = jnp.clip(ends - offset, 0, rows_here)
    mix, peak, total = cache_attention(queries, kv_cache, lo, hi)
    mix_got, peak_got, total_got = tp_exchange(
        [
            mix.astype(jnp.bfloat16).reshape(tp_count, local_heads, ext_tokens, HD),
            peak.reshape(tp_count, local_heads, ext_tokens),
            total.reshape(tp_count, local_heads, ext_tokens),
        ],
        [False, False, False],
        2,
    )
    top = jnp.max(peak_got, 0)
    scales = jnp.exp(peak_got - top[None])
    mix_c = jnp.sum(mix_got.astype(jnp.float32) * scales[..., None], 0)
    total_c = jnp.sum(total_got * scales, 0)
    far_pack = jnp.concatenate(
        [
            mix_c[:, token_count:],
            top[:, None, token_count:],
            total_c[:, None, token_count:],
        ],
        1,
    )
    far_pack = to_partner(far_pack, flip_mask, groups)
    far_back = (far_pack[:, :C], far_pack[:, C], far_pack[:, C + 1])
    combined = (mix_c[:, :token_count], top[:, :token_count], total_c[:, :token_count])
    front = join_partials(tuple(piece[:, :C] for piece in combined), far_back)
    own = tuple(jnp.concatenate([front[i], combined[i][:, C:]], 1) for i in range(3))

    new_keys = rotate_pairs(
        keyval_all[:, : KVH * HD].astype(jnp.float32).reshape(token_count, KVH, HD), positions
    ).astype(jnp.bfloat16)
    new_values = keyval_all[:, KVH * HD :].reshape(token_count, KVH, HD)
    kv_head = (tp_index * local_heads) // (QH // KVH)
    key_rows = lax.dynamic_index_in_dim(new_keys, kv_head, 1, keepdims=False)
    value_rows = lax.dynamic_index_in_dim(new_values, kv_head, 1, keepdims=False)
    token_index = jnp.arange(token_count, dtype=jnp.int32)
    request_of = token_index // C
    within = token_index % C
    self_visible = (request_of[:, None] == request_of[None, :]) & (
        within[None, :] <= within[:, None]
    )
    self_scores = jnp.einsum(
        "htd,sd->hts", query_local, key_rows, preferred_element_type=jnp.float32
    ) * HD ** (-0.5)
    self_scores = jnp.where(self_visible[None], self_scores, -jnp.inf)
    self_peak = jnp.max(self_scores, -1)
    self_weights = jnp.exp(self_scores - self_peak[..., None])
    self_total = jnp.sum(self_weights, -1)
    self_mix = jnp.einsum(
        "hts,sd->htd", self_weights.astype(jnp.bfloat16), value_rows,
        preferred_element_type=jnp.float32,
    )
    final_mix, final_peak, final_total = join_partials(own, (self_mix, self_peak, self_total))
    attention = (final_mix / final_total[..., None]).astype(jnp.bfloat16)
    attention = attention.transpose(1, 0, 2).reshape(token_count, local_heads * HD)
    (attention_ring,) = tp_exchange([attention], [True], 3, ring, 2)
    sums = None
    for step in range(ring):
        source = lax.rem(ring_at - step + ring, ring)
        piece = jnp.dot(
            lax.dynamic_index_in_dim(attention_ring, source, 0, False),
            w_received[step],
            preferred_element_type=jnp.float32,
        )
        sums = piece if sums is None else sums + piece
    (other_got,) = tp_exchange([sums[:, out_width:].astype(jnp.bfloat16)], [True], 4, 2, 1)
    other = lax.dynamic_index_in_dim(other_got, 1 - side, 0, False)
    return (sums[:, :out_width] + other.astype(jnp.float32)).astype(jnp.bfloat16)


def solution(mesh):
    placed = (
        P("grp", None),
        P(),
        P(None, "tp"),
        P(None, "tp"),
        P("tp", None),
        P(("grp", "tp"), None),
        P(),
        P(),
    )
    return jax.shard_map(
        on_device, mesh=mesh, in_specs=placed, out_specs=P("grp", "tp"), check_vma=False
    )
```

```python
import functools

import jax
import jax.numpy as jnp
from jax import lax
from jax.experimental import pallas as pl
from jax.experimental.pallas import tpu as pltpu
from jax.sharding import PartitionSpec as P

HD = 128
QH = 16
KVH = 2
C = 128
R = 2

THETA = 5000000.0
EPS = 1e-05
NEG = -1e30
CHUNK = 640
MESH = pl.DeviceIdType.MESH


def rotate_pairs(values, positions):
    width = values.shape[-1]
    half_width = width // 2
    frequency = THETA ** (-2.0 * jnp.arange(half_width, dtype=jnp.float32) / width)
    angles = positions.astype(jnp.float32)[:, None] * frequency[None, :]
    cosine_part = jnp.cos(angles)[:, None, :]
    sine_part = jnp.sin(angles)[:, None, :]
    first_half = values[..., :half_width]
    second_half = values[..., half_width:]
    return jnp.concatenate(
        [
            first_half * cosine_part - second_half * sine_part,
            second_half * cosine_part + first_half * sine_part,
        ],
        -1,
    )


def exchange_kernel(count, stride, modes, *refs):
    arrays = len(modes)
    ins, outs = refs[:arrays], refs[arrays : 2 * arrays]
    send_sem, recv_sem = refs[2 * arrays :]
    me = lax.axis_index("tp")
    grp = lax.axis_index("grp")
    mine = lax.rem(me // stride, count)
    base = me - mine * stride

    def member(step):
        return lax.rem(mine + step, count)

    barrier = pltpu.get_barrier_semaphore()
    for step in range(1, count):
        pl.semaphore_signal(
            barrier, inc=1, device_id=(grp, base + member(step) * stride), device_id_type=MESH
        )
    pl.semaphore_wait(barrier, count - 1)
    copies = []
    for index in range(arrays):
        for step in range(1, count):
            peer = member(step)
            source = ins[index] if modes[index] else ins[index].at[peer]
            copy = pltpu.make_async_remote_copy(
                src_ref=source,
                dst_ref=outs[index].at[mine],
                send_sem=send_sem.at[index, step],
                recv_sem=recv_sem.at[index, step],
                device_id=(grp, base + peer * stride),
                device_id_type=MESH,
            )
            copy.start()
            copies.append(copy)
        if modes[index]:
            outs[index][mine] = ins[index][...]
        else:
            outs[index][mine] = ins[index][mine]
    for copy in copies:
        copy.wait()


def tp_exchange(arrays, modes, collective_id, count=None, stride=1):
    count = lax.axis_size("tp") if count is None else count
    shapes = []
    for array, gather in zip(arrays, modes):
        block = array.shape if gather else array.shape[1:]
        shapes.append(jax.ShapeDtypeStruct((count,) + tuple(block), array.dtype))
    vmem = pl.BlockSpec(memory_space=pltpu.VMEM)
    return pl.pallas_call(
        functools.partial(exchange_kernel, count, stride, tuple(modes)),
        out_shape=tuple(shapes),
        in_specs=[vmem] * len(arrays),
        out_specs=tuple([vmem] * len(arrays)),
        scratch_shapes=[
            pltpu.SemaphoreType.DMA((len(arrays), count)),
            pltpu.SemaphoreType.DMA((len(arrays), count)),
        ],
        compiler_params=pltpu.CompilerParams(
            collective_id=collective_id, has_side_effects=True, vmem_limit_bytes=48 * 1024 * 1024
        ),
    )(*arrays)


def gather_kernel(arrays, *refs):
    ins, outs = refs[:arrays], refs[arrays : 2 * arrays]
    pair_send, pair_recv, ring_send, ring_recv, hop_send, hop_recv = refs[2 * arrays :]
    me = lax.axis_index("tp")
    grp = lax.axis_index("grp")
    ring = lax.axis_size("tp") // 2
    side = me % 2
    ring_at = me // 2
    partner = (grp, ring_at * 2 + 1 - side)

    def member(step):
        return (grp, lax.rem(ring_at + step, ring) * 2 + side)

    barrier = pltpu.get_barrier_semaphore()
    pl.semaphore_signal(barrier, inc=1, device_id=partner, device_id_type=MESH)
    for step in range(1, ring):
        pl.semaphore_signal(barrier, inc=1, device_id=member(step), device_id_type=MESH)
    pl.semaphore_wait(barrier, ring)
    pairs, direct = [], []
    for index in range(arrays):
        copy = pltpu.make_async_remote_copy(
            src_ref=ins[index],
            dst_ref=outs[index].at[ring_at, side],
            send_sem=pair_send.at[index],
            recv_sem=pair_recv.at[index],
            device_id=partner,
            device_id_type=MESH,
        )
        copy.start()
        pairs.append(copy)
        for step in range(1, ring):
            copy = pltpu.make_async_remote_copy(
                src_ref=ins[index],
                dst_ref=outs[index].at[ring_at, side],
                send_sem=ring_send.at[index, step],
                recv_sem=ring_recv.at[index, step],
                device_id=member(step),
                device_id_type=MESH,
            )
            copy.start()
            direct.append(copy)
        outs[index][ring_at, side] = ins[index][...]
    hops = []
    for index in range(arrays):
        pairs[index].wait_recv()
        for step in range(1, ring):
            copy = pltpu.make_async_remote_copy(
                src_ref=outs[index].at[ring_at, 1 - side],
                dst_ref=outs[index].at[ring_at, 1 - side],
                send_sem=hop_send.at[index, step],
                recv_sem=hop_recv.at[index, step],
                device_id=member(step),
                device_id_type=MESH,
            )
            copy.start()
            hops.append(copy)
    for copy in pairs:
        copy.wait_send()
    for copy in direct + hops:
        copy.wait()


def group_gather(arrays, collective_id):
    ring = lax.axis_size("tp") // 2
    count = len(arrays)
    shapes = [jax.ShapeDtypeStruct((ring, 2) + a.shape, a.dtype) for a in arrays]
    vmem = pl.BlockSpec(memory_space=pltpu.VMEM)
    return pl.pallas_call(
        functools.partial(gather_kernel, count),
        out_shape=tuple(shapes),
        in_specs=[vmem] * count,
        out_specs=tuple([vmem] * count),
        scratch_shapes=[
            pltpu.SemaphoreType.DMA((count,)),
            pltpu.SemaphoreType.DMA((count,)),
            pltpu.SemaphoreType.DMA((count, ring)),
            pltpu.SemaphoreType.DMA((count, ring)),
            pltpu.SemaphoreType.DMA((count, ring)),
            pltpu.SemaphoreType.DMA((count, ring)),
        ],
        compiler_params=pltpu.CompilerParams(
            collective_id=collective_id, has_side_effects=True, vmem_limit_bytes=48 * 1024 * 1024
        ),
    )(*arrays)


def attention_kernel(lo_ref, hi_ref, q_ref, cache_ref, mix_ref, peak_ref, total_ref, keys_t):
    block = pl.program_id(0)
    kv_head = pl.program_id(1)
    lo = lo_ref[block]
    hi = hi_ref[block]
    heads, tokens, width = q_ref.shape
    key_col = pl.multiple_of(kv_head * HD, HD)
    value_col = pl.multiple_of((KVH + kv_head) * HD, HD)
    first = lo // CHUNK
    last = jnp.where(hi > lo, (hi + CHUNK - 1) // CHUNK, first)
    keys_t[...] = cache_ref[:, pl.ds(key_col, HD)].astype(jnp.float32).T.astype(jnp.bfloat16)

    def one_head(head, carry):
        query = q_ref[head]

        def body(chunk, state):
            peak, total, mix = state
            start = pl.multiple_of(chunk * CHUNK, CHUNK)
            values = cache_ref[pl.ds(start, CHUNK), pl.ds(value_col, HD)]
            rows = start + lax.broadcasted_iota(jnp.int32, (1, CHUNK), 1)
            bias = jnp.where((rows >= lo) & (rows < hi), 0.0, -jnp.inf)
            scores = jnp.dot(
                query, keys_t[:, pl.ds(start, CHUNK)], preferred_element_type=jnp.float32
            ) * (HD ** (-0.5)) + bias
            new_peak = jnp.maximum(peak, jnp.max(scores, axis=1, keepdims=True))
            scale = jnp.exp(peak - new_peak)
            weights = jnp.exp(scores - new_peak)
            total = scale * total + jnp.sum(weights, axis=1, keepdims=True)
            mix = scale * mix + jnp.dot(
                weights.astype(jnp.bfloat16), values, preferred_element_type=jnp.float32
            )
            return new_peak, total, mix

        start_state = (
            jnp.full((tokens, 1), NEG, jnp.float32),
            jnp.zeros((tokens, 1), jnp.float32),
            jnp.zeros((tokens, width), jnp.float32),
        )
        peak, total, mix = lax.fori_loop(first, last, body, start_state)
        mix_ref[head] = mix
        peak_ref[head] = peak
        total_ref[head] = total
        return carry

    lax.fori_loop(0, heads, one_head, 0)


def cache_attention(queries, cache_rows, lo, hi):
    heads, tokens, width = queries.shape
    blocks = tokens // C
    group_size = heads // KVH
    return pl.pallas_call(
        attention_kernel,
        out_shape=(
            jax.ShapeDtypeStruct((heads, tokens, width), jnp.float32),
            jax.ShapeDtypeStruct((heads, tokens, 1), jnp.float32),
            jax.ShapeDtypeStruct((heads, tokens, 1), jnp.float32),
        ),
        grid_spec=pltpu.PrefetchScalarGridSpec(
            num_scalar_prefetch=2,
            grid=(blocks, KVH),
            in_specs=[
                pl.BlockSpec((group_size, C, width), lambda b, j, lo, hi: (j, b, 0)),
                pl.BlockSpec(cache_rows.shape, lambda b, j, lo, hi: (0, 0)),
            ],
            out_specs=[
                pl.BlockSpec((group_size, C, width), lambda b, j, lo, hi: (j, b, 0)),
                pl.BlockSpec((group_size, C, 1), lambda b, j, lo, hi: (j, b, 0)),
                pl.BlockSpec((group_size, C, 1), lambda b, j, lo, hi: (j, b, 0)),
            ],
            scratch_shapes=[pltpu.VMEM((width, cache_rows.shape[0]), jnp.bfloat16)],
        ),
        compiler_params=pltpu.CompilerParams(vmem_limit_bytes=48 * 1024 * 1024),
    )(lo, hi, queries, cache_rows)


def join_partials(first, second):
    first_mix, first_peak, first_total = first
    second_mix, second_peak, second_total = second
    new_peak = jnp.maximum(first_peak, second_peak)
    first_scale = jnp.exp(first_peak - new_peak)
    second_scale = jnp.exp(second_peak - new_peak)
    joined_mix = first_mix * first_scale[..., None] + second_mix * second_scale[..., None]
    return (joined_mix, new_peak, first_total * first_scale + second_total * second_scale)


def to_partner(tree, flip_mask, groups):
    def branch(mask):
        pairs = [(i, i ^ mask) for i in range(groups)]
        return lambda t: jax.tree.map(lambda a: lax.ppermute(a, "grp", pairs), t)

    low_count = 8
    low = lax.rem(flip_mask, low_count)
    high = flip_mask // low_count
    tree = lax.switch(low, [lambda t: t] + [branch(mask) for mask in range(1, low_count)], tree)
    high_masks = range(low_count, groups, low_count)
    return lax.switch(high, [lambda t: t] + [branch(mask) for mask in high_masks], tree)


def on_device(hidden, norm_gain, w_query, w_keyval, w_out, kv_cache, cache_len, partner):
    group_index = lax.axis_index("grp")
    tp_index = lax.axis_index("tp")
    tp_count = lax.axis_size("tp")
    groups = lax.axis_size("grp")
    ring = tp_count // 2
    ring_at = tp_index // 2
    side = tp_index % 2
    local_heads = QH // tp_count
    rows_here = kv_cache.shape[0]
    token_count = hidden.shape[0]
    model_width = w_out.shape[1]
    out_width = model_width // tp_count
    flip_mask = partner[0]

    def w_block(member):
        first = lax.dynamic_slice_in_dim(w_out, (2 * member + side) * out_width, out_width, 1)
        second = lax.dynamic_slice_in_dim(w_out, (2 * member + 1 - side) * out_width, out_width, 1)
        return jnp.concatenate([first, second], 1)

    w_received = [w_block(ring_at)]
    for step in range(1, ring):
        send = w_block(lax.rem(ring_at + step, ring))
        pairs = [(i, (i + 2 * step) % tp_count) for i in range(tp_count)]
        w_received.append(lax.ppermute(send, "tp", pairs))

    float_rows = hidden.astype(jnp.float32)
    normed = (
        float_rows
        * lax.rsqrt(jnp.mean(float_rows * float_rows, -1, keepdims=True) + EPS)
        * norm_gain
    ).astype(jnp.bfloat16)
    query_raw = jnp.dot(normed, w_query, preferred_element_type=jnp.float32).reshape(
        token_count, local_heads, HD
    )
    keyval_part = jnp.dot(normed, w_keyval, preferred_element_type=jnp.float32).astype(jnp.bfloat16)
    lengths = lax.dynamic_slice_in_dim(cache_len, group_index * R, R)
    positions = (lengths[:, None] + jnp.arange(C, dtype=jnp.int32)[None, :]).reshape(token_count)
    query_local = rotate_pairs(query_raw, positions).astype(jnp.bfloat16).transpose(1, 0, 2)
    far_query = to_partner(query_local[:, :C], flip_mask, groups)
    query_ext = jnp.concatenate([query_local, far_query], 1)
    ext_tokens = query_ext.shape[1]
    query_got, keyval_got = group_gather([query_ext, keyval_part], 0)
    queries = query_got.reshape(QH, ext_tokens, HD)
    keyval_all = keyval_got.reshape(tp_count, token_count, -1).transpose(1, 0, 2).reshape(
        token_count, -1
    )

    stored_first = lengths[0] - lengths[0] // 2
    bound_one = stored_first
    bound_two = stored_first + lengths[1]
    far_count = cache_len[partner[group_index] * R] // 2
    starts = jnp.stack([0, bound_one, bound_two]).astype(jnp.int32)
    ends = jnp.stack([bound_one, bound_two, bound_two + far_count]).astype(jnp.int32)
    offset = tp_index * rows_here
    lo = jnp.clip(starts - offset, 0, rows_here)
    hi = jnp.clip(ends - offset, 0, rows_here)
    mix, peak, total = cache_attention(queries, kv_cache, lo, hi)
    mix_got, peak_got, total_got = tp_exchange(
        [
            mix.astype(jnp.bfloat16).reshape(tp_count, local_heads, ext_tokens, HD),
            peak.reshape(tp_count, local_heads, ext_tokens),
            total.reshape(tp_count, local_heads, ext_tokens),
        ],
        [False, False, False],
        2,
    )
    top = jnp.max(peak_got, 0)
    scales = jnp.exp(peak_got - top[None])
    mix_c = jnp.sum(mix_got.astype(jnp.float32) * scales[..., None], 0)
    total_c = jnp.sum(total_got * scales, 0)
    far_pack = jnp.concatenate(
        [
            mix_c[:, token_count:],
            top[:, None, token_count:],
            total_c[:, None, token_count:],
        ],
        1,
    )
    far_pack = to_partner(far_pack, flip_mask, groups)
    far_back = (far_pack[:, :C], far_pack[:, C], far_pack[:, C + 1])
    combined = (mix_c[:, :token_count], top[:, :token_count], total_c[:, :token_count])
    front = join_partials(tuple(piece[:, :C] for piece in combined), far_back)
    own = tuple(jnp.concatenate([front[i], combined[i][:, C:]], 1) for i in range(3))

    new_keys = rotate_pairs(
        keyval_all[:, : KVH * HD].astype(jnp.float32).reshape(token_count, KVH, HD), positions
    ).astype(jnp.bfloat16)
    new_values = keyval_all[:, KVH * HD :].reshape(token_count, KVH, HD)
    kv_head = (tp_index * local_heads) // (QH // KVH)
    key_rows = lax.dynamic_index_in_dim(new_keys, kv_head, 1, keepdims=False)
    value_rows = lax.dynamic_index_in_dim(new_values, kv_head, 1, keepdims=False)
    token_index = jnp.arange(token_count, dtype=jnp.int32)
    request_of = token_index // C
    within = token_index % C
    self_visible = (request_of[:, None] == request_of[None, :]) & (
        within[None, :] <= within[:, None]
    )
    self_scores = jnp.einsum(
        "htd,sd->hts", query_local, key_rows, preferred_element_type=jnp.float32
    ) * HD ** (-0.5)
    self_scores = jnp.where(self_visible[None], self_scores, -jnp.inf)
    self_peak = jnp.max(self_scores, -1)
    self_weights = jnp.exp(self_scores - self_peak[..., None])
    self_total = jnp.sum(self_weights, -1)
    self_mix = jnp.einsum(
        "hts,sd->htd", self_weights.astype(jnp.bfloat16), value_rows,
        preferred_element_type=jnp.float32,
    )
    final_mix, final_peak, final_total = join_partials(own, (self_mix, self_peak, self_total))
    attention = (final_mix / final_total[..., None]).astype(jnp.bfloat16)
    attention = attention.transpose(1, 0, 2).reshape(token_count, local_heads * HD)
    (attention_ring,) = tp_exchange([attention], [True], 3, ring, 2)
    sums = None
    for step in range(ring):
        source = lax.rem(ring_at - step + ring, ring)
        piece = jnp.dot(
            lax.dynamic_index_in_dim(attention_ring, source, 0, False),
            w_received[step],
            preferred_element_type=jnp.float32,
        )
        sums = piece if sums is None else sums + piece
    (other_got,) = tp_exchange([sums[:, out_width:].astype(jnp.bfloat16)], [True], 4, 2, 1)
    other = lax.dynamic_index_in_dim(other_got, 1 - side, 0, False)
    return (sums[:, :out_width] + other.astype(jnp.float32)).astype(jnp.bfloat16)


def solution(mesh):
    placed = (
        P("grp", None),
        P(),
        P(None, "tp"),
        P(None, "tp"),
        P("tp", None),
        P(("grp", "tp"), None),
        P(),
        P(),
    )
    return jax.shard_map(
        on_device, mesh=mesh, in_specs=placed, out_specs=P("grp", "tp"), check_vma=False
    )
```

```python
import functools

import jax
import jax.numpy as jnp
from jax import lax
from jax.experimental import pallas as pl
from jax.experimental.pallas import tpu as pltpu
from jax.sharding import PartitionSpec as P

HD = 128
QH = 16
KVH = 2
C = 128
R = 2

THETA = 5000000.0
EPS = 1e-05
NEG = -1e30
CHUNK = 1280
MESH = pl.DeviceIdType.MESH


def rotate_pairs(values, positions):
    width = values.shape[-1]
    half_width = width // 2
    frequency = THETA ** (-2.0 * jnp.arange(half_width, dtype=jnp.float32) / width)
    angles = positions.astype(jnp.float32)[:, None] * frequency[None, :]
    cosine_part = jnp.cos(angles)[:, None, :]
    sine_part = jnp.sin(angles)[:, None, :]
    first_half = values[..., :half_width]
    second_half = values[..., half_width:]
    return jnp.concatenate(
        [
            first_half * cosine_part - second_half * sine_part,
            second_half * cosine_part + first_half * sine_part,
        ],
        -1,
    )


def exchange_kernel(count, stride, modes, *refs):
    arrays = len(modes)
    ins, outs = refs[:arrays], refs[arrays : 2 * arrays]
    send_sem, recv_sem = refs[2 * arrays :]
    me = lax.axis_index("tp")
    grp = lax.axis_index("grp")
    mine = lax.rem(me // stride, count)
    base = me - mine * stride

    def member(step):
        return lax.rem(mine + step, count)

    barrier = pltpu.get_barrier_semaphore()
    for step in range(1, count):
        pl.semaphore_signal(
            barrier, inc=1, device_id=(grp, base + member(step) * stride), device_id_type=MESH
        )
    pl.semaphore_wait(barrier, count - 1)
    copies = []
    for index in range(arrays):
        for step in range(1, count):
            peer = member(step)
            source = ins[index] if modes[index] else ins[index].at[peer]
            copy = pltpu.make_async_remote_copy(
                src_ref=source,
                dst_ref=outs[index].at[mine],
                send_sem=send_sem.at[index, step],
                recv_sem=recv_sem.at[index, step],
                device_id=(grp, base + peer * stride),
                device_id_type=MESH,
            )
            copy.start()
            copies.append(copy)
        if modes[index]:
            outs[index][mine] = ins[index][...]
        else:
            outs[index][mine] = ins[index][mine]
    for copy in copies:
        copy.wait()


def tp_exchange(arrays, modes, collective_id, count=None, stride=1):
    count = lax.axis_size("tp") if count is None else count
    shapes = []
    for array, gather in zip(arrays, modes):
        block = array.shape if gather else array.shape[1:]
        shapes.append(jax.ShapeDtypeStruct((count,) + tuple(block), array.dtype))
    vmem = pl.BlockSpec(memory_space=pltpu.VMEM)
    return pl.pallas_call(
        functools.partial(exchange_kernel, count, stride, tuple(modes)),
        out_shape=tuple(shapes),
        in_specs=[vmem] * len(arrays),
        out_specs=tuple([vmem] * len(arrays)),
        scratch_shapes=[
            pltpu.SemaphoreType.DMA((len(arrays), count)),
            pltpu.SemaphoreType.DMA((len(arrays), count)),
        ],
        compiler_params=pltpu.CompilerParams(
            collective_id=collective_id, has_side_effects=True, vmem_limit_bytes=48 * 1024 * 1024
        ),
    )(*arrays)


def gather_kernel(arrays, *refs):
    ins, outs = refs[:arrays], refs[arrays : 2 * arrays]
    pair_send, pair_recv, ring_send, ring_recv, hop_send, hop_recv = refs[2 * arrays :]
    me = lax.axis_index("tp")
    grp = lax.axis_index("grp")
    ring = lax.axis_size("tp") // 2
    side = me % 2
    ring_at = me // 2
    partner = (grp, ring_at * 2 + 1 - side)

    def member(step):
        return (grp, lax.rem(ring_at + step, ring) * 2 + side)

    barrier = pltpu.get_barrier_semaphore()
    pl.semaphore_signal(barrier, inc=1, device_id=partner, device_id_type=MESH)
    for step in range(1, ring):
        pl.semaphore_signal(barrier, inc=1, device_id=member(step), device_id_type=MESH)
    pl.semaphore_wait(barrier, ring)
    pairs, direct = [], []
    for index in range(arrays):
        copy = pltpu.make_async_remote_copy(
            src_ref=ins[index],
            dst_ref=outs[index].at[ring_at, side],
            send_sem=pair_send.at[index],
            recv_sem=pair_recv.at[index],
            device_id=partner,
            device_id_type=MESH,
        )
        copy.start()
        pairs.append(copy)
        for step in range(1, ring):
            copy = pltpu.make_async_remote_copy(
                src_ref=ins[index],
                dst_ref=outs[index].at[ring_at, side],
                send_sem=ring_send.at[index, step],
                recv_sem=ring_recv.at[index, step],
                device_id=member(step),
                device_id_type=MESH,
            )
            copy.start()
            direct.append(copy)
        outs[index][ring_at, side] = ins[index][...]
    hops = []
    for index in range(arrays):
        pairs[index].wait_recv()
        for step in range(1, ring):
            copy = pltpu.make_async_remote_copy(
                src_ref=outs[index].at[ring_at, 1 - side],
                dst_ref=outs[index].at[ring_at, 1 - side],
                send_sem=hop_send.at[index, step],
                recv_sem=hop_recv.at[index, step],
                device_id=member(step),
                device_id_type=MESH,
            )
            copy.start()
            hops.append(copy)
    for copy in pairs:
        copy.wait_send()
    for copy in direct + hops:
        copy.wait()


def group_gather(arrays, collective_id):
    ring = lax.axis_size("tp") // 2
    count = len(arrays)
    shapes = [jax.ShapeDtypeStruct((ring, 2) + a.shape, a.dtype) for a in arrays]
    vmem = pl.BlockSpec(memory_space=pltpu.VMEM)
    return pl.pallas_call(
        functools.partial(gather_kernel, count),
        out_shape=tuple(shapes),
        in_specs=[vmem] * count,
        out_specs=tuple([vmem] * count),
        scratch_shapes=[
            pltpu.SemaphoreType.DMA((count,)),
            pltpu.SemaphoreType.DMA((count,)),
            pltpu.SemaphoreType.DMA((count, ring)),
            pltpu.SemaphoreType.DMA((count, ring)),
            pltpu.SemaphoreType.DMA((count, ring)),
            pltpu.SemaphoreType.DMA((count, ring)),
        ],
        compiler_params=pltpu.CompilerParams(
            collective_id=collective_id, has_side_effects=True, vmem_limit_bytes=48 * 1024 * 1024
        ),
    )(*arrays)


def attention_kernel(lo_ref, hi_ref, q_ref, cache_ref, mix_ref, peak_ref, total_ref):
    block = pl.program_id(0)
    kv_head = pl.program_id(1)
    lo = lo_ref[block]
    hi = hi_ref[block]
    heads, tokens, width = q_ref.shape
    key_col = pl.multiple_of(kv_head * HD, HD)
    value_col = pl.multiple_of((KVH + kv_head) * HD, HD)
    first = lo // CHUNK
    last = jnp.where(hi > lo, (hi + CHUNK - 1) // CHUNK, first)

    def one_head(head, carry):
        query = q_ref[head]

        def body(chunk, state):
            peak, total, mix = state
            start = pl.multiple_of(chunk * CHUNK, CHUNK)
            keys = cache_ref[pl.ds(start, CHUNK), pl.ds(key_col, HD)]
            values = cache_ref[pl.ds(start, CHUNK), pl.ds(value_col, HD)]
            rows = start + lax.broadcasted_iota(jnp.int32, (1, CHUNK), 1)
            bias = jnp.where((rows >= lo) & (rows < hi), 0.0, -jnp.inf)
            scores = lax.dot_general(
                query, keys, (((1,), (1,)), ((), ())), preferred_element_type=jnp.float32
            ) * (HD ** (-0.5)) + bias
            new_peak = jnp.maximum(peak, jnp.max(scores, axis=1, keepdims=True))
            scale = jnp.exp(peak - new_peak)
            weights = jnp.exp(scores - new_peak)
            total = scale * total + jnp.sum(weights, axis=1, keepdims=True)
            mix = scale * mix + jnp.dot(
                weights.astype(jnp.bfloat16), values, preferred_element_type=jnp.float32
            )
            return new_peak, total, mix

        start_state = (
            jnp.full((tokens, 1), NEG, jnp.float32),
            jnp.zeros((tokens, 1), jnp.float32),
            jnp.zeros((tokens, width), jnp.float32),
        )
        peak, total, mix = lax.fori_loop(first, last, body, start_state)
        mix_ref[head] = mix
        peak_ref[head] = peak
        total_ref[head] = total
        return carry

    lax.fori_loop(0, heads, one_head, 0)


def cache_attention(queries, cache_rows, lo, hi):
    heads, tokens, width = queries.shape
    blocks = tokens // C
    group_size = heads // KVH
    return pl.pallas_call(
        attention_kernel,
        out_shape=(
            jax.ShapeDtypeStruct((heads, tokens, width), jnp.float32),
            jax.ShapeDtypeStruct((heads, tokens, 1), jnp.float32),
            jax.ShapeDtypeStruct((heads, tokens, 1), jnp.float32),
        ),
        grid_spec=pltpu.PrefetchScalarGridSpec(
            num_scalar_prefetch=2,
            grid=(blocks, KVH),
            in_specs=[
                pl.BlockSpec((group_size, C, width), lambda b, j, lo, hi: (j, b, 0)),
                pl.BlockSpec(cache_rows.shape, lambda b, j, lo, hi: (0, 0)),
            ],
            out_specs=[
                pl.BlockSpec((group_size, C, width), lambda b, j, lo, hi: (j, b, 0)),
                pl.BlockSpec((group_size, C, 1), lambda b, j, lo, hi: (j, b, 0)),
                pl.BlockSpec((group_size, C, 1), lambda b, j, lo, hi: (j, b, 0)),
            ],
        ),
        compiler_params=pltpu.CompilerParams(vmem_limit_bytes=48 * 1024 * 1024),
    )(lo, hi, queries, cache_rows)


def join_partials(first, second):
    first_mix, first_peak, first_total = first
    second_mix, second_peak, second_total = second
    new_peak = jnp.maximum(first_peak, second_peak)
    first_scale = jnp.exp(first_peak - new_peak)
    second_scale = jnp.exp(second_peak - new_peak)
    joined_mix = first_mix * first_scale[..., None] + second_mix * second_scale[..., None]
    return (joined_mix, new_peak, first_total * first_scale + second_total * second_scale)


def to_partner(tree, flip_mask, groups):
    def branch(mask):
        pairs = [(i, i ^ mask) for i in range(groups)]
        return lambda t: jax.tree.map(lambda a: lax.ppermute(a, "grp", pairs), t)

    low_count = 8
    low = lax.rem(flip_mask, low_count)
    high = flip_mask // low_count
    tree = lax.switch(low, [lambda t: t] + [branch(mask) for mask in range(1, low_count)], tree)
    high_masks = range(low_count, groups, low_count)
    return lax.switch(high, [lambda t: t] + [branch(mask) for mask in high_masks], tree)


def on_device(hidden, norm_gain, w_query, w_keyval, w_out, kv_cache, cache_len, partner):
    group_index = lax.axis_index("grp")
    tp_index = lax.axis_index("tp")
    tp_count = lax.axis_size("tp")
    groups = lax.axis_size("grp")
    ring = tp_count // 2
    ring_at = tp_index // 2
    side = tp_index % 2
    local_heads = QH // tp_count
    rows_here = kv_cache.shape[0]
    token_count = hidden.shape[0]
    model_width = w_out.shape[1]
    out_width = model_width // tp_count
    flip_mask = partner[0]

    def w_block(member):
        first = lax.dynamic_slice_in_dim(w_out, (2 * member + side) * out_width, out_width, 1)
        second = lax.dynamic_slice_in_dim(w_out, (2 * member + 1 - side) * out_width, out_width, 1)
        return jnp.concatenate([first, second], 1)

    w_received = [w_block(ring_at)]
    for step in range(1, ring):
        send = w_block(lax.rem(ring_at + step, ring))
        pairs = [(i, (i + 2 * step) % tp_count) for i in range(tp_count)]
        w_received.append(lax.ppermute(send, "tp", pairs))

    float_rows = hidden.astype(jnp.float32)
    normed = (
        float_rows
        * lax.rsqrt(jnp.mean(float_rows * float_rows, -1, keepdims=True) + EPS)
        * norm_gain
    ).astype(jnp.bfloat16)
    query_raw = jnp.dot(normed, w_query, preferred_element_type=jnp.float32).reshape(
        token_count, local_heads, HD
    )
    keyval_part = jnp.dot(normed, w_keyval, preferred_element_type=jnp.float32).astype(jnp.bfloat16)
    lengths = lax.dynamic_slice_in_dim(cache_len, group_index * R, R)
    positions = (lengths[:, None] + jnp.arange(C, dtype=jnp.int32)[None, :]).reshape(token_count)
    query_local = rotate_pairs(query_raw, positions).astype(jnp.bfloat16).transpose(1, 0, 2)
    far_query = to_partner(query_local[:, :C], flip_mask, groups)
    query_ext = jnp.concatenate([query_local, far_query], 1)
    ext_tokens = query_ext.shape[1]
    query_got, keyval_got = group_gather([query_ext, keyval_part], 0)
    queries = query_got.reshape(QH, ext_tokens, HD)
    keyval_all = keyval_got.reshape(tp_count, token_count, -1).transpose(1, 0, 2).reshape(
        token_count, -1
    )

    stored_first = lengths[0] - lengths[0] // 2
    bound_one = stored_first
    bound_two = stored_first + lengths[1]
    far_count = cache_len[partner[group_index] * R] // 2
    starts = jnp.stack([0, bound_one, bound_two]).astype(jnp.int32)
    ends = jnp.stack([bound_one, bound_two, bound_two + far_count]).astype(jnp.int32)
    offset = tp_index * rows_here
    lo = jnp.clip(starts - offset, 0, rows_here)
    hi = jnp.clip(ends - offset, 0, rows_here)
    mix, peak, total = cache_attention(queries, kv_cache, lo, hi)
    mix_got, peak_got, total_got = tp_exchange(
        [
            mix.astype(jnp.bfloat16).reshape(tp_count, local_heads, ext_tokens, HD),
            peak.reshape(tp_count, local_heads, ext_tokens),
            total.reshape(tp_count, local_heads, ext_tokens),
        ],
        [False, False, False],
        2,
    )
    top = jnp.max(peak_got, 0)
    scales = jnp.exp(peak_got - top[None])
    mix_c = jnp.sum(mix_got.astype(jnp.float32) * scales[..., None], 0)
    total_c = jnp.sum(total_got * scales, 0)
    far_pack = jnp.concatenate(
        [
            mix_c[:, token_count:],
            top[:, None, token_count:],
            total_c[:, None, token_count:],
        ],
        1,
    )
    far_pack = to_partner(far_pack, flip_mask, groups)
    far_back = (far_pack[:, :C], far_pack[:, C], far_pack[:, C + 1])
    combined = (mix_c[:, :token_count], top[:, :token_count], total_c[:, :token_count])
    front = join_partials(tuple(piece[:, :C] for piece in combined), far_back)
    own = tuple(jnp.concatenate([front[i], combined[i][:, C:]], 1) for i in range(3))

    new_keys = rotate_pairs(
        keyval_all[:, : KVH * HD].astype(jnp.float32).reshape(token_count, KVH, HD), positions
    ).astype(jnp.bfloat16)
    new_values = keyval_all[:, KVH * HD :].reshape(token_count, KVH, HD)
    kv_head = (tp_index * local_heads) // (QH // KVH)
    key_rows = lax.dynamic_index_in_dim(new_keys, kv_head, 1, keepdims=False)
    value_rows = lax.dynamic_index_in_dim(new_values, kv_head, 1, keepdims=False)
    token_index = jnp.arange(token_count, dtype=jnp.int32)
    request_of = token_index // C
    within = token_index % C
    self_visible = (request_of[:, None] == request_of[None, :]) & (
        within[None, :] <= within[:, None]
    )
    self_scores = jnp.einsum(
        "htd,sd->hts", query_local, key_rows, preferred_element_type=jnp.float32
    ) * HD ** (-0.5)
    self_scores = jnp.where(self_visible[None], self_scores, -jnp.inf)
    self_peak = jnp.max(self_scores, -1)
    self_weights = jnp.exp(self_scores - self_peak[..., None])
    self_total = jnp.sum(self_weights, -1)
    self_mix = jnp.einsum(
        "hts,sd->htd", self_weights.astype(jnp.bfloat16), value_rows,
        preferred_element_type=jnp.float32,
    )
    final_mix, final_peak, final_total = join_partials(own, (self_mix, self_peak, self_total))
    attention = (final_mix / final_total[..., None]).astype(jnp.bfloat16)
    attention = attention.transpose(1, 0, 2).reshape(token_count, local_heads * HD)
    (attention_ring,) = tp_exchange([attention], [True], 3, ring, 2)
    sums = None
    for step in range(ring):
        source = lax.rem(ring_at - step + ring, ring)
        piece = jnp.dot(
            lax.dynamic_index_in_dim(attention_ring, source, 0, False),
            w_received[step],
            preferred_element_type=jnp.float32,
        )
        sums = piece if sums is None else sums + piece
    (other_got,) = tp_exchange([sums[:, out_width:].astype(jnp.bfloat16)], [True], 4, 2, 1)
    other = lax.dynamic_index_in_dim(other_got, 1 - side, 0, False)
    return (sums[:, :out_width] + other.astype(jnp.float32)).astype(jnp.bfloat16)


def solution(mesh):
    placed = (
        P("grp", None),
        P(),
        P(None, "tp"),
        P(None, "tp"),
        P("tp", None),
        P(("grp", "tp"), None),
        P(),
        P(),
    )
    return jax.shard_map(
        on_device, mesh=mesh, in_specs=placed, out_specs=P("grp", "tp"), check_vma=False
    )
```
